256 devices in a mesh: blk: 32 (over y, z), rep: 8 (over x, core).
Axes of the slice: x: 4, y: 4, z: 8, core: 2. Of those that a mesh axis runs over, the one named last changes fastest.
Arguments:
- hidden_in: bfloat16 [8, 512, 2560], P('rep', 'blk'), may hold values from -6 to 6
- w_z: bfloat16 [2560, 4096], P(None, 'blk'), may hold values from -0.125 to 0.125
- w_x: bfloat16 [2560, 4096], P(None, 'blk'), may hold values from -0.125 to 0.125
- w_bc: bfloat16 [2560, 256], replicated, may hold values from -0.125 to 0.125
- w_dt: bfloat16 [2560, 64], P(None, 'blk'), may hold values from -0.125 to 0.125
- conv_x: float32 [4, 4096], P(None, 'blk'), may hold values from -3 to 3
- conv_bc: float32 [4, 256], replicated, may hold values from -3 to 3
- dt_bias: float32 [4, 64], P(None, 'blk'), may hold values from -3 to -0.5
- a_log: float32 [64], P('blk'), may hold values from -2.5 to 0.5
- d_skip: float32 [64], P('blk'), may hold values from 0.5 to 1.5
- norm_gain: float32 [4096], P('blk'), may hold values from 0.5 to 1.5
- w_out: bfloat16 [4096, 2560], P('blk'), may hold values from -0.09375 to 0.09375
- edge_x: bfloat16 [256, 3, 4096], P('rep', None, 'blk'), may hold values from -6 to 6
- edge_bc: bfloat16 [256, 3, 256], P('rep'), may hold values from -6 to 6
- pool: float32 [384, 64, 64, 128], P('rep', 'blk'), may hold values from -0.6 to 0.6
- tenant_sizes: int32 [4], replicated, may hold values from 1 to 128, 256 in all
- owner: int32 [256, 1], P('rep'), may hold values from 0 to 7; in each aligned block of 32 rows (0 to 31, 32 to 63, ...) at most 6 rows name the same one
- accepted: int32 [256], P('rep'), may hold values from 1 to 16
- prompt_len: int32 [256], P('rep'), may hold values from 1 to 11
Outputs:
- hidden_out: bfloat16 [8, 512, 2560], P('rep', 'blk')
- new_pool: float32 [384, 64, 64, 128], P('rep', 'blk')
The draws below stay inside these ranges and needn't reach their ends.
Inputs may be any that keep to these rules, and one draw needn't show every extreme that they name: Among the requests of one group (aligned blocks of 32 requests) each owner is named at most 6 times, a bound that some block reaches. `tenant_sizes`: the sizes sum to 256.
All inputs are finite; a program needn't handle non-finite values.
Results may differ from the reference program's by a relative error of at most 0.025.
Values may be sent and summed in bfloat16 or wider, within the bound.
A program may use at most 64 MiB of HBM per device.

```python
import math
import jax
import jax.numpy as jnp
import numpy as np
from jax import lax

D = 2560
STATE = 128
HEAD_DIM = 64
CONV_K = 4
DRAFTS = 16
TENANTS = 4
REQ_GRP = 32
HEADS = 64
INNER = 4096
CAP = 6
OWNER_SLOTS = 48
POOL = 384
REQS = 256
GROUP_TOK = 512
N_REP = 8


def place_ends(result, own_key, smallest, top_value):
    extent = result.shape
    index_at = [jax.random.randint(jax.random.fold_in(own_key, axis), (), 0, extent[axis]) for axis in range(len(extent))]
    result = result.at[tuple(index_at)].set(smallest)
    longest = extent.index(max(extent))
    index_at[longest] = (index_at[longest] + 1) % extent[longest]
    return result.at[tuple(index_at)].set(top_value)


def block_scale(key, shape, shards, low, top_value):
    factor_of, own = 1.0, jax.random.fold_in(key, 6)
    for axis_at, blocks in shards:
        steps = jnp.exp(jax.random.uniform(jax.random.fold_in(own, axis_at), (blocks,), jnp.float32, low / len(shards), top_value / len(shards)))
        factor_of = factor_of * jnp.repeat(steps, shape[axis_at] // blocks).reshape([-1 if axis == axis_at else 1 for axis in range(len(shape))])
    return factor_of


def profile(amount, total, most, lean):
    weights = [(1 << 20) // math.isqrt(rank ** lean) + 1 for rank in range(2, amount + 1)]
    spare, given = total - most - (amount - 1), [1] * (amount - 1)
    while spare > 0:
        movable = [i for i in range(amount - 1) if given[i] < most]
        whole, budget = sum([weights[i] for i in movable]), spare
        for i in movable:
            addition = min(most - given[i], max(1, budget * weights[i] // whole), spare)
            given[i] = given[i] + addition
            spare = spare - addition
    return np.array([most] + given)


def uneven_parts(rng, amount, total, limit, slope):
    if amount == 2:
        one = jax.random.randint(rng, (), max(1, total - limit), min(limit, total - 1) + 1)
        return jnp.stack([one, total - one])
    tallies = jnp.asarray(profile(amount, total, limit, slope), jnp.int32)
    twos = (amount - 1) // 2
    source_of, taker = tallies[1:1 + 2 * twos:2], tallies[2:2 + 2 * twos:2]
    slack = jnp.minimum(source_of - 1, limit - taker)
    moved = jax.random.randint(jax.random.fold_in(rng, 1), (twos,), 0, 1 << 20) % (slack + 1)
    tallies = tallies.at[1:1 + 2 * twos:2].set(source_of - moved).at[2:2 + 2 * twos:2].set(taker + moved)
    return tallies[jax.random.permutation(jax.random.fold_in(rng, 2), amount)]


def deal_out(stream_key, own, number, rows, number_of, top, most, lean):
    ranking = jax.random.permutation(stream_key, number_of)
    crowded, usual = shares(number_of, rows * top, most, lean, True), shares(number_of, rows * top, most, lean, False)
    places = jnp.arange(number_of)

    def named(sizes, offset_by):
        used = int((sizes > 0).sum())
        fixed = max(1, used // 4)
        moved = fixed + (places - fixed + offset_by * (used - fixed)) % max(1, number_of - fixed)
        return jnp.zeros((number_of,), jnp.int32).at[ranking[jnp.where(places < fixed, places, moved)]].set(jnp.asarray(sizes, jnp.int32))

    sizes = jnp.where(number % 4 == 0, named(crowded, number // 4), named(usual, number - number // 4 - 1))
    mixed = jax.random.permutation(jax.random.fold_in(own, 3), number_of)
    giver, receiver = mixed[0:number_of // 2 * 2:2], mixed[1:number_of // 2 * 2:2]
    slack = jnp.minimum(sizes[giver] - 1, most - sizes[receiver]) // 2
    slack = jnp.where((giver == ranking[0]) | (receiver == ranking[0]) | (sizes[receiver] == 0), 0, jnp.maximum(slack, 0))
    moved = jax.random.randint(jax.random.fold_in(own, 4), (number_of // 2,), 0, 1 << 20) % (slack + 1)
    sizes = sizes.at[giver].add(-moved).at[receiver].add(moved)
    items = jnp.searchsorted(jnp.cumsum(sizes), jnp.arange(rows * top), side="right").astype(jnp.int32)
    table = items.reshape(top, rows).T
    table = table[jax.random.permutation(jax.random.fold_in(own, 1), rows)]
    offset_by = jax.random.randint(jax.random.fold_in(own, 2), (rows, 1), 0, top)
    return jnp.take_along_axis(table, (jnp.arange(top)[None, :] + offset_by) % top, axis=1)


def shares(amount, total, reach, slope, full):
    portions = [(1 << 20) // math.isqrt(grade ** slope) + 1 for grade in range(1, amount + 1)]
    largest = reach if full else min(reach, max(-(-total // amount), total * portions[0] // sum(portions)))
    least = 1 if total - largest >= amount - 1 else 0
    holding, spare = [largest] + [least] * (amount - 1), total - largest - least * (amount - 1)
    while spare > 0:
        free = [i for i in range(1, amount) if holding[i] < largest] or [i for i in range(1, amount) if holding[i] < reach]
        whole, left = sum([portions[i] for i in free]), spare
        for i in free:
            more = min(reach - holding[i], max(1, left * portions[i] // whole), spare)
            holding[i] = holding[i] + more
            spare = spare - more
    return np.array(holding)


def noise(stream_key, shape, spread, reach, cuts=(), kind=jnp.bfloat16):
    result = jax.random.normal(stream_key, shape, jnp.float32) * spread
    if len(cuts) > 0:
        result = block_scale(stream_key, shape, cuts, -0.22, 0.18) * result
    return jnp.clip(result, min=-reach, max=reach).astype(kind)


def setup_inputs(seed: int = 0) -> dict:
    seeds = jax.random.split(jax.random.key(seed), 20)
    hidden_in = noise(seeds[0], (N_REP, GROUP_TOK, D), 1.0, 6.0, ((0, 8), (1, 32)))
    w_z = noise(seeds[1], (D, INNER), D ** -0.5, 0.125, ((1, 32),))
    w_x = noise(seeds[2], (D, INNER), D ** -0.5, 0.125, ((1, 32),))
    w_bc = noise(seeds[3], (D, 2 * STATE), D ** -0.5, 0.125)
    w_dt = noise(seeds[4], (D, HEADS), D ** -0.5, 0.125, ((1, 32),))
    conv_x = noise(seeds[5], (CONV_K, INNER), CONV_K ** -0.5, 3.0, ((1, 32),), jnp.float32)
    conv_bc = noise(seeds[6], (CONV_K, 2 * STATE), CONV_K ** -0.5, 3.0, (), jnp.float32)
    dt_bias = jnp.clip(-3.0 + 2.5 * jax.random.uniform(seeds[7], (TENANTS, HEADS), jnp.float32) ** block_scale(seeds[7], (TENANTS, HEADS), ((1, 32),), -0.2, 0.2), -3.0, -0.5)
    a_log = jnp.clip(-2.5 + 3.0 * jax.random.uniform(seeds[8], (HEADS,), jnp.float32) ** block_scale(seeds[8], (HEADS,), ((0, 32),), -0.2, 0.2), -2.5, 0.5)
    d_skip = jnp.clip(0.5 + 1.0 * jax.random.uniform(seeds[9], (HEADS,), jnp.float32) ** block_scale(seeds[9], (HEADS,), ((0, 32),), -0.2, 0.2), 0.5, 1.5)
    norm_gain = jnp.clip(1.0 + 0.1 * jax.random.normal(seeds[10], (INNER,), jnp.float32), 0.5, 1.5)
    w_out = noise(seeds[11], (INNER, D), INNER ** -0.5, 0.09375, ((0, 32),))
    edge_x = noise(seeds[12], (REQS, CONV_K - 1, INNER), 1.0, 6.0, ((0, 8), (2, 32)))
    edge_bc = noise(seeds[13], (REQS, CONV_K - 1, 2 * STATE), 1.0, 6.0, ((0, 8),))
    pool = noise(seeds[14], (POOL, HEADS, HEAD_DIM, STATE), 0.1, 0.6, ((0, 8), (1, 32)), jnp.float32)
    tenant_sizes = uneven_parts(seeds[15], TENANTS, REQS, REQS // 2, 1).astype(jnp.int32)
    owner_keys = jax.random.split(jax.random.fold_in(seeds[16], 1), REQS // REQ_GRP)
    owner_turns = jax.random.permutation(jax.random.fold_in(seeds[16], 3), REQS // REQ_GRP)
    owner = jax.vmap(lambda own, number: deal_out(jax.random.fold_in(seeds[16], 2), own, number, REQ_GRP, N_REP, 1, CAP, 2))(owner_keys, owner_turns).reshape((REQS, 1))
    accepted = place_ends(jax.random.randint(seeds[17], (REQS,), 1, DRAFTS + 1), jax.random.fold_in(seeds[17], 1), 1, DRAFTS).astype(jnp.int32)
    prompt_len = place_ends(jax.random.randint(seeds[18], (REQS,), 1, 12), jax.random.fold_in(seeds[18], 1), 1, 11).astype(jnp.int32)
    return dict(hidden_in=hidden_in, w_z=w_z, w_x=w_x, w_bc=w_bc, w_dt=w_dt, conv_x=conv_x, conv_bc=conv_bc, dt_bias=dt_bias, a_log=a_log, d_skip=d_skip, norm_gain=norm_gain, w_out=w_out, edge_x=edge_x, edge_bc=edge_bc, pool=pool, tenant_sizes=tenant_sizes, owner=owner, accepted=accepted, prompt_len=prompt_len)


def convolve(edge_cells, fresh_cells, kernel, edge_mask):
    sequence = jnp.concatenate([edge_cells * edge_mask[:, :, None].astype(edge_cells.dtype), fresh_cells], 1).astype(jnp.float32)
    steps_count = fresh_cells.shape[1]
    summed = kernel[0] * sequence[:, 0:steps_count]
    for offset in range(1, kernel.shape[0]):
        summed = summed + kernel[offset] * sequence[:, offset:offset + steps_count]
    return jax.nn.silu(summed).astype(jnp.bfloat16)

def reference(hidden_in, w_z, w_x, w_bc, w_dt, conv_x, conv_bc, dt_bias, a_log, d_skip, norm_gain, w_out, edge_x, edge_bc, pool, tenant_sizes, owner, accepted, prompt_len):
    highest = lax.Precision.HIGHEST
    n_req = N_REP * REQ_GRP
    rows_all = hidden_in.reshape(-1, D)
    z_all = jnp.dot(rows_all, w_z, preferred_element_type=jnp.float32).astype(jnp.bfloat16)
    u_all = jnp.dot(rows_all, w_x, preferred_element_type=jnp.float32).astype(jnp.bfloat16)
    bc_all = jnp.dot(rows_all, w_bc, preferred_element_type=jnp.float32).astype(jnp.bfloat16)
    dt_raw = jnp.dot(rows_all, w_dt, preferred_element_type=jnp.float32).astype(jnp.bfloat16)
    edge_mask = prompt_len[:, None] >= (CONV_K - 1 - jnp.arange(CONV_K - 1, dtype=jnp.int32))[None, :]
    x_conv = convolve(edge_x, u_all.reshape(n_req, DRAFTS, INNER), conv_x, edge_mask)
    bc_conv = convolve(edge_bc, bc_all.reshape(n_req, DRAFTS, 2 * STATE), conv_bc, edge_mask)
    b_float = bc_conv[:, :, :STATE].astype(jnp.float32)
    c_float = bc_conv[:, :, STATE:].astype(jnp.float32)
    x_heads = x_conv.reshape(n_req, DRAFTS, HEADS, HEAD_DIM).astype(jnp.float32)
    req_index = jnp.arange(n_req, dtype=jnp.int32)
    tenant_ends = jnp.cumsum(tenant_sizes).astype(jnp.int32)
    tenant_id = lax.optimization_barrier(jnp.sum((req_index[:, None] >= tenant_ends[None, :-1]).astype(jnp.int32), axis=1))
    bias_req = dt_bias[tenant_id]
    step_size = jax.nn.softplus(dt_raw.reshape(n_req, DRAFTS, HEADS).astype(jnp.float32) + bias_req[:, None, :])
    log_decay = jnp.cumsum(step_size * (-jnp.exp(a_log))[None, None, :], axis=1)
    owner_of = owner[:, 0]
    group_of = req_index // REQ_GRP
    earlier = (owner_of[None, :] == owner_of[:, None]) & (group_of[None, :] == group_of[:, None]) & (req_index[None, :] < req_index[:, None])
    rank_within = lax.optimization_barrier(jnp.sum(earlier.astype(jnp.int32), axis=1))
    slot_index = (owner_of * OWNER_SLOTS + group_of * CAP + rank_within).astype(jnp.int32)
    draft_index = jnp.arange(DRAFTS, dtype=jnp.int32)
    causal = draft_index[:, None] >= draft_index[None, :]
    scores = jnp.einsum('rtn,rsn->rts', c_float, b_float, precision=highest)
    log_gap = log_decay[:, :, None, :] - log_decay[:, None, :, :]
    weight = jnp.where(causal[None, :, :, None], jnp.exp(jnp.minimum(log_gap, 0.0)), 0.0) * step_size[:, None, :, :] * scores[:, :, :, None]
    y_local = jnp.einsum('rtsh,rshp->rthp', weight, x_heads, precision=highest) + d_skip[None, None, :, None] * x_heads
    pick_last = (draft_index[None, :] == accepted[:, None] - 1).astype(jnp.float32)
    log_accept = lax.optimization_barrier(jnp.sum(pick_last[:, :, None] * log_decay, axis=1))
    keep_draft = draft_index[None, :] < accepted[:, None]
    coef = jnp.where(keep_draft[:, :, None], jnp.exp(jnp.minimum(log_accept[:, None, :] - log_decay, 0.0)), 0.0) * step_size
    carry_decay = jnp.exp(log_accept)
    c_slot = jnp.zeros((POOL, DRAFTS, STATE), jnp.float32).at[slot_index].set(c_float)
    b_slot = jnp.zeros((POOL, DRAFTS, STATE), jnp.float32).at[slot_index].set(b_float)
    x_slot = jnp.zeros((POOL, DRAFTS, HEADS, HEAD_DIM), jnp.float32).at[slot_index].set(x_heads)
    decay_slot = jnp.zeros((POOL, DRAFTS, HEADS), jnp.float32).at[slot_index].set(jnp.exp(log_decay))
    coef_slot = jnp.zeros((POOL, DRAFTS, HEADS), jnp.float32).at[slot_index].set(coef)
    carry_slot = jnp.zeros((POOL, HEADS), jnp.float32).at[slot_index].set(carry_decay)
    prior_slot = decay_slot[:, :, :, None] * jnp.einsum('jhpn,jtn->jthp', pool, c_slot, precision=highest)
    new_pool = carry_slot[:, :, None, None] * pool + jnp.einsum('jsh,jshp,jsn->jhpn', coef_slot, x_slot, b_slot, precision=highest)
    y_prior = prior_slot[slot_index]
    y_total = (y_local + y_prior).reshape(n_req * DRAFTS, INNER)
    gated = y_total * jax.nn.silu(z_all.astype(jnp.float32))
    mean_sq = lax.optimization_barrier(jnp.mean(gated * gated, axis=1))
    normed = (gated * lax.rsqrt(mean_sq + 1e-05)[:, None] * norm_gain[None, :]).astype(jnp.bfloat16)
    hidden_out = jnp.dot(normed, w_out, preferred_element_type=jnp.float32).astype(jnp.bfloat16)
    return (hidden_out.reshape(N_REP, GROUP_TOK, D), new_pool)
```

```python
import jax
import jax.numpy as jnp
from jax import lax
from jax.sharding import PartitionSpec as P


def convolve(edge_cells, fresh_cells, kernel, edge_mask):
    sequence = jnp.concatenate(
        [edge_cells * edge_mask[:, :, None].astype(edge_cells.dtype), fresh_cells], 1
    ).astype(jnp.float32)
    steps_count = fresh_cells.shape[1]
    summed = kernel[0] * sequence[:, 0:steps_count]
    for offset in range(1, kernel.shape[0]):
        summed = summed + kernel[offset] * sequence[:, offset : offset + steps_count]
    return jax.nn.silu(summed).astype(jnp.bfloat16)


def shards(
    hidden_in,
    w_z,
    w_x,
    w_bc,
    w_dt,
    conv_x,
    conv_bc,
    dt_bias,
    a_log,
    d_skip,
    norm_gain,
    w_out,
    edge_x,
    edge_bc,
    pool,
    tenant_sizes,
    owner,
    accepted,
    prompt_len,
):
    highest = lax.Precision.HIGHEST
    rows_in = hidden_in[0]
    local_rows = rows_in.shape[0]
    n_req = edge_x.shape[0]
    drafts = local_rows * lax.axis_size("blk") // n_req
    state_dim = w_bc.shape[1] // 2
    heads_here = w_dt.shape[1]
    inner_here = w_z.shape[1]
    head_dim = inner_here // heads_here
    slots_here = pool.shape[0]
    cap_group = slots_here // lax.axis_size("rep")
    weights_in = (w_z, w_x, w_dt, w_bc)
    n_blk = lax.axis_size("blk")
    block_rows = lax.all_to_all(
        jnp.broadcast_to(rows_in[None], (n_blk,) + rows_in.shape), "blk", 0, 0, tiled=True
    ).reshape(n_blk * local_rows, rows_in.shape[1])
    projected = jnp.concatenate(
        [
            jnp.dot(block_rows, weight_cols, preferred_element_type=jnp.float32)
            for weight_cols in weights_in
        ],
        1,
    ).astype(jnp.bfloat16)
    z_all = projected[:, :inner_here]
    u_all = projected[:, inner_here : 2 * inner_here]
    dt_raw = projected[:, 2 * inner_here : 2 * inner_here + heads_here]
    bc_all = projected[:, 2 * inner_here + heads_here :]
    edge_len = edge_x.shape[1]
    edge_mask = prompt_len[:, None] >= (edge_len - jnp.arange(edge_len, dtype=jnp.int32))[None, :]
    x_conv = convolve(edge_x, u_all.reshape(n_req, drafts, inner_here), conv_x, edge_mask)
    bc_conv = convolve(edge_bc, bc_all.reshape(n_req, drafts, 2 * state_dim), conv_bc, edge_mask)
    b_half = bc_conv[:, :, :state_dim]
    c_half = bc_conv[:, :, state_dim:]
    b_float = b_half.astype(jnp.float32)
    c_float = c_half.astype(jnp.float32)
    x_heads = x_conv.reshape(n_req, drafts, heads_here, head_dim).astype(jnp.float32)
    req_index = lax.axis_index("rep") * n_req + jnp.arange(n_req, dtype=jnp.int32)
    tenant_ends = jnp.cumsum(tenant_sizes)
    tenant_id = jnp.sum((req_index[:, None] >= tenant_ends[None, :-1]).astype(jnp.int32), axis=1)
    tenant_pick = (
        tenant_id[:, None] == jnp.arange(tenant_sizes.shape[0], dtype=jnp.int32)[None, :]
    ).astype(jnp.float32)
    bias_req = jnp.dot(tenant_pick, dt_bias, precision=highest)
    step_size = jax.nn.softplus(
        dt_raw.reshape(n_req, drafts, heads_here).astype(jnp.float32) + bias_req[:, None, :]
    )
    log_decay = jnp.cumsum(step_size * (-jnp.exp(a_log))[None, None, :], axis=1)
    draft_index = jnp.arange(drafts, dtype=jnp.int32)
    causal = draft_index[:, None] >= draft_index[None, :]
    scores = jnp.einsum("rtn,rsn->rts", c_float, b_float, precision=highest)
    log_gap = log_decay[:, :, None, :] - log_decay[:, None, :, :]
    weight = (
        jnp.where(causal[None, :, :, None], jnp.exp(jnp.minimum(log_gap, 0.0)), 0.0)
        * step_size[:, None, :, :]
        * scores[:, :, :, None]
    )
    y_local = (
        jnp.einsum("rtsh,rshp->rthp", weight, x_heads, precision=highest)
        + d_skip[None, None, :, None] * x_heads
    )
    pick_last = (draft_index[None, :] == accepted[:, None] - 1).astype(jnp.float32)
    log_accept = jnp.sum(pick_last[:, :, None] * log_decay, axis=1)
    keep_draft = draft_index[None, :] < accepted[:, None]
    coef = (
        jnp.where(
            keep_draft[:, :, None],
            jnp.exp(jnp.minimum(log_accept[:, None, :] - log_decay, 0.0)),
            0.0,
        )
        * step_size
    )
    carry_decay = jnp.exp(log_accept)
    decay_now = jnp.exp(log_decay)
    owner_of = owner[:, 0]
    local_index = jnp.arange(n_req, dtype=jnp.int32)
    earlier = (owner_of[None, :] == owner_of[:, None]) & (
        local_index[None, :] < local_index[:, None]
    )
    rank_within = jnp.sum(earlier.astype(jnp.int32), axis=1)
    slot_index = owner_of * cap_group + rank_within
    fetched = lax.all_to_all(
        pool.astype(jnp.bfloat16), "rep", split_axis=0, concat_axis=0, tiled=True
    ).astype(pool.dtype)
    start_state = jnp.take(fetched, slot_index, axis=0)
    y_prior = decay_now[:, :, :, None] * jnp.einsum(
        "rhpn,rtn->rthp", start_state, c_float, precision=highest
    )
    accepted_state = carry_decay[:, :, None, None] * start_state + jnp.einsum(
        "rsh,rshp,rsn->rhpn", coef, x_heads, b_float, precision=highest
    )
    buffer = jnp.zeros(pool.shape, jnp.float32).at[slot_index].set(accepted_state)
    new_pool = lax.all_to_all(
        buffer.astype(jnp.bfloat16), "rep", split_axis=0, concat_axis=0, tiled=True
    ).astype(buffer.dtype)
    y_total = (y_local + y_prior).reshape(n_req * drafts, inner_here)
    gated = y_total * jax.nn.silu(z_all.astype(jnp.float32))
    sq_part = jnp.sum(gated * gated, axis=1)
    sq_hi = sq_part.astype(jnp.bfloat16)
    sq_lo = (sq_part - sq_hi.astype(jnp.float32)).astype(jnp.bfloat16)
    scaled = (gated * norm_gain[None, :]).astype(jnp.bfloat16)
    partial = jnp.dot(scaled, w_out, preferred_element_type=jnp.float32).astype(jnp.bfloat16)
    width = partial.shape[1]
    extra = jnp.zeros((partial.shape[0], 128), jnp.bfloat16)
    extra = extra.at[:, 0].set(sq_hi).at[:, 1].set(sq_lo)
    packed = jnp.concatenate([partial, extra], 1).reshape(n_blk, local_rows, width + 128)
    arrived = lax.all_to_all(packed, "blk", 0, 0, tiled=True).astype(jnp.float32)
    summed = jnp.sum(arrived, axis=0)
    inner_all = inner_here * n_blk
    mean_sq = (summed[:, width] + summed[:, width + 1]) / inner_all
    mixed = (summed[:, :width] * lax.rsqrt(mean_sq + 1e-05)[:, None]).astype(jnp.bfloat16)
    return (mixed[None], new_pool)


def solution(mesh):
    placed = (
        P("rep", "blk", None),
        P(None, "blk"),
        P(None, "blk"),
        P(),
        P(None, "blk"),
        P(None, "blk"),
        P(),
        P(None, "blk"),
        P("blk"),
        P("blk"),
        P("blk"),
        P("blk", None),
        P("rep", None, "blk"),
        P("rep", None, None),
        P("rep", "blk", None, None),
        P(),
        P("rep", None),
        P("rep"),
        P("rep"),
    )
    return jax.shard_map(
        shards,
        mesh=mesh,
        in_specs=placed,
        out_specs=(P("rep", "blk", None), P("rep", "blk", None, None)),
        check_vma=False,
    )
```

```python
import functools

import jax
import jax.numpy as jnp
from jax import lax
from jax.experimental import pallas as pl
from jax.experimental.pallas import tpu as pltpu
from jax.sharding import PartitionSpec as P

MESH = pl.DeviceIdType.MESH
AXES = ("blk", "rep")


def exchange_kernel(n, axis, gather, src_ref, dst_ref, send_sem, recv_sem, local_sem):
    me = lax.axis_index(axis)
    coords = {name: lax.axis_index(name) for name in AXES}

    def device_of(peer):
        return tuple(peer if name == axis else coords[name] for name in AXES)

    barrier = pltpu.get_barrier_semaphore()
    for offset in range(1, n):
        peer = lax.rem(me + offset, n)
        pl.semaphore_signal(barrier, inc=1, device_id=device_of(peer), device_id_type=MESH)
    pl.semaphore_wait(barrier, n - 1)
    local = pltpu.make_async_copy(src_ref if gather else src_ref.at[me], dst_ref.at[me], local_sem)
    local.start()
    copies = []
    for offset in range(1, n):
        peer = lax.rem(me + offset, n)
        copy = pltpu.make_async_remote_copy(
            src_ref=src_ref if gather else src_ref.at[peer],
            dst_ref=dst_ref.at[me],
            send_sem=send_sem.at[offset],
            recv_sem=recv_sem.at[offset],
            device_id=device_of(peer),
            device_id_type=MESH,
        )
        copy.start()
        copies.append(copy)
    local.wait()
    for copy in copies:
        copy.wait()


def exchange(src, axis, gather, collective_id):
    n = lax.axis_size(axis)
    block = src.shape if gather else src.shape[1:]
    return pl.pallas_call(
        functools.partial(exchange_kernel, n, axis, gather),
        out_shape=jax.ShapeDtypeStruct((n,) + tuple(block), src.dtype),
        in_specs=[pl.BlockSpec(memory_space=pl.ANY)],
        out_specs=pl.BlockSpec(memory_space=pl.ANY),
        scratch_shapes=[
            pltpu.SemaphoreType.DMA((n,)),
            pltpu.SemaphoreType.DMA((n,)),
            pltpu.SemaphoreType.DMA,
        ],
        compiler_params=pltpu.CompilerParams(collective_id=collective_id, has_side_effects=True),
    )(src)


def convolve(edge_cells, fresh_cells, kernel, edge_mask):
    sequence = jnp.concatenate(
        [edge_cells * edge_mask[:, :, None].astype(edge_cells.dtype), fresh_cells], 1
    ).astype(jnp.float32)
    steps_count = fresh_cells.shape[1]
    summed = kernel[0] * sequence[:, 0:steps_count]
    for offset in range(1, kernel.shape[0]):
        summed = summed + kernel[offset] * sequence[:, offset : offset + steps_count]
    return jax.nn.silu(summed).astype(jnp.bfloat16)


def shards(
    hidden_in,
    w_z,
    w_x,
    w_bc,
    w_dt,
    conv_x,
    conv_bc,
    dt_bias,
    a_log,
    d_skip,
    norm_gain,
    w_out,
    edge_x,
    edge_bc,
    pool,
    tenant_sizes,
    owner,
    accepted,
    prompt_len,
):
    highest = lax.Precision.HIGHEST
    rows_in = hidden_in[0]
    local_rows = rows_in.shape[0]
    n_req = edge_x.shape[0]
    drafts = local_rows * lax.axis_size("blk") // n_req
    state_dim = w_bc.shape[1] // 2
    heads_here = w_dt.shape[1]
    inner_here = w_z.shape[1]
    head_dim = inner_here // heads_here
    slots_here = pool.shape[0]
    cap_group = slots_here // lax.axis_size("rep")
    weights_in = (w_z, w_x, w_dt, w_bc)
    n_blk = lax.axis_size("blk")
    block_rows = exchange(rows_in, "blk", True, 0).reshape(n_blk * local_rows, rows_in.shape[1])
    projected = jnp.concatenate(
        [
            jnp.dot(block_rows, weight_cols, preferred_element_type=jnp.float32)
            for weight_cols in weights_in
        ],
        1,
    ).astype(jnp.bfloat16)
    z_all = projected[:, :inner_here]
    u_all = projected[:, inner_here : 2 * inner_here]
    dt_raw = projected[:, 2 * inner_here : 2 * inner_here + heads_here]
    bc_all = projected[:, 2 * inner_here + heads_here :]
    edge_len = edge_x.shape[1]
    edge_mask = prompt_len[:, None] >= (edge_len - jnp.arange(edge_len, dtype=jnp.int32))[None, :]
    x_conv = convolve(edge_x, u_all.reshape(n_req, drafts, inner_here), conv_x, edge_mask)
    bc_conv = convolve(edge_bc, bc_all.reshape(n_req, drafts, 2 * state_dim), conv_bc, edge_mask)
    b_half = bc_conv[:, :, :state_dim]
    c_half = bc_conv[:, :, state_dim:]
    b_float = b_half.astype(jnp.float32)
    c_float = c_half.astype(jnp.float32)
    x_heads = x_conv.reshape(n_req, drafts, heads_here, head_dim).astype(jnp.float32)
    req_index = lax.axis_index("rep") * n_req + jnp.arange(n_req, dtype=jnp.int32)
    tenant_ends = jnp.cumsum(tenant_sizes)
    tenant_id = jnp.sum((req_index[:, None] >= tenant_ends[None, :-1]).astype(jnp.int32), axis=1)
    tenant_pick = (
        tenant_id[:, None] == jnp.arange(tenant_sizes.shape[0], dtype=jnp.int32)[None, :]
    ).astype(jnp.float32)
    bias_req = jnp.dot(tenant_pick, dt_bias, precision=highest)
    step_size = jax.nn.softplus(
        dt_raw.reshape(n_req, drafts, heads_here).astype(jnp.float32) + bias_req[:, None, :]
    )
    log_decay = jnp.cumsum(step_size * (-jnp.exp(a_log))[None, None, :], axis=1)
    draft_index = jnp.arange(drafts, dtype=jnp.int32)
    causal = draft_index[:, None] >= draft_index[None, :]
    scores = jnp.einsum("rtn,rsn->rts", c_float, b_float, precision=highest)
    log_gap = log_decay[:, :, None, :] - log_decay[:, None, :, :]
    weight = (
        jnp.where(causal[None, :, :, None], jnp.exp(jnp.minimum(log_gap, 0.0)), 0.0)
        * step_size[:, None, :, :]
        * scores[:, :, :, None]
    )
    y_local = (
        jnp.einsum("rtsh,rshp->rthp", weight, x_heads, precision=highest)
        + d_skip[None, None, :, None] * x_heads
    )
    pick_last = (draft_index[None, :] == accepted[:, None] - 1).astype(jnp.float32)
    log_accept = jnp.sum(pick_last[:, :, None] * log_decay, axis=1)
    keep_draft = draft_index[None, :] < accepted[:, None]
    coef = (
        jnp.where(
            keep_draft[:, :, None],
            jnp.exp(jnp.minimum(log_accept[:, None, :] - log_decay, 0.0)),
            0.0,
        )
        * step_size
    )
    carry_decay = jnp.exp(log_accept)
    decay_now = jnp.exp(log_decay)
    owner_of = owner[:, 0]
    local_index = jnp.arange(n_req, dtype=jnp.int32)
    earlier = (owner_of[None, :] == owner_of[:, None]) & (
        local_index[None, :] < local_index[:, None]
    )
    rank_within = jnp.sum(earlier.astype(jnp.int32), axis=1)
    slot_index = owner_of * cap_group + rank_within
    fetched = lax.all_to_all(
        pool.astype(jnp.bfloat16), "rep", split_axis=0, concat_axis=0, tiled=True
    ).astype(pool.dtype)
    start_state = jnp.take(fetched, slot_index, axis=0)
    y_prior = decay_now[:, :, :, None] * jnp.einsum(
        "rhpn,rtn->rthp", start_state, c_float, precision=highest
    )
    accepted_state = carry_decay[:, :, None, None] * start_state + jnp.einsum(
        "rsh,rshp,rsn->rhpn", coef, x_heads, b_float, precision=highest
    )
    buffer = jnp.zeros(pool.shape, jnp.float32).at[slot_index].set(accepted_state)
    new_pool = lax.all_to_all(
        buffer.astype(jnp.bfloat16), "rep", split_axis=0, concat_axis=0, tiled=True
    ).astype(buffer.dtype)
    y_total = (y_local + y_prior).reshape(n_req * drafts, inner_here)
    gated = y_total * jax.nn.silu(z_all.astype(jnp.float32))
    sq_part = jnp.sum(gated * gated, axis=1)
    sq_hi = sq_part.astype(jnp.bfloat16)
    sq_lo = (sq_part - sq_hi.astype(jnp.float32)).astype(jnp.bfloat16)
    scaled = (gated * norm_gain[None, :]).astype(jnp.bfloat16)
    partial = jnp.dot(scaled, w_out, preferred_element_type=jnp.float32).astype(jnp.bfloat16)
    width = partial.shape[1]
    extra = jnp.zeros((partial.shape[0], 128), jnp.bfloat16)
    extra = extra.at[:, 0].set(sq_hi).at[:, 1].set(sq_lo)
    packed = jnp.concatenate([partial, extra], 1).reshape(n_blk, local_rows, width + 128)
    arrived = exchange(packed, "blk", False, 1).astype(jnp.float32)
    summed = jnp.sum(arrived, axis=0)
    inner_all = inner_here * n_blk
    mean_sq = (summed[:, width] + summed[:, width + 1]) / inner_all
    mixed = (summed[:, :width] * lax.rsqrt(mean_sq + 1e-05)[:, None]).astype(jnp.bfloat16)
    return (mixed[None], new_pool)


def solution(mesh):
    placed = (
        P("rep", "blk", None),
        P(None, "blk"),
        P(None, "blk"),
        P(),
        P(None, "blk"),
        P(None, "blk"),
        P(),
        P(None, "blk"),
        P("blk"),
        P("blk"),
        P("blk"),
        P("blk", None),
        P("rep", None, "blk"),
        P("rep", None, None),
        P("rep", "blk", None, None),
        P(),
        P("rep", None),
        P("rep"),
        P("rep"),
    )
    return jax.shard_map(
        shards,
        mesh=mesh,
        in_specs=placed,
        out_specs=(P("rep", "blk", None), P("rep", "blk", None, None)),
        check_vma=False,
    )
```

```python
import functools

import jax
import jax.numpy as jnp
from jax import lax
from jax.experimental import pallas as pl
from jax.experimental.pallas import tpu as pltpu
from jax.sharding import PartitionSpec as P

MESH = pl.DeviceIdType.MESH
AXES = ("by", "bz", "rep")
BLK = ("by", "bz")
Y_CHIPS = 4


def exchange_kernel(n, axis, gather, src_ref, dst_ref, send_sem, recv_sem, local_sem):
    me = lax.axis_index(axis)
    coords = {name: lax.axis_index(name) for name in AXES}

    def device_of(peer):
        return tuple(peer if name == axis else coords[name] for name in AXES)

    barrier = pltpu.get_barrier_semaphore()
    for offset in range(1, n):
        peer = lax.rem(me + offset, n)
        pl.semaphore_signal(barrier, inc=1, device_id=device_of(peer), device_id_type=MESH)
    pl.semaphore_wait(barrier, n - 1)
    local = pltpu.make_async_copy(src_ref if gather else src_ref.at[me], dst_ref.at[me], local_sem)
    local.start()
    copies = []
    for offset in range(1, n):
        peer = lax.rem(me + offset, n)
        copy = pltpu.make_async_remote_copy(
            src_ref=src_ref if gather else src_ref.at[peer],
            dst_ref=dst_ref.at[me],
            send_sem=send_sem.at[offset],
            recv_sem=recv_sem.at[offset],
            device_id=device_of(peer),
            device_id_type=MESH,
        )
        copy.start()
        copies.append(copy)
    local.wait()
    for copy in copies:
        copy.wait()


def exchange(src, axis, gather, collective_id):
    n = lax.axis_size(axis)
    block = src.shape if gather else src.shape[1:]
    return pl.pallas_call(
        functools.partial(exchange_kernel, n, axis, gather),
        out_shape=jax.ShapeDtypeStruct((n,) + tuple(block), src.dtype),
        in_specs=[pl.BlockSpec(memory_space=pl.ANY)],
        out_specs=pl.BlockSpec(memory_space=pl.ANY),
        scratch_shapes=[
            pltpu.SemaphoreType.DMA((n,)),
            pltpu.SemaphoreType.DMA((n,)),
            pltpu.SemaphoreType.DMA,
        ],
        compiler_params=pltpu.CompilerParams(collective_id=collective_id, has_side_effects=True),
    )(src)


def convolve(edge_cells, fresh_cells, kernel, edge_mask):
    sequence = jnp.concatenate(
        [edge_cells * edge_mask[:, :, None].astype(edge_cells.dtype), fresh_cells], 1
    ).astype(jnp.float32)
    steps_count = fresh_cells.shape[1]
    summed = kernel[0] * sequence[:, 0:steps_count]
    for offset in range(1, kernel.shape[0]):
        summed = summed + kernel[offset] * sequence[:, offset : offset + steps_count]
    return jax.nn.silu(summed).astype(jnp.bfloat16)


def shards(
    hidden_in,
    w_z,
    w_x,
    w_bc,
    w_dt,
    conv_x,
    conv_bc,
    dt_bias,
    a_log,
    d_skip,
    norm_gain,
    w_out,
    edge_x,
    edge_bc,
    pool,
    tenant_sizes,
    owner,
    accepted,
    prompt_len,
):
    highest = lax.Precision.HIGHEST
    rows_in = hidden_in[0]
    local_rows = rows_in.shape[0]
    n_req = edge_x.shape[0]
    drafts = local_rows * lax.axis_size(BLK) // n_req
    state_dim = w_bc.shape[1] // 2
    heads_here = w_dt.shape[1]
    inner_here = w_z.shape[1]
    head_dim = inner_here // heads_here
    slots_here = pool.shape[0]
    cap_group = slots_here // lax.axis_size("rep")
    weights_in = (w_z, w_x, w_dt, w_bc)
    n_blk = lax.axis_size(BLK)
    along_z = exchange(rows_in, "bz", True, 0)
    block_rows = exchange(along_z, "by", True, 1).reshape(n_blk * local_rows, rows_in.shape[1])
    projected = jnp.concatenate(
        [
            jnp.dot(block_rows, weight_cols, preferred_element_type=jnp.float32)
            for weight_cols in weights_in
        ],
        1,
    ).astype(jnp.bfloat16)
    z_all = projected[:, :inner_here]
    u_all = projected[:, inner_here : 2 * inner_here]
    dt_raw = projected[:, 2 * inner_here : 2 * inner_here + heads_here]
    bc_all = projected[:, 2 * inner_here + heads_here :]
    edge_len = edge_x.shape[1]
    edge_mask = prompt_len[:, None] >= (edge_len - jnp.arange(edge_len, dtype=jnp.int32))[None, :]
    x_conv = convolve(edge_x, u_all.reshape(n_req, drafts, inner_here), conv_x, edge_mask)
    bc_conv = convolve(edge_bc, bc_all.reshape(n_req, drafts, 2 * state_dim), conv_bc, edge_mask)
    b_half = bc_conv[:, :, :state_dim]
    c_half = bc_conv[:, :, state_dim:]
    b_float = b_half.astype(jnp.float32)
    c_float = c_half.astype(jnp.float32)
    x_heads = x_conv.reshape(n_req, drafts, heads_here, head_dim).astype(jnp.float32)
    req_index = lax.axis_index("rep") * n_req + jnp.arange(n_req, dtype=jnp.int32)
    tenant_ends = jnp.cumsum(tenant_sizes)
    tenant_id = jnp.sum((req_index[:, None] >= tenant_ends[None, :-1]).astype(jnp.int32), axis=1)
    tenant_pick = (
        tenant_id[:, None] == jnp.arange(tenant_sizes.shape[0], dtype=jnp.int32)[None, :]
    ).astype(jnp.float32)
    bias_req = jnp.dot(tenant_pick, dt_bias, precision=highest)
    step_size = jax.nn.softplus(
        dt_raw.reshape(n_req, drafts, heads_here).astype(jnp.float32) + bias_req[:, None, :]
    )
    log_decay = jnp.cumsum(step_size * (-jnp.exp(a_log))[None, None, :], axis=1)
    draft_index = jnp.arange(drafts, dtype=jnp.int32)
    causal = draft_index[:, None] >= draft_index[None, :]
    scores = jnp.einsum("rtn,rsn->rts", c_float, b_float, precision=highest)
    log_gap = log_decay[:, :, None, :] - log_decay[:, None, :, :]
    weight = (
        jnp.where(causal[None, :, :, None], jnp.exp(jnp.minimum(log_gap, 0.0)), 0.0)
        * step_size[:, None, :, :]
        * scores[:, :, :, None]
    )
    y_local = (
        jnp.einsum("rtsh,rshp->rthp", weight, x_heads, precision=highest)
        + d_skip[None, None, :, None] * x_heads
    )
    pick_last = (draft_index[None, :] == accepted[:, None] - 1).astype(jnp.float32)
    log_accept = jnp.sum(pick_last[:, :, None] * log_decay, axis=1)
    keep_draft = draft_index[None, :] < accepted[:, None]
    coef = (
        jnp.where(
            keep_draft[:, :, None],
            jnp.exp(jnp.minimum(log_accept[:, None, :] - log_decay, 0.0)),
            0.0,
        )
        * step_size
    )
    carry_decay = jnp.exp(log_accept)
    decay_now = jnp.exp(log_decay)
    owner_of = owner[:, 0]
    local_index = jnp.arange(n_req, dtype=jnp.int32)
    earlier = (owner_of[None, :] == owner_of[:, None]) & (
        local_index[None, :] < local_index[:, None]
    )
    rank_within = jnp.sum(earlier.astype(jnp.int32), axis=1)
    slot_index = owner_of * cap_group + rank_within
    fetched = lax.all_to_all(
        pool.astype(jnp.bfloat16), "rep", split_axis=0, concat_axis=0, tiled=True
    ).astype(pool.dtype)
    start_state = jnp.take(fetched, slot_index, axis=0)
    y_prior = decay_now[:, :, :, None] * jnp.einsum(
        "rhpn,rtn->rthp", start_state, c_float, precision=highest
    )
    accepted_state = carry_decay[:, :, None, None] * start_state + jnp.einsum(
        "rsh,rshp,rsn->rhpn", coef, x_heads, b_float, precision=highest
    )
    buffer = jnp.zeros(pool.shape, jnp.float32).at[slot_index].set(accepted_state)
    new_pool = lax.all_to_all(
        buffer.astype(jnp.bfloat16), "rep", split_axis=0, concat_axis=0, tiled=True
    ).astype(buffer.dtype)
    y_total = (y_local + y_prior).reshape(n_req * drafts, inner_here)
    gated = y_total * jax.nn.silu(z_all.astype(jnp.float32))
    sq_part = jnp.sum(gated * gated, axis=1)
    sq_hi = sq_part.astype(jnp.bfloat16)
    sq_lo = (sq_part - sq_hi.astype(jnp.float32)).astype(jnp.bfloat16)
    scaled = (gated * norm_gain[None, :]).astype(jnp.bfloat16)
    partial = jnp.dot(scaled, w_out, preferred_element_type=jnp.float32).astype(jnp.bfloat16)
    width = partial.shape[1]
    extra = jnp.zeros((partial.shape[0], 128), jnp.bfloat16)
    extra = extra.at[:, 0].set(sq_hi).at[:, 1].set(sq_lo)
    n_y = lax.axis_size("by")
    packed = jnp.concatenate([partial, extra], 1).reshape(n_y, n_blk // n_y, local_rows, width + 128)
    half_sum = jnp.sum(exchange(packed, "by", False, 2).astype(jnp.float32), axis=0)
    sq_mid = half_sum[:, :, width] + half_sum[:, :, width + 1]
    sq_mid_hi = sq_mid.astype(jnp.bfloat16)
    sq_mid_lo = (sq_mid - sq_mid_hi.astype(jnp.float32)).astype(jnp.bfloat16)
    half_packed = (
        half_sum.astype(jnp.bfloat16).at[:, :, width].set(sq_mid_hi).at[:, :, width + 1].set(sq_mid_lo)
    )
    summed = jnp.sum(exchange(half_packed, "bz", False, 3).astype(jnp.float32), axis=0)
    inner_all = inner_here * n_blk
    mean_sq = (summed[:, width] + summed[:, width + 1]) / inner_all
    mixed = (summed[:, :width] * lax.rsqrt(mean_sq + 1e-05)[:, None]).astype(jnp.bfloat16)
    return (mixed[None], new_pool)


def solution(mesh):
    placed = (
        P("rep", "blk", None),
        P(None, "blk"),
        P(None, "blk"),
        P(),
        P(None, "blk"),
        P(None, "blk"),
        P(),
        P(None, "blk"),
        P("blk"),
        P("blk"),
        P("blk"),
        P("blk", None),
        P("rep", None, "blk"),
        P("rep", None, None),
        P("rep", "blk", None, None),
        P(),
        P("rep", None),
        P("rep"),
        P("rep"),
    )
    n_blk, n_rep = mesh.shape["blk"], mesh.shape["rep"]
    split_mesh = jax.sharding.Mesh(
        mesh.devices.reshape(Y_CHIPS, n_blk // Y_CHIPS, n_rep), AXES
    )
    placed = tuple(P(*[BLK if part == "blk" else part for part in spec]) for spec in placed)
    return jax.shard_map(
        shards,
        mesh=split_mesh,
        in_specs=placed,
        out_specs=(P("rep", BLK, None), P("rep", BLK, None, None)),
        check_vma=False,
    )
```

```python
import functools

import jax
import jax.numpy as jnp
from jax import lax
from jax.experimental import pallas as pl
from jax.experimental.pallas import tpu as pltpu
from jax.sharding import PartitionSpec as P

MESH = pl.DeviceIdType.MESH
AXES = ("by", "bz", "rep")
BLK = ("by", "bz")
Y_CHIPS = 4


def exchange_kernel(n, axis, gather, src_ref, dst_ref, send_sem, recv_sem, local_sem):
    me = lax.axis_index(axis)
    coords = {name: lax.axis_index(name) for name in AXES}

    def device_of(peer):
        return tuple(peer if name == axis else coords[name] for name in AXES)

    barrier = pltpu.get_barrier_semaphore()
    for offset in range(1, n):
        peer = lax.rem(me + offset, n)
        pl.semaphore_signal(barrier, inc=1, device_id=device_of(peer), device_id_type=MESH)
    pl.semaphore_wait(barrier, n - 1)
    local = pltpu.make_async_copy(src_ref if gather else src_ref.at[me], dst_ref.at[me], local_sem)
    local.start()
    copies = []
    for offset in range(1, n):
        peer = lax.rem(me + offset, n)
        copy = pltpu.make_async_remote_copy(
            src_ref=src_ref if gather else src_ref.at[peer],
            dst_ref=dst_ref.at[me],
            send_sem=send_sem.at[offset],
            recv_sem=recv_sem.at[offset],
            device_id=device_of(peer),
            device_id_type=MESH,
        )
        copy.start()
        copies.append(copy)
    local.wait()
    for copy in copies:
        copy.wait()


def exchange(src, axis, gather, collective_id):
    n = lax.axis_size(axis)
    block = src.shape if gather else src.shape[1:]
    return pl.pallas_call(
        functools.partial(exchange_kernel, n, axis, gather),
        out_shape=jax.ShapeDtypeStruct((n,) + tuple(block), src.dtype),
        in_specs=[pl.BlockSpec(memory_space=pl.ANY)],
        out_specs=pl.BlockSpec(memory_space=pl.ANY),
        scratch_shapes=[
            pltpu.SemaphoreType.DMA((n,)),
            pltpu.SemaphoreType.DMA((n,)),
            pltpu.SemaphoreType.DMA,
        ],
        compiler_params=pltpu.CompilerParams(collective_id=collective_id, has_side_effects=True),
    )(src)


def convolve(edge_cells, fresh_cells, kernel, edge_mask):
    sequence = jnp.concatenate(
        [edge_cells * edge_mask[:, :, None].astype(edge_cells.dtype), fresh_cells], 1
    ).astype(jnp.float32)
    steps_count = fresh_cells.shape[1]
    summed = kernel[0] * sequence[:, 0:steps_count]
    for offset in range(1, kernel.shape[0]):
        summed = summed + kernel[offset] * sequence[:, offset : offset + steps_count]
    return jax.nn.silu(summed).astype(jnp.bfloat16)


def shards(
    hidden_in,
    w_z,
    w_x,
    w_bc,
    w_dt,
    conv_x,
    conv_bc,
    dt_bias,
    a_log,
    d_skip,
    norm_gain,
    w_out,
    edge_x,
    edge_bc,
    pool,
    tenant_sizes,
    owner,
    accepted,
    prompt_len,
):
    highest = lax.Precision.HIGHEST
    rows_in = hidden_in[0]
    local_rows = rows_in.shape[0]
    n_req = edge_x.shape[0]
    drafts = local_rows * lax.axis_size(BLK) // n_req
    state_dim = w_bc.shape[1] // 2
    heads_here = w_dt.shape[1]
    inner_here = w_z.shape[1]
    head_dim = inner_here // heads_here
    slots_here = pool.shape[0]
    cap_group = slots_here // lax.axis_size("rep")
    weights_in = (w_z, w_x, w_dt, w_bc)
    n_blk = lax.axis_size(BLK)
    along_z = exchange(rows_in, "bz", True, 0)
    block_rows = exchange(along_z, "by", True, 1).reshape(n_blk * local_rows, rows_in.shape[1])
    projected = jnp.concatenate(
        [
            jnp.dot(block_rows, weight_cols, preferred_element_type=jnp.float32)
            for weight_cols in weights_in
        ],
        1,
    ).astype(jnp.bfloat16)
    z_all = projected[:, :inner_here]
    u_all = projected[:, inner_here : 2 * inner_here]
    dt_raw = projected[:, 2 * inner_here : 2 * inner_here + heads_here]
    bc_all = projected[:, 2 * inner_here + heads_here :]
    edge_len = edge_x.shape[1]
    edge_mask = prompt_len[:, None] >= (edge_len - jnp.arange(edge_len, dtype=jnp.int32))[None, :]
    x_conv = convolve(edge_x, u_all.reshape(n_req, drafts, inner_here), conv_x, edge_mask)
    bc_conv = convolve(edge_bc, bc_all.reshape(n_req, drafts, 2 * state_dim), conv_bc, edge_mask)
    b_half = bc_conv[:, :, :state_dim]
    c_half = bc_conv[:, :, state_dim:]
    b_float = b_half.astype(jnp.float32)
    c_float = c_half.astype(jnp.float32)
    x_heads = x_conv.reshape(n_req, drafts, heads_here, head_dim).astype(jnp.float32)
    req_index = lax.axis_index("rep") * n_req + jnp.arange(n_req, dtype=jnp.int32)
    tenant_ends = jnp.cumsum(tenant_sizes)
    tenant_id = jnp.sum((req_index[:, None] >= tenant_ends[None, :-1]).astype(jnp.int32), axis=1)
    tenant_pick = (
        tenant_id[:, None] == jnp.arange(tenant_sizes.shape[0], dtype=jnp.int32)[None, :]
    ).astype(jnp.float32)
    bias_req = jnp.dot(tenant_pick, dt_bias, precision=highest)
    step_size = jax.nn.softplus(
        dt_raw.reshape(n_req, drafts, heads_here).astype(jnp.float32) + bias_req[:, None, :]
    )
    log_decay = jnp.cumsum(step_size * (-jnp.exp(a_log))[None, None, :], axis=1)
    draft_index = jnp.arange(drafts, dtype=jnp.int32)
    causal = draft_index[:, None] >= draft_index[None, :]
    scores = jnp.einsum("rtn,rsn->rts", c_float, b_float, precision=highest)
    log_gap = log_decay[:, :, None, :] - log_decay[:, None, :, :]
    weight = (
        jnp.where(causal[None, :, :, None], jnp.exp(jnp.minimum(log_gap, 0.0)), 0.0)
        * step_size[:, None, :, :]
        * scores[:, :, :, None]
    )
    y_local = (
        jnp.einsum("rtsh,rshp->rthp", weight, x_heads, precision=highest)
        + d_skip[None, None, :, None] * x_heads
    )
    pick_last = (draft_index[None, :] == accepted[:, None] - 1).astype(jnp.float32)
    log_accept = jnp.sum(pick_last[:, :, None] * log_decay, axis=1)
    keep_draft = draft_index[None, :] < accepted[:, None]
    coef = (
        jnp.where(
            keep_draft[:, :, None],
            jnp.exp(jnp.minimum(log_accept[:, None, :] - log_decay, 0.0)),
            0.0,
        )
        * step_size
    )
    carry_decay = jnp.exp(log_accept)
    decay_now = jnp.exp(log_decay)
    owner_of = owner[:, 0]
    local_index = jnp.arange(n_req, dtype=jnp.int32)
    earlier = (owner_of[None, :] == owner_of[:, None]) & (
        local_index[None, :] < local_index[:, None]
    )
    rank_within = jnp.sum(earlier.astype(jnp.int32), axis=1)
    slot_index = owner_of * cap_group + rank_within
    fetched = lax.all_to_all(
        pool.astype(jnp.bfloat16), "rep", split_axis=0, concat_axis=0, tiled=True
    ).astype(pool.dtype)
    slots = jnp.arange(slots_here, dtype=jnp.int32)
    slot_pick = (slots[:, None] == slot_index[None, :]).astype(jnp.int32)
    slot_used = jnp.sum(slot_pick, axis=1) > 0
    slot_req = jnp.sum(slot_pick * local_index[None, :], axis=1)

    def to_slots(per_req):
        taken = jnp.take(per_req, slot_req, axis=0)
        return jnp.where(slot_used.reshape((-1,) + (1,) * (per_req.ndim - 1)), taken, 0.0)

    prior_slot = to_slots(decay_now)[:, :, :, None] * jnp.einsum(
        "jhpn,jtn->jthp", fetched, to_slots(c_float), precision=highest
    )
    y_prior = jnp.take(prior_slot, slot_index, axis=0)
    buffer = to_slots(carry_decay)[:, :, None, None] * fetched + jnp.einsum(
        "jsh,jshp,jsn->jhpn", to_slots(coef), to_slots(x_heads), to_slots(b_float), precision=highest
    )
    new_pool = lax.all_to_all(
        buffer.astype(jnp.bfloat16), "rep", split_axis=0, concat_axis=0, tiled=True
    ).astype(buffer.dtype)
    y_total = (y_local + y_prior).reshape(n_req * drafts, inner_here)
    gated = y_total * jax.nn.silu(z_all.astype(jnp.float32))
    sq_part = jnp.sum(gated * gated, axis=1)
    sq_hi = sq_part.astype(jnp.bfloat16)
    sq_lo = (sq_part - sq_hi.astype(jnp.float32)).astype(jnp.bfloat16)
    scaled = (gated * norm_gain[None, :]).astype(jnp.bfloat16)
    partial = jnp.dot(scaled, w_out, preferred_element_type=jnp.float32).astype(jnp.bfloat16)
    width = partial.shape[1]
    extra = jnp.zeros((partial.shape[0], 128), jnp.bfloat16)
    extra = extra.at[:, 0].set(sq_hi).at[:, 1].set(sq_lo)
    n_y = lax.axis_size("by")
    packed = jnp.concatenate([partial, extra], 1).reshape(n_y, n_blk // n_y, local_rows, width + 128)
    half_sum = jnp.sum(exchange(packed, "by", False, 2).astype(jnp.float32), axis=0)
    sq_mid = half_sum[:, :, width] + half_sum[:, :, width + 1]
    sq_mid_hi = sq_mid.astype(jnp.bfloat16)
    sq_mid_lo = (sq_mid - sq_mid_hi.astype(jnp.float32)).astype(jnp.bfloat16)
    half_packed = (
        half_sum.astype(jnp.bfloat16).at[:, :, width].set(sq_mid_hi).at[:, :, width + 1].set(sq_mid_lo)
    )
    summed = jnp.sum(exchange(half_packed, "bz", False, 3).astype(jnp.float32), axis=0)
    inner_all = inner_here * n_blk
    mean_sq = (summed[:, width] + summed[:, width + 1]) / inner_all
    mixed = (summed[:, :width] * lax.rsqrt(mean_sq + 1e-05)[:, None]).astype(jnp.bfloat16)
    return (mixed[None], new_pool)


def solution(mesh):
    placed = (
        P("rep", "blk", None),
        P(None, "blk"),
        P(None, "blk"),
        P(),
        P(None, "blk"),
        P(None, "blk"),
        P(),
        P(None, "blk"),
        P("blk"),
        P("blk"),
        P("blk"),
        P("blk", None),
        P("rep", None, "blk"),
        P("rep", None, None),
        P("rep", "blk", None, None),
        P(),
        P("rep", None),
        P("rep"),
        P("rep"),
    )
    n_blk, n_rep = mesh.shape["blk"], mesh.shape["rep"]
    split_mesh = jax.sharding.Mesh(
        mesh.devices.reshape(Y_CHIPS, n_blk // Y_CHIPS, n_rep), AXES
    )
    placed = tuple(P(*[BLK if part == "blk" else part for part in spec]) for spec in placed)
    return jax.shard_map(
        shards,
        mesh=split_mesh,
        in_specs=placed,
        out_specs=(P("rep", BLK, None), P("rep", BLK, None, None)),
        check_vma=False,
    )
```

```python
import functools

import jax
import jax.numpy as jnp
from jax import lax
from jax.experimental import pallas as pl
from jax.experimental.pallas import tpu as pltpu
from jax.sharding import PartitionSpec as P

MESH = pl.DeviceIdType.MESH
AXES = ("by", "bz", "rep")
BLK = ("by", "bz")
Y_CHIPS = 4


def exchange_kernel(n, axis, gather, src_ref, dst_ref, send_sem, recv_sem, local_sem):
    me = lax.axis_index(axis)
    coords = {name: lax.axis_index(name) for name in AXES}

    def device_of(peer):
        return tuple(peer if name == axis else coords[name] for name in AXES)

    barrier = pltpu.get_barrier_semaphore()
    for offset in range(1, n):
        peer = lax.rem(me + offset, n)
        pl.semaphore_signal(barrier, inc=1, device_id=device_of(peer), device_id_type=MESH)
    pl.semaphore_wait(barrier, n - 1)
    local = pltpu.make_async_copy(src_ref if gather else src_ref.at[me], dst_ref.at[me], local_sem)
    local.start()
    copies = []
    for offset in range(1, n):
        peer = lax.rem(me + offset, n)
        copy = pltpu.make_async_remote_copy(
            src_ref=src_ref if gather else src_ref.at[peer],
            dst_ref=dst_ref.at[me],
            send_sem=send_sem.at[offset],
            recv_sem=recv_sem.at[offset],
            device_id=device_of(peer),
            device_id_type=MESH,
        )
        copy.start()
        copies.append(copy)
    local.wait()
    for copy in copies:
        copy.wait()


def ring4_kernel(axis, gather, src_ref, dst_ref, stage_ref, send_sem, recv_sem, local_sem):
    me = lax.axis_index(axis)
    coords = {name: lax.axis_index(name) for name in AXES}

    def device_of(peer):
        return tuple(peer if name == axis else coords[name] for name in AXES)

    right, left = lax.rem(me + 1, 4), lax.rem(me + 3, 4)
    opposite = lax.rem(me + 2, 4)
    half = dst_ref.shape[1] // 2
    first, second = pl.ds(0, half), pl.ds(half, half)

    def remote(src, dst, index, peer):
        copy = pltpu.make_async_remote_copy(
            src_ref=src,
            dst_ref=dst,
            send_sem=send_sem.at[index],
            recv_sem=recv_sem.at[index],
            device_id=device_of(peer),
            device_id_type=MESH,
        )
        copy.start()
        return copy

    barrier = pltpu.get_barrier_semaphore()
    for peer in (left, right):
        pl.semaphore_signal(barrier, inc=1, device_id=device_of(peer), device_id_type=MESH)
    pl.semaphore_wait(barrier, 2)
    local = pltpu.make_async_copy(src_ref if gather else src_ref.at[me], dst_ref.at[me], local_sem)
    local.start()
    to_right = remote(src_ref if gather else src_ref.at[right], dst_ref.at[me], 0, right)
    to_left = remote(src_ref if gather else src_ref.at[left], dst_ref.at[me], 1, left)
    if gather:
        to_right.wait_recv()
        pass_right = remote(dst_ref.at[left, first], dst_ref.at[left, first], 2, right)
        to_left.wait_recv()
        pass_left = remote(dst_ref.at[right, second], dst_ref.at[right, second], 3, left)
        to_right.wait_send()
        to_left.wait_send()
    else:
        stage_right = remote(src_ref.at[opposite, first], stage_ref.at[0], 2, right)
        stage_left = remote(src_ref.at[opposite, second], stage_ref.at[1], 3, left)
        stage_right.wait_recv()
        pass_right = remote(stage_ref.at[0], dst_ref.at[left, first], 4, right)
        stage_left.wait_recv()
        pass_left = remote(stage_ref.at[1], dst_ref.at[right, second], 5, left)
        stage_right.wait_send()
        stage_left.wait_send()
        to_right.wait()
        to_left.wait()
    local.wait()
    pass_right.wait()
    pass_left.wait()


def exchange4(src, axis, gather, collective_id):
    block = src.shape if gather else src.shape[1:]
    out = jax.ShapeDtypeStruct((4,) + tuple(block), src.dtype)
    stage = jax.ShapeDtypeStruct((2, block[0] // 2) + tuple(block[1:]), src.dtype)
    return pl.pallas_call(
        functools.partial(ring4_kernel, axis, gather),
        out_shape=(out, stage),
        in_specs=[pl.BlockSpec(memory_space=pl.ANY)],
        out_specs=(pl.BlockSpec(memory_space=pl.ANY), pl.BlockSpec(memory_space=pl.ANY)),
        scratch_shapes=[
            pltpu.SemaphoreType.DMA((6,)),
            pltpu.SemaphoreType.DMA((6,)),
            pltpu.SemaphoreType.DMA,
        ],
        compiler_params=pltpu.CompilerParams(collective_id=collective_id, has_side_effects=True),
    )(src)[0]


def exchange(src, axis, gather, collective_id):
    n = lax.axis_size(axis)
    block = src.shape if gather else src.shape[1:]
    return pl.pallas_call(
        functools.partial(exchange_kernel, n, axis, gather),
        out_shape=jax.ShapeDtypeStruct((n,) + tuple(block), src.dtype),
        in_specs=[pl.BlockSpec(memory_space=pl.ANY)],
        out_specs=pl.BlockSpec(memory_space=pl.ANY),
        scratch_shapes=[
            pltpu.SemaphoreType.DMA((n,)),
            pltpu.SemaphoreType.DMA((n,)),
            pltpu.SemaphoreType.DMA,
        ],
        compiler_params=pltpu.CompilerParams(collective_id=collective_id, has_side_effects=True),
    )(src)


def convolve(edge_cells, fresh_cells, kernel, edge_mask):
    sequence = jnp.concatenate(
        [edge_cells * edge_mask[:, :, None].astype(edge_cells.dtype), fresh_cells], 1
    ).astype(jnp.float32)
    steps_count = fresh_cells.shape[1]
    summed = kernel[0] * sequence[:, 0:steps_count]
    for offset in range(1, kernel.shape[0]):
        summed = summed + kernel[offset] * sequence[:, offset : offset + steps_count]
    return jax.nn.silu(summed).astype(jnp.bfloat16)


def shards(
    hidden_in,
    w_z,
    w_x,
    w_bc,
    w_dt,
    conv_x,
    conv_bc,
    dt_bias,
    a_log,
    d_skip,
    norm_gain,
    w_out,
    edge_x,
    edge_bc,
    pool,
    tenant_sizes,
    owner,
    accepted,
    prompt_len,
):
    highest = lax.Precision.HIGHEST
    rows_in = hidden_in[0]
    local_rows = rows_in.shape[0]
    n_req = edge_x.shape[0]
    drafts = local_rows * lax.axis_size(BLK) // n_req
    state_dim = w_bc.shape[1] // 2
    heads_here = w_dt.shape[1]
    inner_here = w_z.shape[1]
    head_dim = inner_here // heads_here
    slots_here = pool.shape[0]
    cap_group = slots_here // lax.axis_size("rep")
    weights_in = (w_z, w_x, w_dt, w_bc)
    n_blk = lax.axis_size(BLK)
    along_z = exchange(rows_in, "bz", True, 0)
    block_rows = exchange4(along_z, "by", True, 1).reshape(n_blk * local_rows, rows_in.shape[1])
    projected = jnp.concatenate(
        [
            jnp.dot(block_rows, weight_cols, preferred_element_type=jnp.float32)
            for weight_cols in weights_in
        ],
        1,
    ).astype(jnp.bfloat16)
    z_all = projected[:, :inner_here]
    u_all = projected[:, inner_here : 2 * inner_here]
    dt_raw = projected[:, 2 * inner_here : 2 * inner_here + heads_here]
    bc_all = projected[:, 2 * inner_here + heads_here :]
    edge_len = edge_x.shape[1]
    edge_mask = prompt_len[:, None] >= (edge_len - jnp.arange(edge_len, dtype=jnp.int32))[None, :]
    x_conv = convolve(edge_x, u_all.reshape(n_req, drafts, inner_here), conv_x, edge_mask)
    bc_conv = convolve(edge_bc, bc_all.reshape(n_req, drafts, 2 * state_dim), conv_bc, edge_mask)
    b_half = bc_conv[:, :, :state_dim]
    c_half = bc_conv[:, :, state_dim:]
    b_float = b_half.astype(jnp.float32)
    c_float = c_half.astype(jnp.float32)
    x_heads = x_conv.reshape(n_req, drafts, heads_here, head_dim).astype(jnp.float32)
    req_index = lax.axis_index("rep") * n_req + jnp.arange(n_req, dtype=jnp.int32)
    tenant_ends = jnp.cumsum(tenant_sizes)
    tenant_id = jnp.sum((req_index[:, None] >= tenant_ends[None, :-1]).astype(jnp.int32), axis=1)
    tenant_pick = (
        tenant_id[:, None] == jnp.arange(tenant_sizes.shape[0], dtype=jnp.int32)[None, :]
    ).astype(jnp.float32)
    bias_req = jnp.dot(tenant_pick, dt_bias, precision=highest)
    step_size = jax.nn.softplus(
        dt_raw.reshape(n_req, drafts, heads_here).astype(jnp.float32) + bias_req[:, None, :]
    )
    log_decay = jnp.cumsum(step_size * (-jnp.exp(a_log))[None, None, :], axis=1)
    draft_index = jnp.arange(drafts, dtype=jnp.int32)
    causal = draft_index[:, None] >= draft_index[None, :]
    scores = jnp.einsum("rtn,rsn->rts", c_float, b_float, precision=highest)
    log_gap = log_decay[:, :, None, :] - log_decay[:, None, :, :]
    weight = (
        jnp.where(causal[None, :, :, None], jnp.exp(jnp.minimum(log_gap, 0.0)), 0.0)
        * step_size[:, None, :, :]
        * scores[:, :, :, None]
    )
    y_local = (
        jnp.einsum("rtsh,rshp->rthp", weight, x_heads, precision=highest)
        + d_skip[None, None, :, None] * x_heads
    )
    pick_last = (draft_index[None, :] == accepted[:, None] - 1).astype(jnp.float32)
    log_accept = jnp.sum(pick_last[:, :, None] * log_decay, axis=1)
    keep_draft = draft_index[None, :] < accepted[:, None]
    coef = (
        jnp.where(
            keep_draft[:, :, None],
            jnp.exp(jnp.minimum(log_accept[:, None, :] - log_decay, 0.0)),
            0.0,
        )
        * step_size
    )
    carry_decay = jnp.exp(log_accept)
    decay_now = jnp.exp(log_decay)
    owner_of = owner[:, 0]
    local_index = jnp.arange(n_req, dtype=jnp.int32)
    earlier = (owner_of[None, :] == owner_of[:, None]) & (
        local_index[None, :] < local_index[:, None]
    )
    rank_within = jnp.sum(earlier.astype(jnp.int32), axis=1)
    slot_index = owner_of * cap_group + rank_within
    fetched = lax.all_to_all(
        pool.astype(jnp.bfloat16), "rep", split_axis=0, concat_axis=0, tiled=True
    ).astype(pool.dtype)
    slots = jnp.arange(slots_here, dtype=jnp.int32)
    slot_pick = (slots[:, None] == slot_index[None, :]).astype(jnp.int32)
    slot_used = jnp.sum(slot_pick, axis=1) > 0
    slot_req = jnp.sum(slot_pick * local_index[None, :], axis=1)

    def to_slots(per_req):
        taken = jnp.take(per_req, slot_req, axis=0)
        return jnp.where(slot_used.reshape((-1,) + (1,) * (per_req.ndim - 1)), taken, 0.0)

    prior_slot = to_slots(decay_now)[:, :, :, None] * jnp.einsum(
        "jhpn,jtn->jthp", fetched, to_slots(c_float), precision=highest
    )
    y_prior = jnp.take(prior_slot, slot_index, axis=0)
    buffer = to_slots(carry_decay)[:, :, None, None] * fetched + jnp.einsum(
        "jsh,jshp,jsn->jhpn", to_slots(coef), to_slots(x_heads), to_slots(b_float), precision=highest
    )
    new_pool = lax.all_to_all(
        buffer.astype(jnp.bfloat16), "rep", split_axis=0, concat_axis=0, tiled=True
    ).astype(buffer.dtype)
    y_total = (y_local + y_prior).reshape(n_req * drafts, inner_here)
    gated = y_total * jax.nn.silu(z_all.astype(jnp.float32))
    sq_part = jnp.sum(gated * gated, axis=1)
    sq_hi = sq_part.astype(jnp.bfloat16)
    sq_lo = (sq_part - sq_hi.astype(jnp.float32)).astype(jnp.bfloat16)
    scaled = (gated * norm_gain[None, :]).astype(jnp.bfloat16)
    partial = jnp.dot(scaled, w_out, preferred_element_type=jnp.float32).astype(jnp.bfloat16)
    width = partial.shape[1]
    extra = jnp.zeros((partial.shape[0], 128), jnp.bfloat16)
    extra = extra.at[:, 0].set(sq_hi).at[:, 1].set(sq_lo)
    n_y = lax.axis_size("by")
    packed = jnp.concatenate([partial, extra], 1).reshape(n_y, n_blk // n_y, local_rows, width + 128)
    half_sum = jnp.sum(exchange4(packed, "by", False, 2).astype(jnp.float32), axis=0)
    sq_mid = half_sum[:, :, width] + half_sum[:, :, width + 1]
    sq_mid_hi = sq_mid.astype(jnp.bfloat16)
    sq_mid_lo = (sq_mid - sq_mid_hi.astype(jnp.float32)).astype(jnp.bfloat16)
    half_packed = (
        half_sum.astype(jnp.bfloat16).at[:, :, width].set(sq_mid_hi).at[:, :, width + 1].set(sq_mid_lo)
    )
    summed = jnp.sum(exchange(half_packed, "bz", False, 3).astype(jnp.float32), axis=0)
    inner_all = inner_here * n_blk
    mean_sq = (summed[:, width] + summed[:, width + 1]) / inner_all
    mixed = (summed[:, :width] * lax.rsqrt(mean_sq + 1e-05)[:, None]).astype(jnp.bfloat16)
    return (mixed[None], new_pool)


def solution(mesh):
    placed = (
        P("rep", "blk", None),
        P(None, "blk"),
        P(None, "blk"),
        P(),
        P(None, "blk"),
        P(None, "blk"),
        P(),
        P(None, "blk"),
        P("blk"),
        P("blk"),
        P("blk"),
        P("blk", None),
        P("rep", None, "blk"),
        P("rep", None, None),
        P("rep", "blk", None, None),
        P(),
        P("rep", None),
        P("rep"),
        P("rep"),
    )
    n_blk, n_rep = mesh.shape["blk"], mesh.shape["rep"]
    split_mesh = jax.sharding.Mesh(
        mesh.devices.reshape(Y_CHIPS, n_blk // Y_CHIPS, n_rep), AXES
    )
    placed = tuple(P(*[BLK if part == "blk" else part for part in spec]) for spec in placed)
    return jax.shard_map(
        shards,
        mesh=split_mesh,
        in_specs=placed,
        out_specs=(P("rep", BLK, None), P("rep", BLK, None, None)),
        check_vma=False,
    )
```

```python
import functools

import jax
import jax.numpy as jnp
from jax import lax
from jax.experimental import pallas as pl
from jax.experimental.pallas import tpu as pltpu
from jax.sharding import PartitionSpec as P

MESH = pl.DeviceIdType.MESH
AXES = ("by", "bz", "rep")
BLK = ("by", "bz")
Y_CHIPS = 4


def exchange_kernel(n, axis, gather, src_ref, dst_ref, send_sem, recv_sem, local_sem):
    me = lax.axis_index(axis)
    coords = {name: lax.axis_index(name) for name in AXES}

    def device_of(peer):
        return tuple(peer if name == axis else coords[name] for name in AXES)

    barrier = pltpu.get_barrier_semaphore()
    for offset in range(1, n):
        peer = lax.rem(me + offset, n)
        pl.semaphore_signal(barrier, inc=1, device_id=device_of(peer), device_id_type=MESH)
    pl.semaphore_wait(barrier, n - 1)
    local = pltpu.make_async_copy(src_ref if gather else src_ref.at[me], dst_ref.at[me], local_sem)
    local.start()
    copies = []
    for offset in range(1, n):
        peer = lax.rem(me + offset, n)
        copy = pltpu.make_async_remote_copy(
            src_ref=src_ref if gather else src_ref.at[peer],
            dst_ref=dst_ref.at[me],
            send_sem=send_sem.at[offset],
            recv_sem=recv_sem.at[offset],
            device_id=device_of(peer),
            device_id_type=MESH,
        )
        copy.start()
        copies.append(copy)
    local.wait()
    for copy in copies:
        copy.wait()


def ring4_kernel(axis, gather, src_ref, dst_ref, stage_ref, send_sem, recv_sem, local_sem):
    me = lax.axis_index(axis)
    coords = {name: lax.axis_index(name) for name in AXES}

    def device_of(peer):
        return tuple(peer if name == axis else coords[name] for name in AXES)

    right, left = lax.rem(me + 1, 4), lax.rem(me + 3, 4)
    opposite = lax.rem(me + 2, 4)
    half = dst_ref.shape[1] // 2
    first, second = pl.ds(0, half), pl.ds(half, half)

    def remote(src, dst, index, peer):
        copy = pltpu.make_async_remote_copy(
            src_ref=src,
            dst_ref=dst,
            send_sem=send_sem.at[index],
            recv_sem=recv_sem.at[index],
            device_id=device_of(peer),
            device_id_type=MESH,
        )
        copy.start()
        return copy

    barrier = pltpu.get_barrier_semaphore()
    for peer in (left, right):
        pl.semaphore_signal(barrier, inc=1, device_id=device_of(peer), device_id_type=MESH)
    pl.semaphore_wait(barrier, 2)
    local = pltpu.make_async_copy(src_ref if gather else src_ref.at[me], dst_ref.at[me], local_sem)
    local.start()
    to_right = remote(src_ref if gather else src_ref.at[right], dst_ref.at[me], 0, right)
    to_left = remote(src_ref if gather else src_ref.at[left], dst_ref.at[me], 1, left)
    if gather:
        to_right.wait_recv()
        pass_right = remote(dst_ref.at[left, first], dst_ref.at[left, first], 2, right)
        to_left.wait_recv()
        pass_left = remote(dst_ref.at[right, second], dst_ref.at[right, second], 3, left)
        to_right.wait_send()
        to_left.wait_send()
    else:
        stage_right = remote(src_ref.at[opposite, first], stage_ref.at[0], 2, right)
        stage_left = remote(src_ref.at[opposite, second], stage_ref.at[1], 3, left)
        stage_right.wait_recv()
        pass_right = remote(stage_ref.at[0], dst_ref.at[left, first], 4, right)
        stage_left.wait_recv()
        pass_left = remote(stage_ref.at[1], dst_ref.at[right, second], 5, left)
        stage_right.wait_send()
        stage_left.wait_send()
        to_right.wait()
        to_left.wait()
    local.wait()
    pass_right.wait()
    pass_left.wait()


def exchange4(src, axis, gather, collective_id):
    block = src.shape if gather else src.shape[1:]
    out = jax.ShapeDtypeStruct((4,) + tuple(block), src.dtype)
    stage = jax.ShapeDtypeStruct((2, block[0] // 2) + tuple(block[1:]), src.dtype)
    return pl.pallas_call(
        functools.partial(ring4_kernel, axis, gather),
        out_shape=(out, stage),
        in_specs=[pl.BlockSpec(memory_space=pl.ANY)],
        out_specs=(pl.BlockSpec(memory_space=pl.ANY), pl.BlockSpec(memory_space=pl.ANY)),
        scratch_shapes=[
            pltpu.SemaphoreType.DMA((6,)),
            pltpu.SemaphoreType.DMA((6,)),
            pltpu.SemaphoreType.DMA,
        ],
        compiler_params=pltpu.CompilerParams(collective_id=collective_id, has_side_effects=True),
    )(src)[0]


def gather2d_kernel(nz, src_ref, dst_ref, send_sem, recv_sem, local_sem):
    y, z = lax.axis_index("by"), lax.axis_index("bz")
    rep = lax.axis_index("rep")
    right, left = lax.rem(y + 1, 4), lax.rem(y + 3, 4)
    half = src_ref.shape[0] // 2
    first, second = pl.ds(0, half), pl.ds(half, half)
    z_sem, r_sem, l_sem, ra_sem, lb_sem = 0, nz, 2 * nz, 3 * nz, 4 * nz

    def remote(src, dst, index, yy, zz):
        copy = pltpu.make_async_remote_copy(
            src_ref=src,
            dst_ref=dst,
            send_sem=send_sem.at[index],
            recv_sem=recv_sem.at[index],
            device_id=(yy, zz, rep),
            device_id_type=MESH,
        )
        copy.start()
        return copy

    barrier = pltpu.get_barrier_semaphore()
    for offset in range(1, nz):
        pl.semaphore_signal(
            barrier, inc=1, device_id=(y, lax.rem(z + offset, nz), rep), device_id_type=MESH
        )
    for yy in (left, right):
        pl.semaphore_signal(barrier, inc=1, device_id=(yy, z, rep), device_id_type=MESH)
    pl.semaphore_wait(barrier, nz + 1)
    local = pltpu.make_async_copy(src_ref, dst_ref.at[y, z], local_sem)
    local.start()
    sent = []
    along_z = []
    for offset in range(1, nz):
        copy = remote(src_ref, dst_ref.at[y, z], z_sem + offset, y, lax.rem(z + offset, nz))
        along_z.append(copy)
    to_right = [remote(src_ref, dst_ref.at[y, z], r_sem, right, z)]
    to_left = [remote(src_ref, dst_ref.at[y, z], l_sem, left, z)]
    for offset in range(1, nz):
        along_z[offset - 1].wait_recv()
        zs = lax.rem(z + nz - offset, nz)
        to_right.append(remote(dst_ref.at[y, zs], dst_ref.at[y, zs], r_sem + offset, right, z))
        to_left.append(remote(dst_ref.at[y, zs], dst_ref.at[y, zs], l_sem + offset, left, z))
    relays = []
    for offset in range(nz):
        zs = lax.rem(z + nz - offset, nz)
        to_right[offset].wait_recv()
        relays.append(
            remote(dst_ref.at[left, zs, first], dst_ref.at[left, zs, first], ra_sem + offset, right, z)
        )
        to_left[offset].wait_recv()
        relays.append(
            remote(dst_ref.at[right, zs, second], dst_ref.at[right, zs, second], lb_sem + offset, left, z)
        )
    local.wait()
    for copy in along_z + to_right + to_left:
        copy.wait_send()
    for copy in relays:
        copy.wait()


def gather2d(src, collective_id):
    nz = lax.axis_size("bz")
    return pl.pallas_call(
        functools.partial(gather2d_kernel, nz),
        out_shape=jax.ShapeDtypeStruct((4, nz) + tuple(src.shape), src.dtype),
        in_specs=[pl.BlockSpec(memory_space=pl.ANY)],
        out_specs=pl.BlockSpec(memory_space=pl.ANY),
        scratch_shapes=[
            pltpu.SemaphoreType.DMA((5 * nz,)),
            pltpu.SemaphoreType.DMA((5 * nz,)),
            pltpu.SemaphoreType.DMA,
        ],
        compiler_params=pltpu.CompilerParams(collective_id=collective_id, has_side_effects=True),
    )(src)


def exchange(src, axis, gather, collective_id):
    n = lax.axis_size(axis)
    block = src.shape if gather else src.shape[1:]
    return pl.pallas_call(
        functools.partial(exchange_kernel, n, axis, gather),
        out_shape=jax.ShapeDtypeStruct((n,) + tuple(block), src.dtype),
        in_specs=[pl.BlockSpec(memory_space=pl.ANY)],
        out_specs=pl.BlockSpec(memory_space=pl.ANY),
        scratch_shapes=[
            pltpu.SemaphoreType.DMA((n,)),
            pltpu.SemaphoreType.DMA((n,)),
            pltpu.SemaphoreType.DMA,
        ],
        compiler_params=pltpu.CompilerParams(collective_id=collective_id, has_side_effects=True),
    )(src)


def convolve(edge_cells, fresh_cells, kernel, edge_mask):
    sequence = jnp.concatenate(
        [edge_cells * edge_mask[:, :, None].astype(edge_cells.dtype), fresh_cells], 1
    ).astype(jnp.float32)
    steps_count = fresh_cells.shape[1]
    summed = kernel[0] * sequence[:, 0:steps_count]
    for offset in range(1, kernel.shape[0]):
        summed = summed + kernel[offset] * sequence[:, offset : offset + steps_count]
    return jax.nn.silu(summed).astype(jnp.bfloat16)


def shards(
    hidden_in,
    w_z,
    w_x,
    w_bc,
    w_dt,
    conv_x,
    conv_bc,
    dt_bias,
    a_log,
    d_skip,
    norm_gain,
    w_out,
    edge_x,
    edge_bc,
    pool,
    tenant_sizes,
    owner,
    accepted,
    prompt_len,
):
    highest = lax.Precision.HIGHEST
    rows_in = hidden_in[0]
    local_rows = rows_in.shape[0]
    n_req = edge_x.shape[0]
    drafts = local_rows * lax.axis_size(BLK) // n_req
    state_dim = w_bc.shape[1] // 2
    heads_here = w_dt.shape[1]
    inner_here = w_z.shape[1]
    head_dim = inner_here // heads_here
    slots_here = pool.shape[0]
    cap_group = slots_here // lax.axis_size("rep")
    weights_in = (w_z, w_x, w_dt, w_bc)
    n_blk = lax.axis_size(BLK)
    block_rows = gather2d(rows_in, 0).reshape(n_blk * local_rows, rows_in.shape[1])
    projected = jnp.concatenate(
        [
            jnp.dot(block_rows, weight_cols, preferred_element_type=jnp.float32)
            for weight_cols in weights_in
        ],
        1,
    ).astype(jnp.bfloat16)
    z_all = projected[:, :inner_here]
    u_all = projected[:, inner_here : 2 * inner_here]
    dt_raw = projected[:, 2 * inner_here : 2 * inner_here + heads_here]
    bc_all = projected[:, 2 * inner_here + heads_here :]
    edge_len = edge_x.shape[1]
    edge_mask = prompt_len[:, None] >= (edge_len - jnp.arange(edge_len, dtype=jnp.int32))[None, :]
    x_conv = convolve(edge_x, u_all.reshape(n_req, drafts, inner_here), conv_x, edge_mask)
    bc_conv = convolve(edge_bc, bc_all.reshape(n_req, drafts, 2 * state_dim), conv_bc, edge_mask)
    b_half = bc_conv[:, :, :state_dim]
    c_half = bc_conv[:, :, state_dim:]
    b_float = b_half.astype(jnp.float32)
    c_float = c_half.astype(jnp.float32)
    x_heads = x_conv.reshape(n_req, drafts, heads_here, head_dim).astype(jnp.float32)
    req_index = lax.axis_index("rep") * n_req + jnp.arange(n_req, dtype=jnp.int32)
    tenant_ends = jnp.cumsum(tenant_sizes)
    tenant_id = jnp.sum((req_index[:, None] >= tenant_ends[None, :-1]).astype(jnp.int32), axis=1)
    tenant_pick = (
        tenant_id[:, None] == jnp.arange(tenant_sizes.shape[0], dtype=jnp.int32)[None, :]
    ).astype(jnp.float32)
    bias_req = jnp.dot(tenant_pick, dt_bias, precision=highest)
    step_size = jax.nn.softplus(
        dt_raw.reshape(n_req, drafts, heads_here).astype(jnp.float32) + bias_req[:, None, :]
    )
    log_decay = jnp.cumsum(step_size * (-jnp.exp(a_log))[None, None, :], axis=1)
    draft_index = jnp.arange(drafts, dtype=jnp.int32)
    causal = draft_index[:, None] >= draft_index[None, :]
    scores = jnp.einsum("rtn,rsn->rts", c_float, b_float, precision=highest)
    log_gap = log_decay[:, :, None, :] - log_decay[:, None, :, :]
    weight = (
        jnp.where(causal[None, :, :, None], jnp.exp(jnp.minimum(log_gap, 0.0)), 0.0)
        * step_size[:, None, :, :]
        * scores[:, :, :, None]
    )
    y_local = (
        jnp.einsum("rtsh,rshp->rthp", weight, x_heads, precision=highest)
        + d_skip[None, None, :, None] * x_heads
    )
    pick_last = (draft_index[None, :] == accepted[:, None] - 1).astype(jnp.float32)
    log_accept = jnp.sum(pick_last[:, :, None] * log_decay, axis=1)
    keep_draft = draft_index[None, :] < accepted[:, None]
    coef = (
        jnp.where(
            keep_draft[:, :, None],
            jnp.exp(jnp.minimum(log_accept[:, None, :] - log_decay, 0.0)),
            0.0,
        )
        * step_size
    )
    carry_decay = jnp.exp(log_accept)
    decay_now = jnp.exp(log_decay)
    owner_of = owner[:, 0]
    local_index = jnp.arange(n_req, dtype=jnp.int32)
    earlier = (owner_of[None, :] == owner_of[:, None]) & (
        local_index[None, :] < local_index[:, None]
    )
    rank_within = jnp.sum(earlier.astype(jnp.int32), axis=1)
    slot_index = owner_of * cap_group + rank_within
    fetched = lax.all_to_all(
        pool.astype(jnp.bfloat16), "rep", split_axis=0, concat_axis=0, tiled=True
    ).astype(pool.dtype)
    slots = jnp.arange(slots_here, dtype=jnp.int32)
    slot_pick = (slots[:, None] == slot_index[None, :]).astype(jnp.int32)
    slot_used = jnp.sum(slot_pick, axis=1) > 0
    slot_req = jnp.sum(slot_pick * local_index[None, :], axis=1)

    def to_slots(per_req):
        taken = jnp.take(per_req, slot_req, axis=0)
        return jnp.where(slot_used.reshape((-1,) + (1,) * (per_req.ndim - 1)), taken, 0.0)

    prior_slot = to_slots(decay_now)[:, :, :, None] * jnp.einsum(
        "jhpn,jtn->jthp", fetched, to_slots(c_float), precision=highest
    )
    y_prior = jnp.take(prior_slot, slot_index, axis=0)
    buffer = to_slots(carry_decay)[:, :, None, None] * fetched + jnp.einsum(
        "jsh,jshp,jsn->jhpn", to_slots(coef), to_slots(x_heads), to_slots(b_float), precision=highest
    )
    new_pool = lax.all_to_all(
        buffer.astype(jnp.bfloat16), "rep", split_axis=0, concat_axis=0, tiled=True
    ).astype(buffer.dtype)
    y_total = (y_local + y_prior).reshape(n_req * drafts, inner_here)
    gated = y_total * jax.nn.silu(z_all.astype(jnp.float32))
    sq_part = jnp.sum(gated * gated, axis=1)
    sq_hi = sq_part.astype(jnp.bfloat16)
    sq_lo = (sq_part - sq_hi.astype(jnp.float32)).astype(jnp.bfloat16)
    scaled = (gated * norm_gain[None, :]).astype(jnp.bfloat16)
    partial = jnp.dot(scaled, w_out, preferred_element_type=jnp.float32).astype(jnp.bfloat16)
    width = partial.shape[1]
    extra = jnp.zeros((partial.shape[0], 128), jnp.bfloat16)
    extra = extra.at[:, 0].set(sq_hi).at[:, 1].set(sq_lo)
    n_y = lax.axis_size("by")
    packed = jnp.concatenate([partial, extra], 1).reshape(n_y, n_blk // n_y, local_rows, width + 128)
    half_sum = jnp.sum(exchange4(packed, "by", False, 2).astype(jnp.float32), axis=0)
    sq_mid = half_sum[:, :, width] + half_sum[:, :, width + 1]
    sq_mid_hi = sq_mid.astype(jnp.bfloat16)
    sq_mid_lo = (sq_mid - sq_mid_hi.astype(jnp.float32)).astype(jnp.bfloat16)
    half_packed = (
        half_sum.astype(jnp.bfloat16).at[:, :, width].set(sq_mid_hi).at[:, :, width + 1].set(sq_mid_lo)
    )
    summed = jnp.sum(exchange(half_packed, "bz", False, 3).astype(jnp.float32), axis=0)
    inner_all = inner_here * n_blk
    mean_sq = (summed[:, width] + summed[:, width + 1]) / inner_all
    mixed = (summed[:, :width] * lax.rsqrt(mean_sq + 1e-05)[:, None]).astype(jnp.bfloat16)
    return (mixed[None], new_pool)


def solution(mesh):
    placed = (
        P("rep", "blk", None),
        P(None, "blk"),
        P(None, "blk"),
        P(),
        P(None, "blk"),
        P(None, "blk"),
        P(),
        P(None, "blk"),
        P("blk"),
        P("blk"),
        P("blk"),
        P("blk", None),
        P("rep", None, "blk"),
        P("rep", None, None),
        P("rep", "blk", None, None),
        P(),
        P("rep", None),
        P("rep"),
        P("rep"),
    )
    n_blk, n_rep = mesh.shape["blk"], mesh.shape["rep"]
    split_mesh = jax.sharding.Mesh(
        mesh.devices.reshape(Y_CHIPS, n_blk // Y_CHIPS, n_rep), AXES
    )
    placed = tuple(P(*[BLK if part == "blk" else part for part in spec]) for spec in placed)
    return jax.shard_map(
        shards,
        mesh=split_mesh,
        in_specs=placed,
        out_specs=(P("rep", BLK, None), P("rep", BLK, None, None)),
        check_vma=False,
    )
```

```python
import functools

import jax
import jax.numpy as jnp
from jax import lax
from jax.experimental import pallas as pl
from jax.experimental.pallas import tpu as pltpu
from jax.sharding import PartitionSpec as P

MESH = pl.DeviceIdType.MESH
AXES = ("by", "bz", "rep")
BLK = ("by", "bz")
Y_CHIPS = 4


def exchange_kernel(n, axis, gather, src_ref, dst_ref, send_sem, recv_sem, local_sem):
    me = lax.axis_index(axis)
    coords = {name: lax.axis_index(name) for name in AXES}

    def device_of(peer):
        return tuple(peer if name == axis else coords[name] for name in AXES)

    barrier = pltpu.get_barrier_semaphore()
    for offset in range(1, n):
        peer = lax.rem(me + offset, n)
        pl.semaphore_signal(barrier, inc=1, device_id=device_of(peer), device_id_type=MESH)
    pl.semaphore_wait(barrier, n - 1)
    local = pltpu.make_async_copy(src_ref if gather else src_ref.at[me], dst_ref.at[me], local_sem)
    local.start()
    copies = []
    for offset in range(1, n):
        peer = lax.rem(me + offset, n)
        copy = pltpu.make_async_remote_copy(
            src_ref=src_ref if gather else src_ref.at[peer],
            dst_ref=dst_ref.at[me],
            send_sem=send_sem.at[offset],
            recv_sem=recv_sem.at[offset],
            device_id=device_of(peer),
            device_id_type=MESH,
        )
        copy.start()
        copies.append(copy)
    local.wait()
    for copy in copies:
        copy.wait()


def ring4_kernel(axis, gather, src_ref, dst_ref, stage_ref, send_sem, recv_sem, local_sem):
    me = lax.axis_index(axis)
    coords = {name: lax.axis_index(name) for name in AXES}

    def device_of(peer):
        return tuple(peer if name == axis else coords[name] for name in AXES)

    right, left = lax.rem(me + 1, 4), lax.rem(me + 3, 4)
    opposite = lax.rem(me + 2, 4)
    half = dst_ref.shape[1] // 2
    first, second = pl.ds(0, half), pl.ds(half, half)

    def remote(src, dst, index, peer):
        copy = pltpu.make_async_remote_copy(
            src_ref=src,
            dst_ref=dst,
            send_sem=send_sem.at[index],
            recv_sem=recv_sem.at[index],
            device_id=device_of(peer),
            device_id_type=MESH,
        )
        copy.start()
        return copy

    barrier = pltpu.get_barrier_semaphore()
    for peer in (left, right):
        pl.semaphore_signal(barrier, inc=1, device_id=device_of(peer), device_id_type=MESH)
    pl.semaphore_wait(barrier, 2)
    local = pltpu.make_async_copy(src_ref if gather else src_ref.at[me], dst_ref.at[me], local_sem)
    local.start()
    to_right = remote(src_ref if gather else src_ref.at[right], dst_ref.at[me], 0, right)
    to_left = remote(src_ref if gather else src_ref.at[left], dst_ref.at[me], 1, left)
    if gather:
        to_right.wait_recv()
        pass_right = remote(dst_ref.at[left, first], dst_ref.at[left, first], 2, right)
        to_left.wait_recv()
        pass_left = remote(dst_ref.at[right, second], dst_ref.at[right, second], 3, left)
        to_right.wait_send()
        to_left.wait_send()
    else:
        stage_right = remote(src_ref.at[opposite, first], stage_ref.at[0], 2, right)
        stage_left = remote(src_ref.at[opposite, second], stage_ref.at[1], 3, left)
        stage_right.wait_recv()
        pass_right = remote(stage_ref.at[0], dst_ref.at[left, first], 4, right)
        stage_left.wait_recv()
        pass_left = remote(stage_ref.at[1], dst_ref.at[right, second], 5, left)
        stage_right.wait_send()
        stage_left.wait_send()
        to_right.wait()
        to_left.wait()
    local.wait()
    pass_right.wait()
    pass_left.wait()


def exchange4(src, axis, gather, collective_id):
    block = src.shape if gather else src.shape[1:]
    out = jax.ShapeDtypeStruct((4,) + tuple(block), src.dtype)
    stage = jax.ShapeDtypeStruct((2, block[0] // 2) + tuple(block[1:]), src.dtype)
    return pl.pallas_call(
        functools.partial(ring4_kernel, axis, gather),
        out_shape=(out, stage),
        in_specs=[pl.BlockSpec(memory_space=pl.ANY)],
        out_specs=(pl.BlockSpec(memory_space=pl.ANY), pl.BlockSpec(memory_space=pl.ANY)),
        scratch_shapes=[
            pltpu.SemaphoreType.DMA((6,)),
            pltpu.SemaphoreType.DMA((6,)),
            pltpu.SemaphoreType.DMA,
        ],
        compiler_params=pltpu.CompilerParams(collective_id=collective_id, has_side_effects=True),
    )(src)[0]


def gather2d_kernel(nz, src_ref, dst_ref, send_sem, recv_sem, local_sem):
    y, z = lax.axis_index("by"), lax.axis_index("bz")
    rep = lax.axis_index("rep")
    right, left = lax.rem(y + 1, 4), lax.rem(y + 3, 4)
    half = src_ref.shape[0] // 2
    first, second = pl.ds(0, half), pl.ds(half, half)
    z_sem, r_sem, l_sem, ra_sem, lb_sem = 0, nz, 2 * nz, 3 * nz, 4 * nz

    def remote(src, dst, index, yy, zz):
        copy = pltpu.make_async_remote_copy(
            src_ref=src,
            dst_ref=dst,
            send_sem=send_sem.at[index],
            recv_sem=recv_sem.at[index],
            device_id=(yy, zz, rep),
            device_id_type=MESH,
        )
        copy.start()
        return copy

    barrier = pltpu.get_barrier_semaphore()
    for offset in range(1, nz):
        pl.semaphore_signal(
            barrier, inc=1, device_id=(y, lax.rem(z + offset, nz), rep), device_id_type=MESH
        )
    for yy in (left, right):
        pl.semaphore_signal(barrier, inc=1, device_id=(yy, z, rep), device_id_type=MESH)
    pl.semaphore_wait(barrier, nz + 1)
    local = pltpu.make_async_copy(src_ref, dst_ref.at[y, z], local_sem)
    local.start()
    sent = []
    along_z = []
    for offset in range(1, nz):
        copy = remote(src_ref, dst_ref.at[y, z], z_sem + offset, y, lax.rem(z + offset, nz))
        along_z.append(copy)
    to_right = [remote(src_ref, dst_ref.at[y, z], r_sem, right, z)]
    to_left = [remote(src_ref, dst_ref.at[y, z], l_sem, left, z)]
    for offset in range(1, nz):
        along_z[offset - 1].wait_recv()
        zs = lax.rem(z + nz - offset, nz)
        to_right.append(remote(dst_ref.at[y, zs], dst_ref.at[y, zs], r_sem + offset, right, z))
        to_left.append(remote(dst_ref.at[y, zs], dst_ref.at[y, zs], l_sem + offset, left, z))
    relays = []
    for offset in range(nz):
        zs = lax.rem(z + nz - offset, nz)
        to_right[offset].wait_recv()
        relays.append(
            remote(dst_ref.at[left, zs, first], dst_ref.at[left, zs, first], ra_sem + offset, right, z)
        )
        to_left[offset].wait_recv()
        relays.append(
            remote(dst_ref.at[right, zs, second], dst_ref.at[right, zs, second], lb_sem + offset, left, z)
        )
    local.wait()
    for copy in along_z + to_right + to_left:
        copy.wait_send()
    for copy in relays:
        copy.wait()


def gather2d(src, collective_id):
    nz = lax.axis_size("bz")
    return pl.pallas_call(
        functools.partial(gather2d_kernel, nz),
        out_shape=jax.ShapeDtypeStruct((4, nz) + tuple(src.shape), src.dtype),
        in_specs=[pl.BlockSpec(memory_space=pl.ANY)],
        out_specs=pl.BlockSpec(memory_space=pl.ANY),
        scratch_shapes=[
            pltpu.SemaphoreType.DMA((5 * nz,)),
            pltpu.SemaphoreType.DMA((5 * nz,)),
            pltpu.SemaphoreType.DMA,
        ],
        compiler_params=pltpu.CompilerParams(collective_id=collective_id, has_side_effects=True),
    )(src)


def exchange(src, axis, gather, collective_id):
    n = lax.axis_size(axis)
    block = src.shape if gather else src.shape[1:]
    return pl.pallas_call(
        functools.partial(exchange_kernel, n, axis, gather),
        out_shape=jax.ShapeDtypeStruct((n,) + tuple(block), src.dtype),
        in_specs=[pl.BlockSpec(memory_space=pl.ANY)],
        out_specs=pl.BlockSpec(memory_space=pl.ANY),
        scratch_shapes=[
            pltpu.SemaphoreType.DMA((n,)),
            pltpu.SemaphoreType.DMA((n,)),
            pltpu.SemaphoreType.DMA,
        ],
        compiler_params=pltpu.CompilerParams(collective_id=collective_id, has_side_effects=True),
    )(src)


def convolve(edge_cells, fresh_cells, kernel, edge_mask):
    sequence = jnp.concatenate(
        [edge_cells * edge_mask[:, :, None].astype(edge_cells.dtype), fresh_cells], 1
    ).astype(jnp.float32)
    steps_count = fresh_cells.shape[1]
    summed = kernel[0] * sequence[:, 0:steps_count]
    for offset in range(1, kernel.shape[0]):
        summed = summed + kernel[offset] * sequence[:, offset : offset + steps_count]
    return jax.nn.silu(summed).astype(jnp.bfloat16)


def split_dot(spec, wide, narrow):
    high = wide.astype(jnp.bfloat16)
    low = (wide - high.astype(jnp.float32)).astype(jnp.bfloat16)
    return jnp.einsum(spec, high, narrow, preferred_element_type=jnp.float32) + jnp.einsum(
        spec, low, narrow, preferred_element_type=jnp.float32
    )


def shards(
    hidden_in,
    w_z,
    w_x,
    w_bc,
    w_dt,
    conv_x,
    conv_bc,
    dt_bias,
    a_log,
    d_skip,
    norm_gain,
    w_out,
    edge_x,
    edge_bc,
    pool,
    tenant_sizes,
    owner,
    accepted,
    prompt_len,
):
    highest = lax.Precision.HIGHEST
    rows_in = hidden_in[0]
    local_rows = rows_in.shape[0]
    n_req = edge_x.shape[0]
    drafts = local_rows * lax.axis_size(BLK) // n_req
    state_dim = w_bc.shape[1] // 2
    heads_here = w_dt.shape[1]
    inner_here = w_z.shape[1]
    head_dim = inner_here // heads_here
    slots_here = pool.shape[0]
    cap_group = slots_here // lax.axis_size("rep")
    weights_in = (w_z, w_x, w_dt, w_bc)
    n_blk = lax.axis_size(BLK)
    block_rows = gather2d(rows_in, 0).reshape(n_blk * local_rows, rows_in.shape[1])
    projected = jnp.concatenate(
        [
            jnp.dot(block_rows, weight_cols, preferred_element_type=jnp.float32)
            for weight_cols in weights_in
        ],
        1,
    ).astype(jnp.bfloat16)
    z_all = projected[:, :inner_here]
    u_all = projected[:, inner_here : 2 * inner_here]
    dt_raw = projected[:, 2 * inner_here : 2 * inner_here + heads_here]
    bc_all = projected[:, 2 * inner_here + heads_here :]
    edge_len = edge_x.shape[1]
    edge_mask = prompt_len[:, None] >= (edge_len - jnp.arange(edge_len, dtype=jnp.int32))[None, :]
    x_conv = convolve(edge_x, u_all.reshape(n_req, drafts, inner_here), conv_x, edge_mask)
    bc_conv = convolve(edge_bc, bc_all.reshape(n_req, drafts, 2 * state_dim), conv_bc, edge_mask)
    b_half = bc_conv[:, :, :state_dim]
    c_half = bc_conv[:, :, state_dim:]
    b_float = b_half.astype(jnp.float32)
    c_float = c_half.astype(jnp.float32)
    x_heads = x_conv.reshape(n_req, drafts, heads_here, head_dim).astype(jnp.float32)
    req_index = lax.axis_index("rep") * n_req + jnp.arange(n_req, dtype=jnp.int32)
    tenant_ends = jnp.cumsum(tenant_sizes)
    tenant_id = jnp.sum((req_index[:, None] >= tenant_ends[None, :-1]).astype(jnp.int32), axis=1)
    tenant_pick = (
        tenant_id[:, None] == jnp.arange(tenant_sizes.shape[0], dtype=jnp.int32)[None, :]
    ).astype(jnp.float32)
    bias_req = jnp.dot(tenant_pick, dt_bias, precision=highest)
    step_size = jax.nn.softplus(
        dt_raw.reshape(n_req, drafts, heads_here).astype(jnp.float32) + bias_req[:, None, :]
    )
    log_decay = jnp.cumsum(step_size * (-jnp.exp(a_log))[None, None, :], axis=1)
    draft_index = jnp.arange(drafts, dtype=jnp.int32)
    causal = draft_index[:, None] >= draft_index[None, :]
    scores = jnp.einsum("rtn,rsn->rts", c_half, b_half, preferred_element_type=jnp.float32)
    log_gap = log_decay[:, :, None, :] - log_decay[:, None, :, :]
    weight = (
        jnp.where(causal[None, :, :, None], jnp.exp(jnp.minimum(log_gap, 0.0)), 0.0)
        * step_size[:, None, :, :]
        * scores[:, :, :, None]
    )
    y_local = (
        split_dot("rtsh,rshp->rthp", weight, x_conv.reshape(n_req, drafts, heads_here, head_dim))
        + d_skip[None, None, :, None] * x_heads
    )
    pick_last = (draft_index[None, :] == accepted[:, None] - 1).astype(jnp.float32)
    log_accept = jnp.sum(pick_last[:, :, None] * log_decay, axis=1)
    keep_draft = draft_index[None, :] < accepted[:, None]
    coef = (
        jnp.where(
            keep_draft[:, :, None],
            jnp.exp(jnp.minimum(log_accept[:, None, :] - log_decay, 0.0)),
            0.0,
        )
        * step_size
    )
    carry_decay = jnp.exp(log_accept)
    decay_now = jnp.exp(log_decay)
    owner_of = owner[:, 0]
    local_index = jnp.arange(n_req, dtype=jnp.int32)
    earlier = (owner_of[None, :] == owner_of[:, None]) & (
        local_index[None, :] < local_index[:, None]
    )
    rank_within = jnp.sum(earlier.astype(jnp.int32), axis=1)
    slot_index = owner_of * cap_group + rank_within
    fetched_half = lax.all_to_all(
        pool.astype(jnp.bfloat16), "rep", split_axis=0, concat_axis=0, tiled=True
    )
    fetched = fetched_half.astype(pool.dtype)
    slots = jnp.arange(slots_here, dtype=jnp.int32)
    slot_pick = (slots[:, None] == slot_index[None, :]).astype(jnp.int32)
    slot_used = jnp.sum(slot_pick, axis=1) > 0
    slot_req = jnp.sum(slot_pick * local_index[None, :], axis=1)

    def to_slots(per_req):
        taken = jnp.take(per_req, slot_req, axis=0)
        return jnp.where(slot_used.reshape((-1,) + (1,) * (per_req.ndim - 1)), taken, 0.0)

    prior_slot = to_slots(decay_now)[:, :, :, None] * jnp.einsum(
        "jhpn,jtn->jthp", fetched_half, to_slots(c_half), preferred_element_type=jnp.float32
    )
    y_prior = jnp.take(prior_slot, slot_index, axis=0)
    buffer = to_slots(carry_decay)[:, :, None, None] * fetched + split_dot(
        "jshp,jsn->jhpn", to_slots(coef[:, :, :, None] * x_heads), to_slots(b_half)
    )
    new_pool = lax.all_to_all(
        buffer.astype(jnp.bfloat16), "rep", split_axis=0, concat_axis=0, tiled=True
    ).astype(buffer.dtype)
    y_total = (y_local + y_prior).reshape(n_req * drafts, inner_here)
    gated = y_total * jax.nn.silu(z_all.astype(jnp.float32))
    sq_part = jnp.sum(gated * gated, axis=1)
    sq_hi = sq_part.astype(jnp.bfloat16)
    sq_lo = (sq_part - sq_hi.astype(jnp.float32)).astype(jnp.bfloat16)
    scaled = (gated * norm_gain[None, :]).astype(jnp.bfloat16)
    partial = jnp.dot(scaled, w_out, preferred_element_type=jnp.float32).astype(jnp.bfloat16)
    width = partial.shape[1]
    extra = jnp.zeros((partial.shape[0], 128), jnp.bfloat16)
    extra = extra.at[:, 0].set(sq_hi).at[:, 1].set(sq_lo)
    n_y = lax.axis_size("by")
    packed = jnp.concatenate([partial, extra], 1).reshape(n_y, n_blk // n_y, local_rows, width + 128)
    half_sum = jnp.sum(exchange4(packed, "by", False, 2).astype(jnp.float32), axis=0)
    sq_mid = half_sum[:, :, width] + half_sum[:, :, width + 1]
    sq_mid_hi = sq_mid.astype(jnp.bfloat16)
    sq_mid_lo = (sq_mid - sq_mid_hi.astype(jnp.float32)).astype(jnp.bfloat16)
    half_packed = (
        half_sum.astype(jnp.bfloat16).at[:, :, width].set(sq_mid_hi).at[:, :, width + 1].set(sq_mid_lo)
    )
    summed = jnp.sum(exchange(half_packed, "bz", False, 3).astype(jnp.float32), axis=0)
    inner_all = inner_here * n_blk
    mean_sq = (summed[:, width] + summed[:, width + 1]) / inner_all
    mixed = (summed[:, :width] * lax.rsqrt(mean_sq + 1e-05)[:, None]).astype(jnp.bfloat16)
    return (mixed[None], new_pool)


def solution(mesh):
    placed = (
        P("rep", "blk", None),
        P(None, "blk"),
        P(None, "blk"),
        P(),
        P(None, "blk"),
        P(None, "blk"),
        P(),
        P(None, "blk"),
        P("blk"),
        P("blk"),
        P("blk"),
        P("blk", None),
        P("rep", None, "blk"),
        P("rep", None, None),
        P("rep", "blk", None, None),
        P(),
        P("rep", None),
        P("rep"),
        P("rep"),
    )
    n_blk, n_rep = mesh.shape["blk"], mesh.shape["rep"]
    split_mesh = jax.sharding.Mesh(
        mesh.devices.reshape(Y_CHIPS, n_blk // Y_CHIPS, n_rep), AXES
    )
    placed = tuple(P(*[BLK if part == "blk" else part for part in spec]) for spec in placed)
    return jax.shard_map(
        shards,
        mesh=split_mesh,
        in_specs=placed,
        out_specs=(P("rep", BLK, None), P("rep", BLK, None, None)),
        check_vma=False,
    )
```

```python
import functools

import jax
import jax.numpy as jnp
from jax import lax
from jax.experimental import pallas as pl
from jax.experimental.pallas import tpu as pltpu
from jax.sharding import PartitionSpec as P

MESH = pl.DeviceIdType.MESH
AXES = ("by", "bz", "rep")
BLK = ("by", "bz")
Y_CHIPS = 4


def exchange_kernel(n, axis, gather, src_ref, dst_ref, send_sem, recv_sem, local_sem):
    me = lax.axis_index(axis)
    coords = {name: lax.axis_index(name) for name in AXES}

    def device_of(peer):
        return tuple(peer if name == axis else coords[name] for name in AXES)

    barrier = pltpu.get_barrier_semaphore()
    for offset in range(1, n):
        peer = lax.rem(me + offset, n)
        pl.semaphore_signal(barrier, inc=1, device_id=device_of(peer), device_id_type=MESH)
    pl.semaphore_wait(barrier, n - 1)
    local = pltpu.make_async_copy(src_ref if gather else src_ref.at[me], dst_ref.at[me], local_sem)
    local.start()
    copies = []
    for offset in range(1, n):
        peer = lax.rem(me + offset, n)
        copy = pltpu.make_async_remote_copy(
            src_ref=src_ref if gather else src_ref.at[peer],
            dst_ref=dst_ref.at[me],
            send_sem=send_sem.at[offset],
            recv_sem=recv_sem.at[offset],
            device_id=device_of(peer),
            device_id_type=MESH,
        )
        copy.start()
        copies.append(copy)
    local.wait()
    for copy in copies:
        copy.wait()


def ring4_kernel(axis, gather, src_ref, dst_ref, stage_ref, send_sem, recv_sem, local_sem):
    me = lax.axis_index(axis)
    coords = {name: lax.axis_index(name) for name in AXES}

    def device_of(peer):
        return tuple(peer if name == axis else coords[name] for name in AXES)

    right, left = lax.rem(me + 1, 4), lax.rem(me + 3, 4)
    opposite = lax.rem(me + 2, 4)
    half = dst_ref.shape[1] // 2
    first, second = pl.ds(0, half), pl.ds(half, half)

    def remote(src, dst, index, peer):
        copy = pltpu.make_async_remote_copy(
            src_ref=src,
            dst_ref=dst,
            send_sem=send_sem.at[index],
            recv_sem=recv_sem.at[index],
            device_id=device_of(peer),
            device_id_type=MESH,
        )
        copy.start()
        return copy

    barrier = pltpu.get_barrier_semaphore()
    for peer in (left, right):
        pl.semaphore_signal(barrier, inc=1, device_id=device_of(peer), device_id_type=MESH)
    pl.semaphore_wait(barrier, 2)
    local = pltpu.make_async_copy(src_ref if gather else src_ref.at[me], dst_ref.at[me], local_sem)
    local.start()
    to_right = remote(src_ref if gather else src_ref.at[right], dst_ref.at[me], 0, right)
    to_left = remote(src_ref if gather else src_ref.at[left], dst_ref.at[me], 1, left)
    if gather:
        to_right.wait_recv()
        pass_right = remote(dst_ref.at[left, first], dst_ref.at[left, first], 2, right)
        to_left.wait_recv()
        pass_left = remote(dst_ref.at[right, second], dst_ref.at[right, second], 3, left)
        to_right.wait_send()
        to_left.wait_send()
    else:
        stage_right = remote(src_ref.at[opposite, first], stage_ref.at[0], 2, right)
        stage_left = remote(src_ref.at[opposite, second], stage_ref.at[1], 3, left)
        stage_right.wait_recv()
        pass_right = remote(stage_ref.at[0], dst_ref.at[left, first], 4, right)
        stage_left.wait_recv()
        pass_left = remote(stage_ref.at[1], dst_ref.at[right, second], 5, left)
        stage_right.wait_send()
        stage_left.wait_send()
        to_right.wait()
        to_left.wait()
    local.wait()
    pass_right.wait()
    pass_left.wait()


def exchange4(src, axis, gather, collective_id):
    block = src.shape if gather else src.shape[1:]
    out = jax.ShapeDtypeStruct((4,) + tuple(block), src.dtype)
    stage = jax.ShapeDtypeStruct((2, block[0] // 2) + tuple(block[1:]), src.dtype)
    return pl.pallas_call(
        functools.partial(ring4_kernel, axis, gather),
        out_shape=(out, stage),
        in_specs=[pl.BlockSpec(memory_space=pl.ANY)],
        out_specs=(pl.BlockSpec(memory_space=pl.ANY), pl.BlockSpec(memory_space=pl.ANY)),
        scratch_shapes=[
            pltpu.SemaphoreType.DMA((6,)),
            pltpu.SemaphoreType.DMA((6,)),
            pltpu.SemaphoreType.DMA,
        ],
        compiler_params=pltpu.CompilerParams(collective_id=collective_id, has_side_effects=True),
    )(src)[0]


def gather2d_kernel(nz, src_ref, dst_ref, send_sem, recv_sem, local_sem):
    y, z = lax.axis_index("by"), lax.axis_index("bz")
    rep = lax.axis_index("rep")
    right, left = lax.rem(y + 1, 4), lax.rem(y + 3, 4)
    half = src_ref.shape[0] // 2
    first, second = pl.ds(0, half), pl.ds(half, half)
    z_sem, r_sem, l_sem, ra_sem, lb_sem = 0, nz, 2 * nz, 3 * nz, 4 * nz

    def remote(src, dst, index, yy, zz):
        copy = pltpu.make_async_remote_copy(
            src_ref=src,
            dst_ref=dst,
            send_sem=send_sem.at[index],
            recv_sem=recv_sem.at[index],
            device_id=(yy, zz, rep),
            device_id_type=MESH,
        )
        copy.start()
        return copy

    barrier = pltpu.get_barrier_semaphore()
    for offset in range(1, nz):
        pl.semaphore_signal(
            barrier, inc=1, device_id=(y, lax.rem(z + offset, nz), rep), device_id_type=MESH
        )
    for yy in (left, right):
        pl.semaphore_signal(barrier, inc=1, device_id=(yy, z, rep), device_id_type=MESH)
    pl.semaphore_wait(barrier, nz + 1)
    local = pltpu.make_async_copy(src_ref, dst_ref.at[y, z], local_sem)
    local.start()
    sent = []
    along_z = []
    for offset in range(1, nz):
        copy = remote(src_ref, dst_ref.at[y, z], z_sem + offset, y, lax.rem(z + offset, nz))
        along_z.append(copy)
    to_right = [remote(src_ref, dst_ref.at[y, z], r_sem, right, z)]
    to_left = [remote(src_ref, dst_ref.at[y, z], l_sem, left, z)]
    for offset in range(1, nz):
        along_z[offset - 1].wait_recv()
        zs = lax.rem(z + nz - offset, nz)
        to_right.append(remote(dst_ref.at[y, zs], dst_ref.at[y, zs], r_sem + offset, right, z))
        to_left.append(remote(dst_ref.at[y, zs], dst_ref.at[y, zs], l_sem + offset, left, z))
    relays = []
    for offset in range(nz):
        zs = lax.rem(z + nz - offset, nz)
        to_right[offset].wait_recv()
        relays.append(
            remote(dst_ref.at[left, zs, first], dst_ref.at[left, zs, first], ra_sem + offset, right, z)
        )
        to_left[offset].wait_recv()
        relays.append(
            remote(dst_ref.at[right, zs, second], dst_ref.at[right, zs, second], lb_sem + offset, left, z)
        )
    local.wait()
    for copy in along_z + to_right + to_left:
        copy.wait_send()
    for copy in relays:
        copy.wait()


def gather2d(src, collective_id):
    nz = lax.axis_size("bz")
    return pl.pallas_call(
        functools.partial(gather2d_kernel, nz),
        out_shape=jax.ShapeDtypeStruct((4, nz) + tuple(src.shape), src.dtype),
        in_specs=[pl.BlockSpec(memory_space=pl.ANY)],
        out_specs=pl.BlockSpec(memory_space=pl.ANY),
        scratch_shapes=[
            pltpu.SemaphoreType.DMA((5 * nz,)),
            pltpu.SemaphoreType.DMA((5 * nz,)),
            pltpu.SemaphoreType.DMA,
        ],
        compiler_params=pltpu.CompilerParams(collective_id=collective_id, has_side_effects=True),
    )(src)


def scatter2d_kernel(nz, width, src_ref, out_ref, mid_ref, stage_ref, sent_ref, held, ready,
                     send_sem, recv_sem, load_sem, put_sem, local_sem):
    y, z = lax.axis_index("by"), lax.axis_index("bz")
    rep = lax.axis_index("rep")
    right, left = lax.rem(y + 1, 4), lax.rem(y + 3, 4)
    opposite = lax.rem(y + 2, 4)
    half = nz // 2
    first, second = pl.ds(0, half), pl.ds(half, half)

    def remote(src, dst, index, yy, zz):
        copy = pltpu.make_async_remote_copy(
            src_ref=src,
            dst_ref=dst,
            send_sem=send_sem.at[index],
            recv_sem=recv_sem.at[index],
            device_id=(yy, zz, rep),
            device_id_type=MESH,
        )
        copy.start()
        return copy

    barrier = pltpu.get_barrier_semaphore()
    for offset in range(1, nz):
        pl.semaphore_signal(
            barrier, inc=1, device_id=(y, lax.rem(z + offset, nz), rep), device_id_type=MESH
        )
    for yy in (left, right):
        pl.semaphore_signal(barrier, inc=1, device_id=(yy, z, rep), device_id_type=MESH)
    pl.semaphore_wait(barrier, nz + 1)
    local = pltpu.make_async_copy(src_ref.at[y], mid_ref.at[y], local_sem)
    local.start()
    to_right = remote(src_ref.at[right], mid_ref.at[y], 0, right, z)
    to_left = remote(src_ref.at[left], mid_ref.at[y], 1, left, z)
    stage_right = remote(src_ref.at[opposite, first], stage_ref.at[0], 2, right, z)
    stage_left = remote(src_ref.at[opposite, second], stage_ref.at[1], 3, left, z)
    stage_right.wait_recv()
    pass_right = remote(stage_ref.at[0], mid_ref.at[left, first], 4, right, z)
    stage_left.wait_recv()
    pass_left = remote(stage_ref.at[1], mid_ref.at[right, second], 5, left, z)
    local.wait()
    to_right.wait()
    to_left.wait()
    pass_right.wait()
    pass_left.wait()
    stage_right.wait_send()
    stage_left.wait_send()
    column = lax.broadcasted_iota(jnp.int32, held.shape[1:], 1)
    along_z = []
    for offset in range(nz):
        target = lax.rem(z + offset, nz)
        load = pltpu.make_async_copy(mid_ref.at[:, target], held, load_sem)
        load.start()
        load.wait()
        total = jnp.sum(held[...].astype(jnp.float32), axis=0)
        squares = jnp.sum(
            jnp.where((column == width) | (column == width + 1), total, 0.0), axis=1, keepdims=True
        )
        high = squares.astype(jnp.bfloat16).astype(jnp.float32)
        low = squares - high
        total = jnp.where(column == width, high, jnp.where(column == width + 1, low, total))
        ready[offset] = total.astype(ready.dtype)
        put = pltpu.make_async_copy(ready.at[offset], sent_ref.at[offset], put_sem)
        put.start()
        put.wait()
        if offset == 0:
            mine = pltpu.make_async_copy(sent_ref.at[0], out_ref.at[z], local_sem)
            mine.start()
        else:
            along_z.append(remote(sent_ref.at[offset], out_ref.at[z], 6 + offset, y, target))
    mine.wait()
    for copy in along_z:
        copy.wait()


def scatter2d(src, width, collective_id):
    nz = src.shape[1]
    block = tuple(src.shape[2:])
    kind = jax.ShapeDtypeStruct
    return pl.pallas_call(
        functools.partial(scatter2d_kernel, nz, width),
        out_shape=(
            kind((nz,) + block, src.dtype),
            kind((4, nz) + block, src.dtype),
            kind((2, nz // 2) + block, src.dtype),
            kind((nz,) + block, src.dtype),
        ),
        in_specs=[pl.BlockSpec(memory_space=pl.ANY)],
        out_specs=tuple(pl.BlockSpec(memory_space=pl.ANY) for _ in range(4)),
        scratch_shapes=[
            pltpu.VMEM((4,) + block, src.dtype),
            pltpu.VMEM((nz,) + block, src.dtype),
            pltpu.SemaphoreType.DMA((6 + nz,)),
            pltpu.SemaphoreType.DMA((6 + nz,)),
            pltpu.SemaphoreType.DMA,
            pltpu.SemaphoreType.DMA,
            pltpu.SemaphoreType.DMA,
        ],
        compiler_params=pltpu.CompilerParams(collective_id=collective_id, has_side_effects=True),
    )(src)[0]


def exchange(src, axis, gather, collective_id):
    n = lax.axis_size(axis)
    block = src.shape if gather else src.shape[1:]
    return pl.pallas_call(
        functools.partial(exchange_kernel, n, axis, gather),
        out_shape=jax.ShapeDtypeStruct((n,) + tuple(block), src.dtype),
        in_specs=[pl.BlockSpec(memory_space=pl.ANY)],
        out_specs=pl.BlockSpec(memory_space=pl.ANY),
        scratch_shapes=[
            pltpu.SemaphoreType.DMA((n,)),
            pltpu.SemaphoreType.DMA((n,)),
            pltpu.SemaphoreType.DMA,
        ],
        compiler_params=pltpu.CompilerParams(collective_id=collective_id, has_side_effects=True),
    )(src)


def convolve(edge_cells, fresh_cells, kernel, edge_mask):
    sequence = jnp.concatenate(
        [edge_cells * edge_mask[:, :, None].astype(edge_cells.dtype), fresh_cells], 1
    ).astype(jnp.float32)
    steps_count = fresh_cells.shape[1]
    summed = kernel[0] * sequence[:, 0:steps_count]
    for offset in range(1, kernel.shape[0]):
        summed = summed + kernel[offset] * sequence[:, offset : offset + steps_count]
    return jax.nn.silu(summed).astype(jnp.bfloat16)


def split_dot(spec, wide, narrow):
    high = wide.astype(jnp.bfloat16)
    low = (wide - high.astype(jnp.float32)).astype(jnp.bfloat16)
    return jnp.einsum(spec, high, narrow, preferred_element_type=jnp.float32) + jnp.einsum(
        spec, low, narrow, preferred_element_type=jnp.float32
    )


def shards(
    hidden_in,
    w_z,
    w_x,
    w_bc,
    w_dt,
    conv_x,
    conv_bc,
    dt_bias,
    a_log,
    d_skip,
    norm_gain,
    w_out,
    edge_x,
    edge_bc,
    pool,
    tenant_sizes,
    owner,
    accepted,
    prompt_len,
):
    highest = lax.Precision.HIGHEST
    rows_in = hidden_in[0]
    local_rows = rows_in.shape[0]
    n_req = edge_x.shape[0]
    drafts = local_rows * lax.axis_size(BLK) // n_req
    state_dim = w_bc.shape[1] // 2
    heads_here = w_dt.shape[1]
    inner_here = w_z.shape[1]
    head_dim = inner_here // heads_here
    slots_here = pool.shape[0]
    cap_group = slots_here // lax.axis_size("rep")
    weights_in = (w_z, w_x, w_dt, w_bc)
    n_blk = lax.axis_size(BLK)
    block_rows = gather2d(rows_in, 0).reshape(n_blk * local_rows, rows_in.shape[1])
    projected = jnp.concatenate(
        [
            jnp.dot(block_rows, weight_cols, preferred_element_type=jnp.float32)
            for weight_cols in weights_in
        ],
        1,
    ).astype(jnp.bfloat16)
    z_all = projected[:, :inner_here]
    u_all = projected[:, inner_here : 2 * inner_here]
    dt_raw = projected[:, 2 * inner_here : 2 * inner_here + heads_here]
    bc_all = projected[:, 2 * inner_here + heads_here :]
    edge_len = edge_x.shape[1]
    edge_mask = prompt_len[:, None] >= (edge_len - jnp.arange(edge_len, dtype=jnp.int32))[None, :]
    x_conv = convolve(edge_x, u_all.reshape(n_req, drafts, inner_here), conv_x, edge_mask)
    bc_conv = convolve(edge_bc, bc_all.reshape(n_req, drafts, 2 * state_dim), conv_bc, edge_mask)
    b_half = bc_conv[:, :, :state_dim]
    c_half = bc_conv[:, :, state_dim:]
    b_float = b_half.astype(jnp.float32)
    c_float = c_half.astype(jnp.float32)
    x_heads = x_conv.reshape(n_req, drafts, heads_here, head_dim).astype(jnp.float32)
    req_index = lax.axis_index("rep") * n_req + jnp.arange(n_req, dtype=jnp.int32)
    tenant_ends = jnp.cumsum(tenant_sizes)
    tenant_id = jnp.sum((req_index[:, None] >= tenant_ends[None, :-1]).astype(jnp.int32), axis=1)
    tenant_pick = (
        tenant_id[:, None] == jnp.arange(tenant_sizes.shape[0], dtype=jnp.int32)[None, :]
    ).astype(jnp.float32)
    bias_req = jnp.dot(tenant_pick, dt_bias, precision=highest)
    step_size = jax.nn.softplus(
        dt_raw.reshape(n_req, drafts, heads_here).astype(jnp.float32) + bias_req[:, None, :]
    )
    log_decay = jnp.cumsum(step_size * (-jnp.exp(a_log))[None, None, :], axis=1)
    draft_index = jnp.arange(drafts, dtype=jnp.int32)
    causal = draft_index[:, None] >= draft_index[None, :]
    scores = jnp.einsum("rtn,rsn->rts", c_half, b_half, preferred_element_type=jnp.float32)
    log_gap = log_decay[:, :, None, :] - log_decay[:, None, :, :]
    weight = (
        jnp.where(causal[None, :, :, None], jnp.exp(jnp.minimum(log_gap, 0.0)), 0.0)
        * step_size[:, None, :, :]
        * scores[:, :, :, None]
    )
    y_local = (
        split_dot("rtsh,rshp->rthp", weight, x_conv.reshape(n_req, drafts, heads_here, head_dim))
        + d_skip[None, None, :, None] * x_heads
    )
    pick_last = (draft_index[None, :] == accepted[:, None] - 1).astype(jnp.float32)
    log_accept = jnp.sum(pick_last[:, :, None] * log_decay, axis=1)
    keep_draft = draft_index[None, :] < accepted[:, None]
    coef = (
        jnp.where(
            keep_draft[:, :, None],
            jnp.exp(jnp.minimum(log_accept[:, None, :] - log_decay, 0.0)),
            0.0,
        )
        * step_size
    )
    carry_decay = jnp.exp(log_accept)
    decay_now = jnp.exp(log_decay)
    owner_of = owner[:, 0]
    local_index = jnp.arange(n_req, dtype=jnp.int32)
    earlier = (owner_of[None, :] == owner_of[:, None]) & (
        local_index[None, :] < local_index[:, None]
    )
    rank_within = jnp.sum(earlier.astype(jnp.int32), axis=1)
    slot_index = owner_of * cap_group + rank_within
    fetched_half = lax.all_to_all(
        pool.astype(jnp.bfloat16), "rep", split_axis=0, concat_axis=0, tiled=True
    )
    fetched = fetched_half.astype(pool.dtype)
    slots = jnp.arange(slots_here, dtype=jnp.int32)
    slot_pick = (slots[:, None] == slot_index[None, :]).astype(jnp.int32)
    slot_used = jnp.sum(slot_pick, axis=1) > 0
    slot_req = jnp.sum(slot_pick * local_index[None, :], axis=1)

    def to_slots(per_req):
        taken = jnp.take(per_req, slot_req, axis=0)
        return jnp.where(slot_used.reshape((-1,) + (1,) * (per_req.ndim - 1)), taken, 0.0)

    prior_slot = to_slots(decay_now)[:, :, :, None] * jnp.einsum(
        "jhpn,jtn->jthp", fetched_half, to_slots(c_half), preferred_element_type=jnp.float32
    )
    y_prior = jnp.take(prior_slot, slot_index, axis=0)
    buffer = to_slots(carry_decay)[:, :, None, None] * fetched + split_dot(
        "jshp,jsn->jhpn", to_slots(coef[:, :, :, None] * x_heads), to_slots(b_half)
    )
    new_pool = lax.all_to_all(
        buffer.astype(jnp.bfloat16), "rep", split_axis=0, concat_axis=0, tiled=True
    ).astype(buffer.dtype)
    y_total = (y_local + y_prior).reshape(n_req * drafts, inner_here)
    gated = y_total * jax.nn.silu(z_all.astype(jnp.float32))
    sq_part = jnp.sum(gated * gated, axis=1)
    sq_hi = sq_part.astype(jnp.bfloat16)
    sq_lo = (sq_part - sq_hi.astype(jnp.float32)).astype(jnp.bfloat16)
    scaled = (gated * norm_gain[None, :]).astype(jnp.bfloat16)
    partial = jnp.dot(scaled, w_out, preferred_element_type=jnp.float32).astype(jnp.bfloat16)
    width = partial.shape[1]
    extra = jnp.zeros((partial.shape[0], 128), jnp.bfloat16)
    extra = extra.at[:, 0].set(sq_hi).at[:, 1].set(sq_lo)
    n_y = lax.axis_size("by")
    packed = jnp.concatenate([partial, extra], 1).reshape(n_y, n_blk // n_y, local_rows, width + 128)
    summed = jnp.sum(scatter2d(packed, width, 2).astype(jnp.float32), axis=0)
    inner_all = inner_here * n_blk
    mean_sq = (summed[:, width] + summed[:, width + 1]) / inner_all
    mixed = (summed[:, :width] * lax.rsqrt(mean_sq + 1e-05)[:, None]).astype(jnp.bfloat16)
    return (mixed[None], new_pool)


def solution(mesh):
    placed = (
        P("rep", "blk", None),
        P(None, "blk"),
        P(None, "blk"),
        P(),
        P(None, "blk"),
        P(None, "blk"),
        P(),
        P(None, "blk"),
        P("blk"),
        P("blk"),
        P("blk"),
        P("blk", None),
        P("rep", None, "blk"),
        P("rep", None, None),
        P("rep", "blk", None, None),
        P(),
        P("rep", None),
        P("rep"),
        P("rep"),
    )
    n_blk, n_rep = mesh.shape["blk"], mesh.shape["rep"]
    split_mesh = jax.sharding.Mesh(
        mesh.devices.reshape(Y_CHIPS, n_blk // Y_CHIPS, n_rep), AXES
    )
    placed = tuple(P(*[BLK if part == "blk" else part for part in spec]) for spec in placed)
    return jax.shard_map(
        shards,
        mesh=split_mesh,
        in_specs=placed,
        out_specs=(P("rep", BLK, None), P("rep", BLK, None, None)),
        check_vma=False,
    )
```

```python
import functools

import jax
import jax.numpy as jnp
from jax import lax
from jax.experimental import pallas as pl
from jax.experimental.pallas import tpu as pltpu
from jax.sharding import PartitionSpec as P

MESH = pl.DeviceIdType.MESH
AXES = ("by", "bz", "rep")
BLK = ("by", "bz")
Y_CHIPS = 4


def exchange_kernel(n, axis, gather, src_ref, dst_ref, send_sem, recv_sem, local_sem):
    me = lax.axis_index(axis)
    coords = {name: lax.axis_index(name) for name in AXES}

    def device_of(peer):
        return tuple(peer if name == axis else coords[name] for name in AXES)

    barrier = pltpu.get_barrier_semaphore()
    for offset in range(1, n):
        peer = lax.rem(me + offset, n)
        pl.semaphore_signal(barrier, inc=1, device_id=device_of(peer), device_id_type=MESH)
    pl.semaphore_wait(barrier, n - 1)
    local = pltpu.make_async_copy(src_ref if gather else src_ref.at[me], dst_ref.at[me], local_sem)
    local.start()
    copies = []
    for offset in range(1, n):
        peer = lax.rem(me + offset, n)
        copy = pltpu.make_async_remote_copy(
            src_ref=src_ref if gather else src_ref.at[peer],
            dst_ref=dst_ref.at[me],
            send_sem=send_sem.at[offset],
            recv_sem=recv_sem.at[offset],
            device_id=device_of(peer),
            device_id_type=MESH,
        )
        copy.start()
        copies.append(copy)
    local.wait()
    for copy in copies:
        copy.wait()


def ring4_kernel(axis, gather, src_ref, dst_ref, stage_ref, send_sem, recv_sem, local_sem):
    me = lax.axis_index(axis)
    coords = {name: lax.axis_index(name) for name in AXES}

    def device_of(peer):
        return tuple(peer if name == axis else coords[name] for name in AXES)

    right, left = lax.rem(me + 1, 4), lax.rem(me + 3, 4)
    opposite = lax.rem(me + 2, 4)
    half = dst_ref.shape[1] // 2
    first, second = pl.ds(0, half), pl.ds(half, half)

    def remote(src, dst, index, peer):
        copy = pltpu.make_async_remote_copy(
            src_ref=src,
            dst_ref=dst,
            send_sem=send_sem.at[index],
            recv_sem=recv_sem.at[index],
            device_id=device_of(peer),
            device_id_type=MESH,
        )
        copy.start()
        return copy

    barrier = pltpu.get_barrier_semaphore()
    for peer in (left, right):
        pl.semaphore_signal(barrier, inc=1, device_id=device_of(peer), device_id_type=MESH)
    pl.semaphore_wait(barrier, 2)
    local = pltpu.make_async_copy(src_ref if gather else src_ref.at[me], dst_ref.at[me], local_sem)
    local.start()
    to_right = remote(src_ref if gather else src_ref.at[right], dst_ref.at[me], 0, right)
    to_left = remote(src_ref if gather else src_ref.at[left], dst_ref.at[me], 1, left)
    if gather:
        to_right.wait_recv()
        pass_right = remote(dst_ref.at[left, first], dst_ref.at[left, first], 2, right)
        to_left.wait_recv()
        pass_left = remote(dst_ref.at[right, second], dst_ref.at[right, second], 3, left)
        to_right.wait_send()
        to_left.wait_send()
    else:
        stage_right = remote(src_ref.at[opposite, first], stage_ref.at[0], 2, right)
        stage_left = remote(src_ref.at[opposite, second], stage_ref.at[1], 3, left)
        stage_right.wait_recv()
        pass_right = remote(stage_ref.at[0], dst_ref.at[left, first], 4, right)
        stage_left.wait_recv()
        pass_left = remote(stage_ref.at[1], dst_ref.at[right, second], 5, left)
        stage_right.wait_send()
        stage_left.wait_send()
        to_right.wait()
        to_left.wait()
    local.wait()
    pass_right.wait()
    pass_left.wait()


def exchange4(src, axis, gather, collective_id):
    block = src.shape if gather else src.shape[1:]
    out = jax.ShapeDtypeStruct((4,) + tuple(block), src.dtype)
    stage = jax.ShapeDtypeStruct((2, block[0] // 2) + tuple(block[1:]), src.dtype)
    return pl.pallas_call(
        functools.partial(ring4_kernel, axis, gather),
        out_shape=(out, stage),
        in_specs=[pl.BlockSpec(memory_space=pl.ANY)],
        out_specs=(pl.BlockSpec(memory_space=pl.ANY), pl.BlockSpec(memory_space=pl.ANY)),
        scratch_shapes=[
            pltpu.SemaphoreType.DMA((6,)),
            pltpu.SemaphoreType.DMA((6,)),
            pltpu.SemaphoreType.DMA,
        ],
        compiler_params=pltpu.CompilerParams(collective_id=collective_id, has_side_effects=True),
    )(src)[0]


def gather2d_kernel(nz, src_ref, dst_ref, send_sem, recv_sem, local_sem):
    y, z = lax.axis_index("by"), lax.axis_index("bz")
    rep = lax.axis_index("rep")
    right, left = lax.rem(y + 1, 4), lax.rem(y + 3, 4)
    half = src_ref.shape[0] // 2
    first, second = pl.ds(0, half), pl.ds(half, half)
    z_sem, r_sem, l_sem, ra_sem, lb_sem = 0, nz, 2 * nz, 3 * nz, 4 * nz

    def remote(src, dst, index, yy, zz):
        copy = pltpu.make_async_remote_copy(
            src_ref=src,
            dst_ref=dst,
            send_sem=send_sem.at[index],
            recv_sem=recv_sem.at[index],
            device_id=(yy, zz, rep),
            device_id_type=MESH,
        )
        copy.start()
        return copy

    barrier = pltpu.get_barrier_semaphore()
    for offset in range(1, nz):
        pl.semaphore_signal(
            barrier, inc=1, device_id=(y, lax.rem(z + offset, nz), rep), device_id_type=MESH
        )
    for yy in (left, right):
        pl.semaphore_signal(barrier, inc=1, device_id=(yy, z, rep), device_id_type=MESH)
    pl.semaphore_wait(barrier, nz + 1)
    local = pltpu.make_async_copy(src_ref, dst_ref.at[y, z], local_sem)
    local.start()
    sent = []
    along_z = []
    for offset in range(1, nz):
        copy = remote(src_ref, dst_ref.at[y, z], z_sem + offset, y, lax.rem(z + offset, nz))
        along_z.append(copy)
    to_right = [remote(src_ref, dst_ref.at[y, z], r_sem, right, z)]
    to_left = [remote(src_ref, dst_ref.at[y, z], l_sem, left, z)]
    relays = []

    def relay(offset):
        zs = lax.rem(z + nz - offset, nz)
        to_right[offset].wait_recv()
        relays.append(
            remote(dst_ref.at[left, zs, first], dst_ref.at[left, zs, first], ra_sem + offset, right, z)
        )
        to_left[offset].wait_recv()
        relays.append(
            remote(dst_ref.at[right, zs, second], dst_ref.at[right, zs, second], lb_sem + offset, left, z)
        )

    for offset in range(1, nz):
        along_z[offset - 1].wait_recv()
        zs = lax.rem(z + nz - offset, nz)
        to_right.append(remote(dst_ref.at[y, zs], dst_ref.at[y, zs], r_sem + offset, right, z))
        to_left.append(remote(dst_ref.at[y, zs], dst_ref.at[y, zs], l_sem + offset, left, z))
        relay(offset - 1)
    relay(nz - 1)
    local.wait()
    for copy in along_z + to_right + to_left:
        copy.wait_send()
    for copy in relays:
        copy.wait()


def gather2d(src, collective_id):
    nz = lax.axis_size("bz")
    return pl.pallas_call(
        functools.partial(gather2d_kernel, nz),
        out_shape=jax.ShapeDtypeStruct((4, nz) + tuple(src.shape), src.dtype),
        in_specs=[pl.BlockSpec(memory_space=pl.ANY)],
        out_specs=pl.BlockSpec(memory_space=pl.ANY),
        scratch_shapes=[
            pltpu.SemaphoreType.DMA((5 * nz,)),
            pltpu.SemaphoreType.DMA((5 * nz,)),
            pltpu.SemaphoreType.DMA,
        ],
        compiler_params=pltpu.CompilerParams(collective_id=collective_id, has_side_effects=True),
    )(src)


def exchange(src, axis, gather, collective_id):
    n = lax.axis_size(axis)
    block = src.shape if gather else src.shape[1:]
    return pl.pallas_call(
        functools.partial(exchange_kernel, n, axis, gather),
        out_shape=jax.ShapeDtypeStruct((n,) + tuple(block), src.dtype),
        in_specs=[pl.BlockSpec(memory_space=pl.ANY)],
        out_specs=pl.BlockSpec(memory_space=pl.ANY),
        scratch_shapes=[
            pltpu.SemaphoreType.DMA((n,)),
            pltpu.SemaphoreType.DMA((n,)),
            pltpu.SemaphoreType.DMA,
        ],
        compiler_params=pltpu.CompilerParams(collective_id=collective_id, has_side_effects=True),
    )(src)


def convolve(edge_cells, fresh_cells, kernel, edge_mask):
    sequence = jnp.concatenate(
        [edge_cells * edge_mask[:, :, None].astype(edge_cells.dtype), fresh_cells], 1
    ).astype(jnp.float32)
    steps_count = fresh_cells.shape[1]
    summed = kernel[0] * sequence[:, 0:steps_count]
    for offset in range(1, kernel.shape[0]):
        summed = summed + kernel[offset] * sequence[:, offset : offset + steps_count]
    return jax.nn.silu(summed).astype(jnp.bfloat16)


def split_dot(spec, wide, narrow):
    high = wide.astype(jnp.bfloat16)
    low = (wide - high.astype(jnp.float32)).astype(jnp.bfloat16)
    return jnp.einsum(spec, high, narrow, preferred_element_type=jnp.float32) + jnp.einsum(
        spec, low, narrow, preferred_element_type=jnp.float32
    )


def shards(
    hidden_in,
    w_z,
    w_x,
    w_bc,
    w_dt,
    conv_x,
    conv_bc,
    dt_bias,
    a_log,
    d_skip,
    norm_gain,
    w_out,
    edge_x,
    edge_bc,
    pool,
    tenant_sizes,
    owner,
    accepted,
    prompt_len,
):
    highest = lax.Precision.HIGHEST
    rows_in = hidden_in[0]
    local_rows = rows_in.shape[0]
    n_req = edge_x.shape[0]
    drafts = local_rows * lax.axis_size(BLK) // n_req
    state_dim = w_bc.shape[1] // 2
    heads_here = w_dt.shape[1]
    inner_here = w_z.shape[1]
    head_dim = inner_here // heads_here
    slots_here = pool.shape[0]
    cap_group = slots_here // lax.axis_size("rep")
    weights_in = (w_z, w_x, w_dt, w_bc)
    n_blk = lax.axis_size(BLK)
    block_rows = gather2d(rows_in, 0).reshape(n_blk * local_rows, rows_in.shape[1])
    projected = jnp.concatenate(
        [
            jnp.dot(block_rows, weight_cols, preferred_element_type=jnp.float32)
            for weight_cols in weights_in
        ],
        1,
    ).astype(jnp.bfloat16)
    z_all = projected[:, :inner_here]
    u_all = projected[:, inner_here : 2 * inner_here]
    dt_raw = projected[:, 2 * inner_here : 2 * inner_here + heads_here]
    bc_all = projected[:, 2 * inner_here + heads_here :]
    edge_len = edge_x.shape[1]
    edge_mask = prompt_len[:, None] >= (edge_len - jnp.arange(edge_len, dtype=jnp.int32))[None, :]
    x_conv = convolve(edge_x, u_all.reshape(n_req, drafts, inner_here), conv_x, edge_mask)
    bc_conv = convolve(edge_bc, bc_all.reshape(n_req, drafts, 2 * state_dim), conv_bc, edge_mask)
    b_half = bc_conv[:, :, :state_dim]
    c_half = bc_conv[:, :, state_dim:]
    b_float = b_half.astype(jnp.float32)
    c_float = c_half.astype(jnp.float32)
    x_heads = x_conv.reshape(n_req, drafts, heads_here, head_dim).astype(jnp.float32)
    req_index = lax.axis_index("rep") * n_req + jnp.arange(n_req, dtype=jnp.int32)
    tenant_ends = jnp.cumsum(tenant_sizes)
    tenant_id = jnp.sum((req_index[:, None] >= tenant_ends[None, :-1]).astype(jnp.int32), axis=1)
    tenant_pick = (
        tenant_id[:, None] == jnp.arange(tenant_sizes.shape[0], dtype=jnp.int32)[None, :]
    ).astype(jnp.float32)
    bias_req = jnp.dot(tenant_pick, dt_bias, precision=highest)
    step_size = jax.nn.softplus(
        dt_raw.reshape(n_req, drafts, heads_here).astype(jnp.float32) + bias_req[:, None, :]
    )
    log_decay = jnp.cumsum(step_size * (-jnp.exp(a_log))[None, None, :], axis=1)
    draft_index = jnp.arange(drafts, dtype=jnp.int32)
    causal = draft_index[:, None] >= draft_index[None, :]
    scores = jnp.einsum("rtn,rsn->rts", c_half, b_half, preferred_element_type=jnp.float32)
    log_gap = log_decay[:, :, None, :] - log_decay[:, None, :, :]
    weight = (
        jnp.where(causal[None, :, :, None], jnp.exp(jnp.minimum(log_gap, 0.0)), 0.0)
        * step_size[:, None, :, :]
        * scores[:, :, :, None]
    )
    y_local = (
        split_dot("rtsh,rshp->rthp", weight, x_conv.reshape(n_req, drafts, heads_here, head_dim))
        + d_skip[None, None, :, None] * x_heads
    )
    pick_last = (draft_index[None, :] == accepted[:, None] - 1).astype(jnp.float32)
    log_accept = jnp.sum(pick_last[:, :, None] * log_decay, axis=1)
    keep_draft = draft_index[None, :] < accepted[:, None]
    coef = (
        jnp.where(
            keep_draft[:, :, None],
            jnp.exp(jnp.minimum(log_accept[:, None, :] - log_decay, 0.0)),
            0.0,
        )
        * step_size
    )
    carry_decay = jnp.exp(log_accept)
    decay_now = jnp.exp(log_decay)
    owner_of = owner[:, 0]
    local_index = jnp.arange(n_req, dtype=jnp.int32)
    earlier = (owner_of[None, :] == owner_of[:, None]) & (
        local_index[None, :] < local_index[:, None]
    )
    rank_within = jnp.sum(earlier.astype(jnp.int32), axis=1)
    slot_index = owner_of * cap_group + rank_within
    fetched_half = lax.all_to_all(
        pool.astype(jnp.bfloat16), "rep", split_axis=0, concat_axis=0, tiled=True
    )
    fetched = fetched_half.astype(pool.dtype)
    slots = jnp.arange(slots_here, dtype=jnp.int32)
    slot_pick = (slots[:, None] == slot_index[None, :]).astype(jnp.int32)
    slot_used = jnp.sum(slot_pick, axis=1) > 0
    slot_req = jnp.sum(slot_pick * local_index[None, :], axis=1)

    def to_slots(per_req):
        taken = jnp.take(per_req, slot_req, axis=0)
        return jnp.where(slot_used.reshape((-1,) + (1,) * (per_req.ndim - 1)), taken, 0.0)

    prior_slot = to_slots(decay_now)[:, :, :, None] * jnp.einsum(
        "jhpn,jtn->jthp", fetched_half, to_slots(c_half), preferred_element_type=jnp.float32
    )
    y_prior = jnp.take(prior_slot, slot_index, axis=0)
    buffer = to_slots(carry_decay)[:, :, None, None] * fetched + split_dot(
        "jshp,jsn->jhpn", to_slots(coef[:, :, :, None] * x_heads), to_slots(b_half)
    )
    new_pool = lax.all_to_all(
        buffer.astype(jnp.bfloat16), "rep", split_axis=0, concat_axis=0, tiled=True
    ).astype(buffer.dtype)
    y_total = (y_local + y_prior).reshape(n_req * drafts, inner_here)
    gated = y_total * jax.nn.silu(z_all.astype(jnp.float32))
    sq_part = jnp.sum(gated * gated, axis=1)
    sq_hi = sq_part.astype(jnp.bfloat16)
    sq_lo = (sq_part - sq_hi.astype(jnp.float32)).astype(jnp.bfloat16)
    scaled = (gated * norm_gain[None, :]).astype(jnp.bfloat16)
    partial = jnp.dot(scaled, w_out, preferred_element_type=jnp.float32).astype(jnp.bfloat16)
    width = partial.shape[1]
    extra = jnp.zeros((partial.shape[0], 128), jnp.bfloat16)
    extra = extra.at[:, 0].set(sq_hi).at[:, 1].set(sq_lo)
    n_y = lax.axis_size("by")
    packed = jnp.concatenate([partial, extra], 1).reshape(n_y, n_blk // n_y, local_rows, width + 128)
    half_sum = jnp.sum(exchange4(packed, "by", False, 2).astype(jnp.float32), axis=0)
    sq_mid = half_sum[:, :, width] + half_sum[:, :, width + 1]
    sq_mid_hi = sq_mid.astype(jnp.bfloat16)
    sq_mid_lo = (sq_mid - sq_mid_hi.astype(jnp.float32)).astype(jnp.bfloat16)
    half_packed = (
        half_sum.astype(jnp.bfloat16).at[:, :, width].set(sq_mid_hi).at[:, :, width + 1].set(sq_mid_lo)
    )
    summed = jnp.sum(exchange(half_packed, "bz", False, 3).astype(jnp.float32), axis=0)
    inner_all = inner_here * n_blk
    mean_sq = (summed[:, width] + summed[:, width + 1]) / inner_all
    mixed = (summed[:, :width] * lax.rsqrt(mean_sq + 1e-05)[:, None]).astype(jnp.bfloat16)
    return (mixed[None], new_pool)


def solution(mesh):
    placed = (
        P("rep", "blk", None),
        P(None, "blk"),
        P(None, "blk"),
        P(),
        P(None, "blk"),
        P(None, "blk"),
        P(),
        P(None, "blk"),
        P("blk"),
        P("blk"),
        P("blk"),
        P("blk", None),
        P("rep", None, "blk"),
        P("rep", None, None),
        P("rep", "blk", None, None),
        P(),
        P("rep", None),
        P("rep"),
        P("rep"),
    )
    n_blk, n_rep = mesh.shape["blk"], mesh.shape["rep"]
    split_mesh = jax.sharding.Mesh(
        mesh.devices.reshape(Y_CHIPS, n_blk // Y_CHIPS, n_rep), AXES
    )
    placed = tuple(P(*[BLK if part == "blk" else part for part in spec]) for spec in placed)
    return jax.shard_map(
        shards,
        mesh=split_mesh,
        in_specs=placed,
        out_specs=(P("rep", BLK, None), P("rep", BLK, None, None)),
        check_vma=False,
    )
```

```python
import functools

import jax
import jax.numpy as jnp
from jax import lax
from jax.experimental import pallas as pl
from jax.experimental.pallas import tpu as pltpu
from jax.sharding import PartitionSpec as P

MESH = pl.DeviceIdType.MESH
AXES = ("by", "bz", "rep")
BLK = ("by", "bz")
Y_CHIPS = 4


def exchange_kernel(n, axis, gather, src_ref, dst_ref, send_sem, recv_sem, local_sem):
    me = lax.axis_index(axis)
    coords = {name: lax.axis_index(name) for name in AXES}

    def device_of(peer):
        return tuple(peer if name == axis else coords[name] for name in AXES)

    barrier = pltpu.get_barrier_semaphore()
    for offset in range(1, n):
        peer = lax.rem(me + offset, n)
        pl.semaphore_signal(barrier, inc=1, device_id=device_of(peer), device_id_type=MESH)
    pl.semaphore_wait(barrier, n - 1)
    local = pltpu.make_async_copy(src_ref if gather else src_ref.at[me], dst_ref.at[me], local_sem)
    local.start()
    copies = []
    for offset in range(1, n):
        peer = lax.rem(me + offset, n)
        copy = pltpu.make_async_remote_copy(
            src_ref=src_ref if gather else src_ref.at[peer],
            dst_ref=dst_ref.at[me],
            send_sem=send_sem.at[offset],
            recv_sem=recv_sem.at[offset],
            device_id=device_of(peer),
            device_id_type=MESH,
        )
        copy.start()
        copies.append(copy)
    local.wait()
    for copy in copies:
        copy.wait()


def ring4_kernel(axis, gather, src_ref, dst_ref, stage_ref, send_sem, recv_sem, local_sem):
    me = lax.axis_index(axis)
    coords = {name: lax.axis_index(name) for name in AXES}

    def device_of(peer):
        return tuple(peer if name == axis else coords[name] for name in AXES)

    right, left = lax.rem(me + 1, 4), lax.rem(me + 3, 4)
    opposite = lax.rem(me + 2, 4)
    half = dst_ref.shape[1] // 2
    first, second = pl.ds(0, half), pl.ds(half, half)

    def remote(src, dst, index, peer):
        copy = pltpu.make_async_remote_copy(
            src_ref=src,
            dst_ref=dst,
            send_sem=send_sem.at[index],
            recv_sem=recv_sem.at[index],
            device_id=device_of(peer),
            device_id_type=MESH,
        )
        copy.start()
        return copy

    barrier = pltpu.get_barrier_semaphore()
    for peer in (left, right):
        pl.semaphore_signal(barrier, inc=1, device_id=device_of(peer), device_id_type=MESH)
    pl.semaphore_wait(barrier, 2)
    local = pltpu.make_async_copy(src_ref if gather else src_ref.at[me], dst_ref.at[me], local_sem)
    local.start()
    to_right = remote(src_ref if gather else src_ref.at[right], dst_ref.at[me], 0, right)
    to_left = remote(src_ref if gather else src_ref.at[left], dst_ref.at[me], 1, left)
    if gather:
        to_right.wait_recv()
        pass_right = remote(dst_ref.at[left, first], dst_ref.at[left, first], 2, right)
        to_left.wait_recv()
        pass_left = remote(dst_ref.at[right, second], dst_ref.at[right, second], 3, left)
        to_right.wait_send()
        to_left.wait_send()
    else:
        stage_right = remote(src_ref.at[opposite, first], stage_ref.at[0], 2, right)
        stage_left = remote(src_ref.at[opposite, second], stage_ref.at[1], 3, left)
        stage_right.wait_recv()
        pass_right = remote(stage_ref.at[0], dst_ref.at[left, first], 4, right)
        stage_left.wait_recv()
        pass_left = remote(stage_ref.at[1], dst_ref.at[right, second], 5, left)
        stage_right.wait_send()
        stage_left.wait_send()
        to_right.wait()
        to_left.wait()
    local.wait()
    pass_right.wait()
    pass_left.wait()


def exchange4(src, axis, gather, collective_id):
    block = src.shape if gather else src.shape[1:]
    out = jax.ShapeDtypeStruct((4,) + tuple(block), src.dtype)
    stage = jax.ShapeDtypeStruct((2, block[0] // 2) + tuple(block[1:]), src.dtype)
    return pl.pallas_call(
        functools.partial(ring4_kernel, axis, gather),
        out_shape=(out, stage),
        in_specs=[pl.BlockSpec(memory_space=pl.ANY)],
        out_specs=(pl.BlockSpec(memory_space=pl.ANY), pl.BlockSpec(memory_space=pl.ANY)),
        scratch_shapes=[
            pltpu.SemaphoreType.DMA((6,)),
            pltpu.SemaphoreType.DMA((6,)),
            pltpu.SemaphoreType.DMA,
        ],
        compiler_params=pltpu.CompilerParams(collective_id=collective_id, has_side_effects=True),
    )(src)[0]


def gather2d_kernel(nz, src_ref, dst_ref, send_sem, recv_sem, local_sem):
    y, z = lax.axis_index("by"), lax.axis_index("bz")
    rep = lax.axis_index("rep")
    right, left = lax.rem(y + 1, 4), lax.rem(y + 3, 4)
    half = src_ref.shape[0] // 2
    first, second = pl.ds(0, half), pl.ds(half, half)
    z_sem, r_sem, l_sem, ra_sem, lb_sem = 0, nz, 2 * nz, 3 * nz, 4 * nz

    def remote(src, dst, index, yy, zz):
        copy = pltpu.make_async_remote_copy(
            src_ref=src,
            dst_ref=dst,
            send_sem=send_sem.at[index],
            recv_sem=recv_sem.at[index],
            device_id=(yy, zz, rep),
            device_id_type=MESH,
        )
        copy.start()
        return copy

    barrier = pltpu.get_barrier_semaphore()
    for offset in range(1, nz):
        pl.semaphore_signal(
            barrier, inc=1, device_id=(y, lax.rem(z + offset, nz), rep), device_id_type=MESH
        )
    for yy in (left, right):
        pl.semaphore_signal(barrier, inc=1, device_id=(yy, z, rep), device_id_type=MESH)
    pl.semaphore_wait(barrier, nz + 1)
    local = pltpu.make_async_copy(src_ref, dst_ref.at[y, z], local_sem)
    local.start()
    nearest = sorted(range(1, nz), key=lambda offset: (min(offset, nz - offset), offset))
    along_z = {}
    for offset in nearest:
        along_z[offset] = remote(src_ref, dst_ref.at[y, z], z_sem + offset, y, lax.rem(z + offset, nz))
    to_right = [remote(src_ref, dst_ref.at[y, z], r_sem, right, z)]
    to_left = [remote(src_ref, dst_ref.at[y, z], l_sem, left, z)]
    relays = []

    def relay(offset):
        zs = lax.rem(z + nz - offset, nz)
        to_right[offset].wait_recv()
        relays.append(
            remote(dst_ref.at[left, zs, first], dst_ref.at[left, zs, first], ra_sem + offset, right, z)
        )
        to_left[offset].wait_recv()
        relays.append(
            remote(dst_ref.at[right, zs, second], dst_ref.at[right, zs, second], lb_sem + offset, left, z)
        )

    to_right, to_left = {0: to_right[0]}, {0: to_left[0]}
    before = 0
    for offset in nearest:
        along_z[offset].wait_recv()
        zs = lax.rem(z + nz - offset, nz)
        to_right[offset] = remote(dst_ref.at[y, zs], dst_ref.at[y, zs], r_sem + offset, right, z)
        to_left[offset] = remote(dst_ref.at[y, zs], dst_ref.at[y, zs], l_sem + offset, left, z)
        relay(before)
        before = offset
    relay(before)
    local.wait()
    for copy in list(along_z.values()) + list(to_right.values()) + list(to_left.values()):
        copy.wait_send()
    for copy in relays:
        copy.wait()


def gather2d(src, collective_id):
    nz = lax.axis_size("bz")
    return pl.pallas_call(
        functools.partial(gather2d_kernel, nz),
        out_shape=jax.ShapeDtypeStruct((4, nz) + tuple(src.shape), src.dtype),
        in_specs=[pl.BlockSpec(memory_space=pl.ANY)],
        out_specs=pl.BlockSpec(memory_space=pl.ANY),
        scratch_shapes=[
            pltpu.SemaphoreType.DMA((5 * nz,)),
            pltpu.SemaphoreType.DMA((5 * nz,)),
            pltpu.SemaphoreType.DMA,
        ],
        compiler_params=pltpu.CompilerParams(collective_id=collective_id, has_side_effects=True),
    )(src)


def exchange(src, axis, gather, collective_id):
    n = lax.axis_size(axis)
    block = src.shape if gather else src.shape[1:]
    return pl.pallas_call(
        functools.partial(exchange_kernel, n, axis, gather),
        out_shape=jax.ShapeDtypeStruct((n,) + tuple(block), src.dtype),
        in_specs=[pl.BlockSpec(memory_space=pl.ANY)],
        out_specs=pl.BlockSpec(memory_space=pl.ANY),
        scratch_shapes=[
            pltpu.SemaphoreType.DMA((n,)),
            pltpu.SemaphoreType.DMA((n,)),
            pltpu.SemaphoreType.DMA,
        ],
        compiler_params=pltpu.CompilerParams(collective_id=collective_id, has_side_effects=True),
    )(src)


def convolve(edge_cells, fresh_cells, kernel, edge_mask):
    sequence = jnp.concatenate(
        [edge_cells * edge_mask[:, :, None].astype(edge_cells.dtype), fresh_cells], 1
    ).astype(jnp.float32)
    steps_count = fresh_cells.shape[1]
    summed = kernel[0] * sequence[:, 0:steps_count]
    for offset in range(1, kernel.shape[0]):
        summed = summed + kernel[offset] * sequence[:, offset : offset + steps_count]
    return jax.nn.silu(summed).astype(jnp.bfloat16)


def split_dot(spec, wide, narrow):
    high = wide.astype(jnp.bfloat16)
    low = (wide - high.astype(jnp.float32)).astype(jnp.bfloat16)
    return jnp.einsum(spec, high, narrow, preferred_element_type=jnp.float32) + jnp.einsum(
        spec, low, narrow, preferred_element_type=jnp.float32
    )


def shards(
    hidden_in,
    w_z,
    w_x,
    w_bc,
    w_dt,
    conv_x,
    conv_bc,
    dt_bias,
    a_log,
    d_skip,
    norm_gain,
    w_out,
    edge_x,
    edge_bc,
    pool,
    tenant_sizes,
    owner,
    accepted,
    prompt_len,
):
    highest = lax.Precision.HIGHEST
    rows_in = hidden_in[0]
    local_rows = rows_in.shape[0]
    n_req = edge_x.shape[0]
    drafts = local_rows * lax.axis_size(BLK) // n_req
    state_dim = w_bc.shape[1] // 2
    heads_here = w_dt.shape[1]
    inner_here = w_z.shape[1]
    head_dim = inner_here // heads_here
    slots_here = pool.shape[0]
    cap_group = slots_here // lax.axis_size("rep")
    weights_in = (w_z, w_x, w_dt, w_bc)
    n_blk = lax.axis_size(BLK)
    block_rows = gather2d(rows_in, 0).reshape(n_blk * local_rows, rows_in.shape[1])
    projected = jnp.concatenate(
        [
            jnp.dot(block_rows, weight_cols, preferred_element_type=jnp.float32)
            for weight_cols in weights_in
        ],
        1,
    ).astype(jnp.bfloat16)
    z_all = projected[:, :inner_here]
    u_all = projected[:, inner_here : 2 * inner_here]
    dt_raw = projected[:, 2 * inner_here : 2 * inner_here + heads_here]
    bc_all = projected[:, 2 * inner_here + heads_here :]
    edge_len = edge_x.shape[1]
    edge_mask = prompt_len[:, None] >= (edge_len - jnp.arange(edge_len, dtype=jnp.int32))[None, :]
    x_conv = convolve(edge_x, u_all.reshape(n_req, drafts, inner_here), conv_x, edge_mask)
    bc_conv = convolve(edge_bc, bc_all.reshape(n_req, drafts, 2 * state_dim), conv_bc, edge_mask)
    b_half = bc_conv[:, :, :state_dim]
    c_half = bc_conv[:, :, state_dim:]
    b_float = b_half.astype(jnp.float32)
    c_float = c_half.astype(jnp.float32)
    x_heads = x_conv.reshape(n_req, drafts, heads_here, head_dim).astype(jnp.float32)
    req_index = lax.axis_index("rep") * n_req + jnp.arange(n_req, dtype=jnp.int32)
    tenant_ends = jnp.cumsum(tenant_sizes)
    tenant_id = jnp.sum((req_index[:, None] >= tenant_ends[None, :-1]).astype(jnp.int32), axis=1)
    tenant_pick = (
        tenant_id[:, None] == jnp.arange(tenant_sizes.shape[0], dtype=jnp.int32)[None, :]
    ).astype(jnp.float32)
    bias_req = jnp.dot(tenant_pick, dt_bias, precision=highest)
    step_size = jax.nn.softplus(
        dt_raw.reshape(n_req, drafts, heads_here).astype(jnp.float32) + bias_req[:, None, :]
    )
    log_decay = jnp.cumsum(step_size * (-jnp.exp(a_log))[None, None, :], axis=1)
    draft_index = jnp.arange(drafts, dtype=jnp.int32)
    causal = draft_index[:, None] >= draft_index[None, :]
    scores = jnp.einsum("rtn,rsn->rts", c_half, b_half, preferred_element_type=jnp.float32)
    log_gap = log_decay[:, :, None, :] - log_decay[:, None, :, :]
    weight = (
        jnp.where(causal[None, :, :, None], jnp.exp(jnp.minimum(log_gap, 0.0)), 0.0)
        * step_size[:, None, :, :]
        * scores[:, :, :, None]
    )
    y_local = (
        split_dot("rtsh,rshp->rthp", weight, x_conv.reshape(n_req, drafts, heads_here, head_dim))
        + d_skip[None, None, :, None] * x_heads
    )
    pick_last = (draft_index[None, :] == accepted[:, None] - 1).astype(jnp.float32)
    log_accept = jnp.sum(pick_last[:, :, None] * log_decay, axis=1)
    keep_draft = draft_index[None, :] < accepted[:, None]
    coef = (
        jnp.where(
            keep_draft[:, :, None],
            jnp.exp(jnp.minimum(log_accept[:, None, :] - log_decay, 0.0)),
            0.0,
        )
        * step_size
    )
    carry_decay = jnp.exp(log_accept)
    decay_now = jnp.exp(log_decay)
    owner_of = owner[:, 0]
    local_index = jnp.arange(n_req, dtype=jnp.int32)
    earlier = (owner_of[None, :] == owner_of[:, None]) & (
        local_index[None, :] < local_index[:, None]
    )
    rank_within = jnp.sum(earlier.astype(jnp.int32), axis=1)
    slot_index = owner_of * cap_group + rank_within
    fetched_half = lax.all_to_all(
        pool.astype(jnp.bfloat16), "rep", split_axis=0, concat_axis=0, tiled=True
    )
    fetched = fetched_half.astype(pool.dtype)
    slots = jnp.arange(slots_here, dtype=jnp.int32)
    slot_pick = (slots[:, None] == slot_index[None, :]).astype(jnp.int32)
    slot_used = jnp.sum(slot_pick, axis=1) > 0
    slot_req = jnp.sum(slot_pick * local_index[None, :], axis=1)

    def to_slots(per_req):
        taken = jnp.take(per_req, slot_req, axis=0)
        return jnp.where(slot_used.reshape((-1,) + (1,) * (per_req.ndim - 1)), taken, 0.0)

    prior_slot = to_slots(decay_now)[:, :, :, None] * jnp.einsum(
        "jhpn,jtn->jthp", fetched_half, to_slots(c_half), preferred_element_type=jnp.float32
    )
    y_prior = jnp.take(prior_slot, slot_index, axis=0)
    buffer = to_slots(carry_decay)[:, :, None, None] * fetched + split_dot(
        "jshp,jsn->jhpn", to_slots(coef[:, :, :, None] * x_heads), to_slots(b_half)
    )
    new_pool = lax.all_to_all(
        buffer.astype(jnp.bfloat16), "rep", split_axis=0, concat_axis=0, tiled=True
    ).astype(buffer.dtype)
    y_total = (y_local + y_prior).reshape(n_req * drafts, inner_here)
    gated = y_total * jax.nn.silu(z_all.astype(jnp.float32))
    sq_part = jnp.sum(gated * gated, axis=1)
    sq_hi = sq_part.astype(jnp.bfloat16)
    sq_lo = (sq_part - sq_hi.astype(jnp.float32)).astype(jnp.bfloat16)
    scaled = (gated * norm_gain[None, :]).astype(jnp.bfloat16)
    partial = jnp.dot(scaled, w_out, preferred_element_type=jnp.float32).astype(jnp.bfloat16)
    width = partial.shape[1]
    extra = jnp.zeros((partial.shape[0], 128), jnp.bfloat16)
    extra = extra.at[:, 0].set(sq_hi).at[:, 1].set(sq_lo)
    n_y = lax.axis_size("by")
    packed = jnp.concatenate([partial, extra], 1).reshape(n_y, n_blk // n_y, local_rows, width + 128)
    half_sum = jnp.sum(exchange4(packed, "by", False, 2).astype(jnp.float32), axis=0)
    sq_mid = half_sum[:, :, width] + half_sum[:, :, width + 1]
    sq_mid_hi = sq_mid.astype(jnp.bfloat16)
    sq_mid_lo = (sq_mid - sq_mid_hi.astype(jnp.float32)).astype(jnp.bfloat16)
    half_packed = (
        half_sum.astype(jnp.bfloat16).at[:, :, width].set(sq_mid_hi).at[:, :, width + 1].set(sq_mid_lo)
    )
    summed = jnp.sum(exchange(half_packed, "bz", False, 3).astype(jnp.float32), axis=0)
    inner_all = inner_here * n_blk
    mean_sq = (summed[:, width] + summed[:, width + 1]) / inner_all
    mixed = (summed[:, :width] * lax.rsqrt(mean_sq + 1e-05)[:, None]).astype(jnp.bfloat16)
    return (mixed[None], new_pool)


def solution(mesh):
    placed = (
        P("rep", "blk", None),
        P(None, "blk"),
        P(None, "blk"),
        P(),
        P(None, "blk"),
        P(None, "blk"),
        P(),
        P(None, "blk"),
        P("blk"),
        P("blk"),
        P("blk"),
        P("blk", None),
        P("rep", None, "blk"),
        P("rep", None, None),
        P("rep", "blk", None, None),
        P(),
        P("rep", None),
        P("rep"),
        P("rep"),
    )
    n_blk, n_rep = mesh.shape["blk"], mesh.shape["rep"]
    split_mesh = jax.sharding.Mesh(
        mesh.devices.reshape(Y_CHIPS, n_blk // Y_CHIPS, n_rep), AXES
    )
    placed = tuple(P(*[BLK if part == "blk" else part for part in spec]) for spec in placed)
    return jax.shard_map(
        shards,
        mesh=split_mesh,
        in_specs=placed,
        out_specs=(P("rep", BLK, None), P("rep", BLK, None, None)),
        check_vma=False,
    )
```

```python
import functools

import jax
import jax.numpy as jnp
from jax import lax
from jax.experimental import pallas as pl
from jax.experimental.pallas import tpu as pltpu
from jax.sharding import PartitionSpec as P

MESH = pl.DeviceIdType.MESH
AXES = ("by", "bz", "rep")
BLK = ("by", "bz")
Y_CHIPS = 4


def exchange_kernel(n, axis, gather, src_ref, dst_ref, send_sem, recv_sem, local_sem):
    me = lax.axis_index(axis)
    coords = {name: lax.axis_index(name) for name in AXES}

    def device_of(peer):
        return tuple(peer if name == axis else coords[name] for name in AXES)

    barrier = pltpu.get_barrier_semaphore()
    for offset in range(1, n):
        peer = lax.rem(me + offset, n)
        pl.semaphore_signal(barrier, inc=1, device_id=device_of(peer), device_id_type=MESH)
    pl.semaphore_wait(barrier, n - 1)
    local = pltpu.make_async_copy(src_ref if gather else src_ref.at[me], dst_ref.at[me], local_sem)
    local.start()
    copies = []
    for offset in sorted(range(1, n), key=lambda offset: (min(offset, n - offset), offset)):
        peer = lax.rem(me + offset, n)
        copy = pltpu.make_async_remote_copy(
            src_ref=src_ref if gather else src_ref.at[peer],
            dst_ref=dst_ref.at[me],
            send_sem=send_sem.at[offset],
            recv_sem=recv_sem.at[offset],
            device_id=device_of(peer),
            device_id_type=MESH,
        )
        copy.start()
        copies.append(copy)
    local.wait()
    for copy in copies:
        copy.wait()


def ring4_kernel(axis, gather, src_ref, dst_ref, stage_ref, send_sem, recv_sem, local_sem):
    me = lax.axis_index(axis)
    coords = {name: lax.axis_index(name) for name in AXES}

    def device_of(peer):
        return tuple(peer if name == axis else coords[name] for name in AXES)

    right, left = lax.rem(me + 1, 4), lax.rem(me + 3, 4)
    opposite = lax.rem(me + 2, 4)
    half = dst_ref.shape[1] // 2
    first, second = pl.ds(0, half), pl.ds(half, half)

    def remote(src, dst, index, peer):
        copy = pltpu.make_async_remote_copy(
            src_ref=src,
            dst_ref=dst,
            send_sem=send_sem.at[index],
            recv_sem=recv_sem.at[index],
            device_id=device_of(peer),
            device_id_type=MESH,
        )
        copy.start()
        return copy

    barrier = pltpu.get_barrier_semaphore()
    for peer in (left, right):
        pl.semaphore_signal(barrier, inc=1, device_id=device_of(peer), device_id_type=MESH)
    pl.semaphore_wait(barrier, 2)
    if not gather:
        stage_right = remote(src_ref.at[opposite, first], stage_ref.at[0], 2, right)
        stage_left = remote(src_ref.at[opposite, second], stage_ref.at[1], 3, left)
    local = pltpu.make_async_copy(src_ref if gather else src_ref.at[me], dst_ref.at[me], local_sem)
    local.start()
    to_right = remote(src_ref if gather else src_ref.at[right], dst_ref.at[me], 0, right)
    to_left = remote(src_ref if gather else src_ref.at[left], dst_ref.at[me], 1, left)
    if gather:
        to_right.wait_recv()
        pass_right = remote(dst_ref.at[left, first], dst_ref.at[left, first], 2, right)
        to_left.wait_recv()
        pass_left = remote(dst_ref.at[right, second], dst_ref.at[right, second], 3, left)
        to_right.wait_send()
        to_left.wait_send()
    else:
        stage_right.wait_recv()
        pass_right = remote(stage_ref.at[0], dst_ref.at[left, first], 4, right)
        stage_left.wait_recv()
        pass_left = remote(stage_ref.at[1], dst_ref.at[right, second], 5, left)
        stage_right.wait_send()
        stage_left.wait_send()
        to_right.wait()
        to_left.wait()
    local.wait()
    pass_right.wait()
    pass_left.wait()


def exchange4(src, axis, gather, collective_id):
    block = src.shape if gather else src.shape[1:]
    out = jax.ShapeDtypeStruct((4,) + tuple(block), src.dtype)
    stage = jax.ShapeDtypeStruct((2, block[0] // 2) + tuple(block[1:]), src.dtype)
    return pl.pallas_call(
        functools.partial(ring4_kernel, axis, gather),
        out_shape=(out, stage),
        in_specs=[pl.BlockSpec(memory_space=pl.ANY)],
        out_specs=(pl.BlockSpec(memory_space=pl.ANY), pl.BlockSpec(memory_space=pl.ANY)),
        scratch_shapes=[
            pltpu.SemaphoreType.DMA((6,)),
            pltpu.SemaphoreType.DMA((6,)),
            pltpu.SemaphoreType.DMA,
        ],
        compiler_params=pltpu.CompilerParams(collective_id=collective_id, has_side_effects=True),
    )(src)[0]


def gather2d_kernel(nz, src_ref, dst_ref, send_sem, recv_sem, local_sem):
    y, z = lax.axis_index("by"), lax.axis_index("bz")
    rep = lax.axis_index("rep")
    right, left = lax.rem(y + 1, 4), lax.rem(y + 3, 4)
    half = src_ref.shape[0] // 2
    first, second = pl.ds(0, half), pl.ds(half, half)
    z_sem, r_sem, l_sem, ra_sem, lb_sem = 0, nz, 2 * nz, 3 * nz, 4 * nz

    def remote(src, dst, index, yy, zz):
        copy = pltpu.make_async_remote_copy(
            src_ref=src,
            dst_ref=dst,
            send_sem=send_sem.at[index],
            recv_sem=recv_sem.at[index],
            device_id=(yy, zz, rep),
            device_id_type=MESH,
        )
        copy.start()
        return copy

    barrier = pltpu.get_barrier_semaphore()
    for offset in range(1, nz):
        pl.semaphore_signal(
            barrier, inc=1, device_id=(y, lax.rem(z + offset, nz), rep), device_id_type=MESH
        )
    for yy in (left, right):
        pl.semaphore_signal(barrier, inc=1, device_id=(yy, z, rep), device_id_type=MESH)
    pl.semaphore_wait(barrier, nz + 1)
    local = pltpu.make_async_copy(src_ref, dst_ref.at[y, z], local_sem)
    local.start()
    nearest = sorted(range(1, nz), key=lambda offset: (min(offset, nz - offset), offset))
    along_z = {}
    for offset in nearest:
        along_z[offset] = remote(src_ref, dst_ref.at[y, z], z_sem + offset, y, lax.rem(z + offset, nz))
    to_right = [remote(src_ref, dst_ref.at[y, z], r_sem, right, z)]
    to_left = [remote(src_ref, dst_ref.at[y, z], l_sem, left, z)]
    relays = []

    def relay(offset):
        zs = lax.rem(z + nz - offset, nz)
        to_right[offset].wait_recv()
        relays.append(
            remote(dst_ref.at[left, zs, first], dst_ref.at[left, zs, first], ra_sem + offset, right, z)
        )
        to_left[offset].wait_recv()
        relays.append(
            remote(dst_ref.at[right, zs, second], dst_ref.at[right, zs, second], lb_sem + offset, left, z)
        )

    to_right, to_left = {0: to_right[0]}, {0: to_left[0]}
    before = 0
    for offset in nearest:
        along_z[offset].wait_recv()
        zs = lax.rem(z + nz - offset, nz)
        to_right[offset] = remote(dst_ref.at[y, zs], dst_ref.at[y, zs], r_sem + offset, right, z)
        to_left[offset] = remote(dst_ref.at[y, zs], dst_ref.at[y, zs], l_sem + offset, left, z)
        relay(before)
        before = offset
    relay(before)
    local.wait()
    for copy in list(along_z.values()) + list(to_right.values()) + list(to_left.values()):
        copy.wait_send()
    for copy in relays:
        copy.wait()


def gather2d(src, collective_id):
    nz = lax.axis_size("bz")
    return pl.pallas_call(
        functools.partial(gather2d_kernel, nz),
        out_shape=jax.ShapeDtypeStruct((4, nz) + tuple(src.shape), src.dtype),
        in_specs=[pl.BlockSpec(memory_space=pl.ANY)],
        out_specs=pl.BlockSpec(memory_space=pl.ANY),
        scratch_shapes=[
            pltpu.SemaphoreType.DMA((5 * nz,)),
            pltpu.SemaphoreType.DMA((5 * nz,)),
            pltpu.SemaphoreType.DMA,
        ],
        compiler_params=pltpu.CompilerParams(collective_id=collective_id, has_side_effects=True),
    )(src)


def exchange(src, axis, gather, collective_id):
    n = lax.axis_size(axis)
    block = src.shape if gather else src.shape[1:]
    return pl.pallas_call(
        functools.partial(exchange_kernel, n, axis, gather),
        out_shape=jax.ShapeDtypeStruct((n,) + tuple(block), src.dtype),
        in_specs=[pl.BlockSpec(memory_space=pl.ANY)],
        out_specs=pl.BlockSpec(memory_space=pl.ANY),
        scratch_shapes=[
            pltpu.SemaphoreType.DMA((n,)),
            pltpu.SemaphoreType.DMA((n,)),
            pltpu.SemaphoreType.DMA,
        ],
        compiler_params=pltpu.CompilerParams(collective_id=collective_id, has_side_effects=True),
    )(src)


def convolve(edge_cells, fresh_cells, kernel, edge_mask):
    sequence = jnp.concatenate(
        [edge_cells * edge_mask[:, :, None].astype(edge_cells.dtype), fresh_cells], 1
    ).astype(jnp.float32)
    steps_count = fresh_cells.shape[1]
    summed = kernel[0] * sequence[:, 0:steps_count]
    for offset in range(1, kernel.shape[0]):
        summed = summed + kernel[offset] * sequence[:, offset : offset + steps_count]
    return jax.nn.silu(summed).astype(jnp.bfloat16)


def split_dot(spec, wide, narrow):
    high = wide.astype(jnp.bfloat16)
    low = (wide - high.astype(jnp.float32)).astype(jnp.bfloat16)
    return jnp.einsum(spec, high, narrow, preferred_element_type=jnp.float32) + jnp.einsum(
        spec, low, narrow, preferred_element_type=jnp.float32
    )


def shards(
    hidden_in,
    w_z,
    w_x,
    w_bc,
    w_dt,
    conv_x,
    conv_bc,
    dt_bias,
    a_log,
    d_skip,
    norm_gain,
    w_out,
    edge_x,
    edge_bc,
    pool,
    tenant_sizes,
    owner,
    accepted,
    prompt_len,
):
    highest = lax.Precision.HIGHEST
    rows_in = hidden_in[0]
    local_rows = rows_in.shape[0]
    n_req = edge_x.shape[0]
    drafts = local_rows * lax.axis_size(BLK) // n_req
    state_dim = w_bc.shape[1] // 2
    heads_here = w_dt.shape[1]
    inner_here = w_z.shape[1]
    head_dim = inner_here // heads_here
    slots_here = pool.shape[0]
    cap_group = slots_here // lax.axis_size("rep")
    weights_in = (w_z, w_x, w_dt, w_bc)
    n_blk = lax.axis_size(BLK)
    block_rows = gather2d(rows_in, 0).reshape(n_blk * local_rows, rows_in.shape[1])
    projected = jnp.concatenate(
        [
            jnp.dot(block_rows, weight_cols, preferred_element_type=jnp.float32)
            for weight_cols in weights_in
        ],
        1,
    ).astype(jnp.bfloat16)
    z_all = projected[:, :inner_here]
    u_all = projected[:, inner_here : 2 * inner_here]
    dt_raw = projected[:, 2 * inner_here : 2 * inner_here + heads_here]
    bc_all = projected[:, 2 * inner_here + heads_here :]
    edge_len = edge_x.shape[1]
    edge_mask = prompt_len[:, None] >= (edge_len - jnp.arange(edge_len, dtype=jnp.int32))[None, :]
    x_conv = convolve(edge_x, u_all.reshape(n_req, drafts, inner_here), conv_x, edge_mask)
    bc_conv = convolve(edge_bc, bc_all.reshape(n_req, drafts, 2 * state_dim), conv_bc, edge_mask)
    b_half = bc_conv[:, :, :state_dim]
    c_half = bc_conv[:, :, state_dim:]
    b_float = b_half.astype(jnp.float32)
    c_float = c_half.astype(jnp.float32)
    x_heads = x_conv.reshape(n_req, drafts, heads_here, head_dim).astype(jnp.float32)
    req_index = lax.axis_index("rep") * n_req + jnp.arange(n_req, dtype=jnp.int32)
    tenant_ends = jnp.cumsum(tenant_sizes)
    tenant_id = jnp.sum((req_index[:, None] >= tenant_ends[None, :-1]).astype(jnp.int32), axis=1)
    tenant_pick = (
        tenant_id[:, None] == jnp.arange(tenant_sizes.shape[0], dtype=jnp.int32)[None, :]
    ).astype(jnp.float32)
    bias_req = jnp.dot(tenant_pick, dt_bias, precision=highest)
    step_size = jax.nn.softplus(
        dt_raw.reshape(n_req, drafts, heads_here).astype(jnp.float32) + bias_req[:, None, :]
    )
    log_decay = jnp.cumsum(step_size * (-jnp.exp(a_log))[None, None, :], axis=1)
    draft_index = jnp.arange(drafts, dtype=jnp.int32)
    causal = draft_index[:, None] >= draft_index[None, :]
    scores = jnp.einsum("rtn,rsn->rts", c_half, b_half, preferred_element_type=jnp.float32)
    log_gap = log_decay[:, :, None, :] - log_decay[:, None, :, :]
    weight = (
        jnp.where(causal[None, :, :, None], jnp.exp(jnp.minimum(log_gap, 0.0)), 0.0)
        * step_size[:, None, :, :]
        * scores[:, :, :, None]
    )
    y_local = (
        split_dot("rtsh,rshp->rthp", weight, x_conv.reshape(n_req, drafts, heads_here, head_dim))
        + d_skip[None, None, :, None] * x_heads
    )
    pick_last = (draft_index[None, :] == accepted[:, None] - 1).astype(jnp.float32)
    log_accept = jnp.sum(pick_last[:, :, None] * log_decay, axis=1)
    keep_draft = draft_index[None, :] < accepted[:, None]
    coef = (
        jnp.where(
            keep_draft[:, :, None],
            jnp.exp(jnp.minimum(log_accept[:, None, :] - log_decay, 0.0)),
            0.0,
        )
        * step_size
    )
    carry_decay = jnp.exp(log_accept)
    decay_now = jnp.exp(log_decay)
    owner_of = owner[:, 0]
    local_index = jnp.arange(n_req, dtype=jnp.int32)
    earlier = (owner_of[None, :] == owner_of[:, None]) & (
        local_index[None, :] < local_index[:, None]
    )
    rank_within = jnp.sum(earlier.astype(jnp.int32), axis=1)
    slot_index = owner_of * cap_group + rank_within
    fetched_half = lax.all_to_all(
        pool.astype(jnp.bfloat16), "rep", split_axis=0, concat_axis=0, tiled=True
    )
    fetched = fetched_half.astype(pool.dtype)
    slots = jnp.arange(slots_here, dtype=jnp.int32)
    slot_pick = (slots[:, None] == slot_index[None, :]).astype(jnp.int32)
    slot_used = jnp.sum(slot_pick, axis=1) > 0
    slot_req = jnp.sum(slot_pick * local_index[None, :], axis=1)

    def to_slots(per_req):
        taken = jnp.take(per_req, slot_req, axis=0)
        return jnp.where(slot_used.reshape((-1,) + (1,) * (per_req.ndim - 1)), taken, 0.0)

    prior_slot = to_slots(decay_now)[:, :, :, None] * jnp.einsum(
        "jhpn,jtn->jthp", fetched_half, to_slots(c_half), preferred_element_type=jnp.float32
    )
    y_prior = jnp.take(prior_slot, slot_index, axis=0)
    buffer = to_slots(carry_decay)[:, :, None, None] * fetched + split_dot(
        "jshp,jsn->jhpn", to_slots(coef[:, :, :, None] * x_heads), to_slots(b_half)
    )
    new_pool = lax.all_to_all(
        buffer.astype(jnp.bfloat16), "rep", split_axis=0, concat_axis=0, tiled=True
    ).astype(buffer.dtype)
    y_total = (y_local + y_prior).reshape(n_req * drafts, inner_here)
    gated = y_total * jax.nn.silu(z_all.astype(jnp.float32))
    sq_part = jnp.sum(gated * gated, axis=1)
    sq_hi = sq_part.astype(jnp.bfloat16)
    sq_lo = (sq_part - sq_hi.astype(jnp.float32)).astype(jnp.bfloat16)
    scaled = (gated * norm_gain[None, :]).astype(jnp.bfloat16)
    partial = jnp.dot(scaled, w_out, preferred_element_type=jnp.float32).astype(jnp.bfloat16)
    width = partial.shape[1]
    extra = jnp.zeros((partial.shape[0], 128), jnp.bfloat16)
    extra = extra.at[:, 0].set(sq_hi).at[:, 1].set(sq_lo)
    n_y = lax.axis_size("by")
    packed = jnp.concatenate([partial, extra], 1).reshape(n_y, n_blk // n_y, local_rows, width + 128)
    half_sum = jnp.sum(exchange4(packed, "by", False, 2).astype(jnp.float32), axis=0)
    sq_mid = half_sum[:, :, width] + half_sum[:, :, width + 1]
    sq_mid_hi = sq_mid.astype(jnp.bfloat16)
    sq_mid_lo = (sq_mid - sq_mid_hi.astype(jnp.float32)).astype(jnp.bfloat16)
    half_packed = (
        half_sum.astype(jnp.bfloat16).at[:, :, width].set(sq_mid_hi).at[:, :, width + 1].set(sq_mid_lo)
    )
    summed = jnp.sum(exchange(half_packed, "bz", False, 3).astype(jnp.float32), axis=0)
    inner_all = inner_here * n_blk
    mean_sq = (summed[:, width] + summed[:, width + 1]) / inner_all
    mixed = (summed[:, :width] * lax.rsqrt(mean_sq + 1e-05)[:, None]).astype(jnp.bfloat16)
    return (mixed[None], new_pool)


def solution(mesh):
    placed = (
        P("rep", "blk", None),
        P(None, "blk"),
        P(None, "blk"),
        P(),
        P(None, "blk"),
        P(None, "blk"),
        P(),
        P(None, "blk"),
        P("blk"),
        P("blk"),
        P("blk"),
        P("blk", None),
        P("rep", None, "blk"),
        P("rep", None, None),
        P("rep", "blk", None, None),
        P(),
        P("rep", None),
        P("rep"),
        P("rep"),
    )
    n_blk, n_rep = mesh.shape["blk"], mesh.shape["rep"]
    split_mesh = jax.sharding.Mesh(
        mesh.devices.reshape(Y_CHIPS, n_blk // Y_CHIPS, n_rep), AXES
    )
    placed = tuple(P(*[BLK if part == "blk" else part for part in spec]) for spec in placed)
    return jax.shard_map(
        shards,
        mesh=split_mesh,
        in_specs=placed,
        out_specs=(P("rep", BLK, None), P("rep", BLK, None, None)),
        check_vma=False,
    )
```

```python
import functools

import jax
import jax.numpy as jnp
from jax import lax
from jax.experimental import pallas as pl
from jax.experimental.pallas import tpu as pltpu
from jax.sharding import PartitionSpec as P

MESH = pl.DeviceIdType.MESH
AXES = ("by", "bz", "rep")
BLK = ("by", "bz")
Y_CHIPS = 4


def exchange_kernel(n, axis, gather, src_ref, dst_ref, send_sem, recv_sem, local_sem):
    me = lax.axis_index(axis)
    coords = {name: lax.axis_index(name) for name in AXES}

    def device_of(peer):
        return tuple(peer if name == axis else coords[name] for name in AXES)

    barrier = pltpu.get_barrier_semaphore()
    for offset in range(1, n):
        peer = lax.rem(me + offset, n)
        pl.semaphore_signal(barrier, inc=1, device_id=device_of(peer), device_id_type=MESH)
    pl.semaphore_wait(barrier, n - 1)
    local = pltpu.make_async_copy(src_ref if gather else src_ref.at[me], dst_ref.at[me], local_sem)
    local.start()
    copies = []
    for offset in sorted(range(1, n), key=lambda offset: (min(offset, n - offset), offset)):
        peer = lax.rem(me + offset, n)
        copy = pltpu.make_async_remote_copy(
            src_ref=src_ref if gather else src_ref.at[peer],
            dst_ref=dst_ref.at[me],
            send_sem=send_sem.at[offset],
            recv_sem=recv_sem.at[offset],
            device_id=device_of(peer),
            device_id_type=MESH,
        )
        copy.start()
        copies.append(copy)
    local.wait()
    for copy in copies:
        copy.wait()


def ring4_kernel(axis, gather, src_ref, dst_ref, stage_ref, send_sem, recv_sem, local_sem):
    me = lax.axis_index(axis)
    coords = {name: lax.axis_index(name) for name in AXES}

    def device_of(peer):
        return tuple(peer if name == axis else coords[name] for name in AXES)

    right, left = lax.rem(me + 1, 4), lax.rem(me + 3, 4)
    opposite = lax.rem(me + 2, 4)
    half = dst_ref.shape[1] // 2
    first, second = pl.ds(0, half), pl.ds(half, half)

    def remote(src, dst, index, peer):
        copy = pltpu.make_async_remote_copy(
            src_ref=src,
            dst_ref=dst,
            send_sem=send_sem.at[index],
            recv_sem=recv_sem.at[index],
            device_id=device_of(peer),
            device_id_type=MESH,
        )
        copy.start()
        return copy

    barrier = pltpu.get_barrier_semaphore()
    for peer in (left, right):
        pl.semaphore_signal(barrier, inc=1, device_id=device_of(peer), device_id_type=MESH)
    pl.semaphore_wait(barrier, 2)
    if not gather:
        stage_right = remote(src_ref.at[opposite, first], stage_ref.at[0], 2, right)
        stage_left = remote(src_ref.at[opposite, second], stage_ref.at[1], 3, left)
    local = pltpu.make_async_copy(src_ref if gather else src_ref.at[me], dst_ref.at[me], local_sem)
    local.start()
    to_right = remote(src_ref if gather else src_ref.at[right], dst_ref.at[me], 0, right)
    to_left = remote(src_ref if gather else src_ref.at[left], dst_ref.at[me], 1, left)
    if gather:
        to_right.wait_recv()
        pass_right = remote(dst_ref.at[left, first], dst_ref.at[left, first], 2, right)
        to_left.wait_recv()
        pass_left = remote(dst_ref.at[right, second], dst_ref.at[right, second], 3, left)
        to_right.wait_send()
        to_left.wait_send()
    else:
        stage_right.wait_recv()
        pass_right = remote(stage_ref.at[0], dst_ref.at[left, first], 4, right)
        stage_left.wait_recv()
        pass_left = remote(stage_ref.at[1], dst_ref.at[right, second], 5, left)
        stage_right.wait_send()
        stage_left.wait_send()
        to_right.wait()
        to_left.wait()
    local.wait()
    pass_right.wait()
    pass_left.wait()


def exchange4(src, axis, gather, collective_id):
    block = src.shape if gather else src.shape[1:]
    out = jax.ShapeDtypeStruct((4,) + tuple(block), src.dtype)
    stage = jax.ShapeDtypeStruct((2, block[0] // 2) + tuple(block[1:]), src.dtype)
    return pl.pallas_call(
        functools.partial(ring4_kernel, axis, gather),
        out_shape=(out, stage),
        in_specs=[pl.BlockSpec(memory_space=pl.ANY)],
        out_specs=(pl.BlockSpec(memory_space=pl.ANY), pl.BlockSpec(memory_space=pl.ANY)),
        scratch_shapes=[
            pltpu.SemaphoreType.DMA((6,)),
            pltpu.SemaphoreType.DMA((6,)),
            pltpu.SemaphoreType.DMA,
        ],
        compiler_params=pltpu.CompilerParams(collective_id=collective_id, has_side_effects=True),
    )(src)[0]


def gather2d_kernel(nz, src_ref, dst_ref, send_sem, recv_sem, local_sem):
    y, z = lax.axis_index("by"), lax.axis_index("bz")
    rep = lax.axis_index("rep")
    right, left = lax.rem(y + 1, 4), lax.rem(y + 3, 4)
    half = src_ref.shape[0] // 2
    first, second = pl.ds(0, half), pl.ds(half, half)
    z_sem, r_sem, l_sem, ra_sem, lb_sem = 0, nz, 2 * nz, 3 * nz, 4 * nz

    def remote(src, dst, index, yy, zz):
        copy = pltpu.make_async_remote_copy(
            src_ref=src,
            dst_ref=dst,
            send_sem=send_sem.at[index],
            recv_sem=recv_sem.at[index],
            device_id=(yy, zz, rep),
            device_id_type=MESH,
        )
        copy.start()
        return copy

    barrier = pltpu.get_barrier_semaphore()
    for offset in range(1, nz):
        pl.semaphore_signal(
            barrier, inc=1, device_id=(y, lax.rem(z + offset, nz), rep), device_id_type=MESH
        )
    for yy in (left, right):
        pl.semaphore_signal(barrier, inc=1, device_id=(yy, z, rep), device_id_type=MESH)
    pl.semaphore_wait(barrier, nz + 1)
    local = pltpu.make_async_copy(src_ref, dst_ref.at[y, z], local_sem)
    local.start()
    to_right = [remote(src_ref, dst_ref.at[y, z], r_sem, right, z)]
    to_left = [remote(src_ref, dst_ref.at[y, z], l_sem, left, z)]
    nearest = sorted(range(1, nz), key=lambda offset: (min(offset, nz - offset), offset))
    along_z = {}
    for offset in nearest:
        along_z[offset] = remote(src_ref, dst_ref.at[y, z], z_sem + offset, y, lax.rem(z + offset, nz))
    relays = []

    def relay(offset):
        zs = lax.rem(z + nz - offset, nz)
        to_right[offset].wait_recv()
        relays.append(
            remote(dst_ref.at[left, zs, first], dst_ref.at[left, zs, first], ra_sem + offset, right, z)
        )
        to_left[offset].wait_recv()
        relays.append(
            remote(dst_ref.at[right, zs, second], dst_ref.at[right, zs, second], lb_sem + offset, left, z)
        )

    to_right, to_left = {0: to_right[0]}, {0: to_left[0]}
    before = 0
    for offset in nearest:
        along_z[offset].wait_recv()
        zs = lax.rem(z + nz - offset, nz)
        to_right[offset] = remote(dst_ref.at[y, zs], dst_ref.at[y, zs], r_sem + offset, right, z)
        to_left[offset] = remote(dst_ref.at[y, zs], dst_ref.at[y, zs], l_sem + offset, left, z)
        relay(before)
        before = offset
    relay(before)
    local.wait()
    for copy in list(along_z.values()) + list(to_right.values()) + list(to_left.values()):
        copy.wait_send()
    for copy in relays:
        copy.wait()


def gather2d(src, collective_id):
    nz = lax.axis_size("bz")
    return pl.pallas_call(
        functools.partial(gather2d_kernel, nz),
        out_shape=jax.ShapeDtypeStruct((4, nz) + tuple(src.shape), src.dtype),
        in_specs=[pl.BlockSpec(memory_space=pl.ANY)],
        out_specs=pl.BlockSpec(memory_space=pl.ANY),
        scratch_shapes=[
            pltpu.SemaphoreType.DMA((5 * nz,)),
            pltpu.SemaphoreType.DMA((5 * nz,)),
            pltpu.SemaphoreType.DMA,
        ],
        compiler_params=pltpu.CompilerParams(collective_id=collective_id, has_side_effects=True),
    )(src)


def exchange(src, axis, gather, collective_id):
    n = lax.axis_size(axis)
    block = src.shape if gather else src.shape[1:]
    return pl.pallas_call(
        functools.partial(exchange_kernel, n, axis, gather),
        out_shape=jax.ShapeDtypeStruct((n,) + tuple(block), src.dtype),
        in_specs=[pl.BlockSpec(memory_space=pl.ANY)],
        out_specs=pl.BlockSpec(memory_space=pl.ANY),
        scratch_shapes=[
            pltpu.SemaphoreType.DMA((n,)),
            pltpu.SemaphoreType.DMA((n,)),
            pltpu.SemaphoreType.DMA,
        ],
        compiler_params=pltpu.CompilerParams(collective_id=collective_id, has_side_effects=True),
    )(src)


def convolve(edge_cells, fresh_cells, kernel, edge_mask):
    sequence = jnp.concatenate(
        [edge_cells * edge_mask[:, :, None].astype(edge_cells.dtype), fresh_cells], 1
    ).astype(jnp.float32)
    steps_count = fresh_cells.shape[1]
    summed = kernel[0] * sequence[:, 0:steps_count]
    for offset in range(1, kernel.shape[0]):
        summed = summed + kernel[offset] * sequence[:, offset : offset + steps_count]
    return jax.nn.silu(summed).astype(jnp.bfloat16)


def split_dot(spec, wide, narrow):
    high = wide.astype(jnp.bfloat16)
    low = (wide - high.astype(jnp.float32)).astype(jnp.bfloat16)
    return jnp.einsum(spec, high, narrow, preferred_element_type=jnp.float32) + jnp.einsum(
        spec, low, narrow, preferred_element_type=jnp.float32
    )


def shards(
    hidden_in,
    w_z,
    w_x,
    w_bc,
    w_dt,
    conv_x,
    conv_bc,
    dt_bias,
    a_log,
    d_skip,
    norm_gain,
    w_out,
    edge_x,
    edge_bc,
    pool,
    tenant_sizes,
    owner,
    accepted,
    prompt_len,
):
    highest = lax.Precision.HIGHEST
    rows_in = hidden_in[0]
    local_rows = rows_in.shape[0]
    n_req = edge_x.shape[0]
    drafts = local_rows * lax.axis_size(BLK) // n_req
    state_dim = w_bc.shape[1] // 2
    heads_here = w_dt.shape[1]
    inner_here = w_z.shape[1]
    head_dim = inner_here // heads_here
    slots_here = pool.shape[0]
    cap_group = slots_here // lax.axis_size("rep")
    weights_in = (w_z, w_x, w_dt, w_bc)
    n_blk = lax.axis_size(BLK)
    block_rows = gather2d(rows_in, 0).reshape(n_blk * local_rows, rows_in.shape[1])
    projected = jnp.concatenate(
        [
            jnp.dot(block_rows, weight_cols, preferred_element_type=jnp.float32)
            for weight_cols in weights_in
        ],
        1,
    ).astype(jnp.bfloat16)
    z_all = projected[:, :inner_here]
    u_all = projected[:, inner_here : 2 * inner_here]
    dt_raw = projected[:, 2 * inner_here : 2 * inner_here + heads_here]
    bc_all = projected[:, 2 * inner_here + heads_here :]
    edge_len = edge_x.shape[1]
    edge_mask = prompt_len[:, None] >= (edge_len - jnp.arange(edge_len, dtype=jnp.int32))[None, :]
    x_conv = convolve(edge_x, u_all.reshape(n_req, drafts, inner_here), conv_x, edge_mask)
    bc_conv = convolve(edge_bc, bc_all.reshape(n_req, drafts, 2 * state_dim), conv_bc, edge_mask)
    b_half = bc_conv[:, :, :state_dim]
    c_half = bc_conv[:, :, state_dim:]
    b_float = b_half.astype(jnp.float32)
    c_float = c_half.astype(jnp.float32)
    x_heads = x_conv.reshape(n_req, drafts, heads_here, head_dim).astype(jnp.float32)
    req_index = lax.axis_index("rep") * n_req + jnp.arange(n_req, dtype=jnp.int32)
    tenant_ends = jnp.cumsum(tenant_sizes)
    tenant_id = jnp.sum((req_index[:, None] >= tenant_ends[None, :-1]).astype(jnp.int32), axis=1)
    tenant_pick = (
        tenant_id[:, None] == jnp.arange(tenant_sizes.shape[0], dtype=jnp.int32)[None, :]
    ).astype(jnp.float32)
    bias_req = jnp.dot(tenant_pick, dt_bias, precision=highest)
    step_size = jax.nn.softplus(
        dt_raw.reshape(n_req, drafts, heads_here).astype(jnp.float32) + bias_req[:, None, :]
    )
    log_decay = jnp.cumsum(step_size * (-jnp.exp(a_log))[None, None, :], axis=1)
    draft_index = jnp.arange(drafts, dtype=jnp.int32)
    causal = draft_index[:, None] >= draft_index[None, :]
    scores = jnp.einsum("rtn,rsn->rts", c_half, b_half, preferred_element_type=jnp.float32)
    log_gap = log_decay[:, :, None, :] - log_decay[:, None, :, :]
    weight = (
        jnp.where(causal[None, :, :, None], jnp.exp(jnp.minimum(log_gap, 0.0)), 0.0)
        * step_size[:, None, :, :]
        * scores[:, :, :, None]
    )
    y_local = (
        split_dot("rtsh,rshp->rthp", weight, x_conv.reshape(n_req, drafts, heads_here, head_dim))
        + d_skip[None, None, :, None] * x_heads
    )
    pick_last = (draft_index[None, :] == accepted[:, None] - 1).astype(jnp.float32)
    log_accept = jnp.sum(pick_last[:, :, None] * log_decay, axis=1)
    keep_draft = draft_index[None, :] < accepted[:, None]
    coef = (
        jnp.where(
            keep_draft[:, :, None],
            jnp.exp(jnp.minimum(log_accept[:, None, :] - log_decay, 0.0)),
            0.0,
        )
        * step_size
    )
    carry_decay = jnp.exp(log_accept)
    decay_now = jnp.exp(log_decay)
    owner_of = owner[:, 0]
    local_index = jnp.arange(n_req, dtype=jnp.int32)
    earlier = (owner_of[None, :] == owner_of[:, None]) & (
        local_index[None, :] < local_index[:, None]
    )
    rank_within = jnp.sum(earlier.astype(jnp.int32), axis=1)
    slot_index = owner_of * cap_group + rank_within
    fetched_half = lax.all_to_all(
        pool.astype(jnp.bfloat16), "rep", split_axis=0, concat_axis=0, tiled=True
    )
    fetched = fetched_half.astype(pool.dtype)
    slots = jnp.arange(slots_here, dtype=jnp.int32)
    slot_pick = (slots[:, None] == slot_index[None, :]).astype(jnp.int32)
    slot_used = jnp.sum(slot_pick, axis=1) > 0
    slot_req = jnp.sum(slot_pick * local_index[None, :], axis=1)

    def to_slots(per_req):
        taken = jnp.take(per_req, slot_req, axis=0)
        return jnp.where(slot_used.reshape((-1,) + (1,) * (per_req.ndim - 1)), taken, 0.0)

    prior_slot = to_slots(decay_now)[:, :, :, None] * jnp.einsum(
        "jhpn,jtn->jthp", fetched_half, to_slots(c_half), preferred_element_type=jnp.float32
    )
    y_prior = jnp.take(prior_slot, slot_index, axis=0)
    buffer = to_slots(carry_decay)[:, :, None, None] * fetched + split_dot(
        "jshp,jsn->jhpn", to_slots(coef[:, :, :, None] * x_heads), to_slots(b_half)
    )
    new_pool = lax.all_to_all(
        buffer.astype(jnp.bfloat16), "rep", split_axis=0, concat_axis=0, tiled=True
    ).astype(buffer.dtype)
    y_total = (y_local + y_prior).reshape(n_req * drafts, inner_here)
    gated = y_total * jax.nn.silu(z_all.astype(jnp.float32))
    sq_part = jnp.sum(gated * gated, axis=1)
    sq_hi = sq_part.astype(jnp.bfloat16)
    sq_lo = (sq_part - sq_hi.astype(jnp.float32)).astype(jnp.bfloat16)
    scaled = (gated * norm_gain[None, :]).astype(jnp.bfloat16)
    partial = jnp.dot(scaled, w_out, preferred_element_type=jnp.float32).astype(jnp.bfloat16)
    width = partial.shape[1]
    extra = jnp.zeros((partial.shape[0], 128), jnp.bfloat16)
    extra = extra.at[:, 0].set(sq_hi).at[:, 1].set(sq_lo)
    n_y = lax.axis_size("by")
    packed = jnp.concatenate([partial, extra], 1).reshape(n_y, n_blk // n_y, local_rows, width + 128)
    half_sum = jnp.sum(exchange4(packed, "by", False, 2).astype(jnp.float32), axis=0)
    sq_mid = half_sum[:, :, width] + half_sum[:, :, width + 1]
    sq_mid_hi = sq_mid.astype(jnp.bfloat16)
    sq_mid_lo = (sq_mid - sq_mid_hi.astype(jnp.float32)).astype(jnp.bfloat16)
    half_packed = (
        half_sum.astype(jnp.bfloat16).at[:, :, width].set(sq_mid_hi).at[:, :, width + 1].set(sq_mid_lo)
    )
    summed = jnp.sum(exchange(half_packed, "bz", False, 3).astype(jnp.float32), axis=0)
    inner_all = inner_here * n_blk
    mean_sq = (summed[:, width] + summed[:, width + 1]) / inner_all
    mixed = (summed[:, :width] * lax.rsqrt(mean_sq + 1e-05)[:, None]).astype(jnp.bfloat16)
    return (mixed[None], new_pool)


def solution(mesh):
    placed = (
        P("rep", "blk", None),
        P(None, "blk"),
        P(None, "blk"),
        P(),
        P(None, "blk"),
        P(None, "blk"),
        P(),
        P(None, "blk"),
        P("blk"),
        P("blk"),
        P("blk"),
        P("blk", None),
        P("rep", None, "blk"),
        P("rep", None, None),
        P("rep", "blk", None, None),
        P(),
        P("rep", None),
        P("rep"),
        P("rep"),
    )
    n_blk, n_rep = mesh.shape["blk"], mesh.shape["rep"]
    split_mesh = jax.sharding.Mesh(
        mesh.devices.reshape(Y_CHIPS, n_blk // Y_CHIPS, n_rep), AXES
    )
    placed = tuple(P(*[BLK if part == "blk" else part for part in spec]) for spec in placed)
    return jax.shard_map(
        shards,
        mesh=split_mesh,
        in_specs=placed,
        out_specs=(P("rep", BLK, None), P("rep", BLK, None, None)),
        check_vma=False,
    )
```

```python
import functools

import jax
import jax.numpy as jnp
from jax import lax
from jax.experimental import pallas as pl
from jax.experimental.pallas import tpu as pltpu
from jax.sharding import PartitionSpec as P

MESH = pl.DeviceIdType.MESH
AXES = ("by", "bz", "rep")
BLK = ("by", "bz")
Y_CHIPS = 4


def exchange_kernel(n, axis, gather, src_ref, dst_ref, stage_ref, send_sem, recv_sem, local_sem):
    me = lax.axis_index(axis)
    coords = {name: lax.axis_index(name) for name in AXES}
    far = n // 2 if (not gather and n >= 4 and n % 2 == 0) else 0
    half = dst_ref.shape[1] // 2
    first, second = pl.ds(0, half), pl.ds(half, half)

    def device_of(peer):
        return tuple(peer if name == axis else coords[name] for name in AXES)

    def remote(src, dst, index, peer):
        copy = pltpu.make_async_remote_copy(
            src_ref=src,
            dst_ref=dst,
            send_sem=send_sem.at[index],
            recv_sem=recv_sem.at[index],
            device_id=device_of(peer),
            device_id_type=MESH,
        )
        copy.start()
        return copy

    barrier = pltpu.get_barrier_semaphore()
    for offset in range(1, n):
        peer = lax.rem(me + offset, n)
        pl.semaphore_signal(barrier, inc=1, device_id=device_of(peer), device_id_type=MESH)
    pl.semaphore_wait(barrier, n - 1)
    if far:
        left = lax.rem(me + n - 1, n)
        staged = remote(src_ref.at[lax.rem(me + far, n), second], stage_ref, n, left)
    local = pltpu.make_async_copy(src_ref if gather else src_ref.at[me], dst_ref.at[me], local_sem)
    local.start()
    copies = []
    for offset in sorted(range(1, n), key=lambda offset: (min(offset, n - offset), offset)):
        peer = lax.rem(me + offset, n)
        if offset == far:
            copies.append(remote(src_ref.at[peer, first], dst_ref.at[me, first], offset, peer))
        else:
            copies.append(remote(src_ref if gather else src_ref.at[peer], dst_ref.at[me], offset, peer))
    if far:
        staged.wait_recv()
        origin = lax.rem(me + 1, n)
        copies.append(
            remote(stage_ref, dst_ref.at[origin, second], n + 1, lax.rem(origin + far, n))
        )
        staged.wait_send()
    local.wait()
    for copy in copies:
        copy.wait()


def ring4_kernel(axis, gather, src_ref, dst_ref, stage_ref, send_sem, recv_sem, local_sem):
    me = lax.axis_index(axis)
    coords = {name: lax.axis_index(name) for name in AXES}

    def device_of(peer):
        return tuple(peer if name == axis else coords[name] for name in AXES)

    right, left = lax.rem(me + 1, 4), lax.rem(me + 3, 4)
    opposite = lax.rem(me + 2, 4)
    half = dst_ref.shape[1] // 2
    first, second = pl.ds(0, half), pl.ds(half, half)

    def remote(src, dst, index, peer):
        copy = pltpu.make_async_remote_copy(
            src_ref=src,
            dst_ref=dst,
            send_sem=send_sem.at[index],
            recv_sem=recv_sem.at[index],
            device_id=device_of(peer),
            device_id_type=MESH,
        )
        copy.start()
        return copy

    barrier = pltpu.get_barrier_semaphore()
    for peer in (left, right):
        pl.semaphore_signal(barrier, inc=1, device_id=device_of(peer), device_id_type=MESH)
    pl.semaphore_wait(barrier, 2)
    if not gather:
        stage_right = remote(src_ref.at[opposite, first], stage_ref.at[0], 2, right)
        stage_left = remote(src_ref.at[opposite, second], stage_ref.at[1], 3, left)
    local = pltpu.make_async_copy(src_ref if gather else src_ref.at[me], dst_ref.at[me], local_sem)
    local.start()
    to_right = remote(src_ref if gather else src_ref.at[right], dst_ref.at[me], 0, right)
    to_left = remote(src_ref if gather else src_ref.at[left], dst_ref.at[me], 1, left)
    if gather:
        to_right.wait_recv()
        pass_right = remote(dst_ref.at[left, first], dst_ref.at[left, first], 2, right)
        to_left.wait_recv()
        pass_left = remote(dst_ref.at[right, second], dst_ref.at[right, second], 3, left)
        to_right.wait_send()
        to_left.wait_send()
    else:
        stage_right.wait_recv()
        pass_right = remote(stage_ref.at[0], dst_ref.at[left, first], 4, right)
        stage_left.wait_recv()
        pass_left = remote(stage_ref.at[1], dst_ref.at[right, second], 5, left)
        stage_right.wait_send()
        stage_left.wait_send()
        to_right.wait()
        to_left.wait()
    local.wait()
    pass_right.wait()
    pass_left.wait()


def exchange4(src, axis, gather, collective_id):
    block = src.shape if gather else src.shape[1:]
    out = jax.ShapeDtypeStruct((4,) + tuple(block), src.dtype)
    stage = jax.ShapeDtypeStruct((2, block[0] // 2) + tuple(block[1:]), src.dtype)
    return pl.pallas_call(
        functools.partial(ring4_kernel, axis, gather),
        out_shape=(out, stage),
        in_specs=[pl.BlockSpec(memory_space=pl.ANY)],
        out_specs=(pl.BlockSpec(memory_space=pl.ANY), pl.BlockSpec(memory_space=pl.ANY)),
        scratch_shapes=[
            pltpu.SemaphoreType.DMA((6,)),
            pltpu.SemaphoreType.DMA((6,)),
            pltpu.SemaphoreType.DMA,
        ],
        compiler_params=pltpu.CompilerParams(collective_id=collective_id, has_side_effects=True),
    )(src)[0]


def gather2d_kernel(nz, src_ref, dst_ref, send_sem, recv_sem, local_sem):
    y, z = lax.axis_index("by"), lax.axis_index("bz")
    rep = lax.axis_index("rep")
    right, left = lax.rem(y + 1, 4), lax.rem(y + 3, 4)
    half = src_ref.shape[0] // 2
    first, second = pl.ds(0, half), pl.ds(half, half)
    z_sem, r_sem, l_sem, ra_sem, lb_sem = 0, nz, 2 * nz, 3 * nz, 4 * nz

    def remote(src, dst, index, yy, zz):
        copy = pltpu.make_async_remote_copy(
            src_ref=src,
            dst_ref=dst,
            send_sem=send_sem.at[index],
            recv_sem=recv_sem.at[index],
            device_id=(yy, zz, rep),
            device_id_type=MESH,
        )
        copy.start()
        return copy

    barrier = pltpu.get_barrier_semaphore()
    for offset in range(1, nz):
        pl.semaphore_signal(
            barrier, inc=1, device_id=(y, lax.rem(z + offset, nz), rep), device_id_type=MESH
        )
    for yy in (left, right):
        pl.semaphore_signal(barrier, inc=1, device_id=(yy, z, rep), device_id_type=MESH)
    pl.semaphore_wait(barrier, nz + 1)
    local = pltpu.make_async_copy(src_ref, dst_ref.at[y, z], local_sem)
    local.start()
    nearest = sorted(range(1, nz), key=lambda offset: (min(offset, nz - offset), offset))
    along_z = {}
    for offset in nearest:
        along_z[offset] = remote(src_ref, dst_ref.at[y, z], z_sem + offset, y, lax.rem(z + offset, nz))
    to_right = [remote(src_ref, dst_ref.at[y, z], r_sem, right, z)]
    to_left = [remote(src_ref, dst_ref.at[y, z], l_sem, left, z)]
    relays = []

    def relay(offset):
        zs = lax.rem(z + nz - offset, nz)
        to_right[offset].wait_recv()
        relays.append(
            remote(dst_ref.at[left, zs, first], dst_ref.at[left, zs, first], ra_sem + offset, right, z)
        )
        to_left[offset].wait_recv()
        relays.append(
            remote(dst_ref.at[right, zs, second], dst_ref.at[right, zs, second], lb_sem + offset, left, z)
        )

    to_right, to_left = {0: to_right[0]}, {0: to_left[0]}
    before = 0
    for offset in nearest:
        along_z[offset].wait_recv()
        zs = lax.rem(z + nz - offset, nz)
        to_right[offset] = remote(dst_ref.at[y, zs], dst_ref.at[y, zs], r_sem + offset, right, z)
        to_left[offset] = remote(dst_ref.at[y, zs], dst_ref.at[y, zs], l_sem + offset, left, z)
        relay(before)
        before = offset
    relay(before)
    local.wait()
    for copy in list(along_z.values()) + list(to_right.values()) + list(to_left.values()):
        copy.wait_send()
    for copy in relays:
        copy.wait()


def gather2d(src, collective_id):
    nz = lax.axis_size("bz")
    return pl.pallas_call(
        functools.partial(gather2d_kernel, nz),
        out_shape=jax.ShapeDtypeStruct((4, nz) + tuple(src.shape), src.dtype),
        in_specs=[pl.BlockSpec(memory_space=pl.ANY)],
        out_specs=pl.BlockSpec(memory_space=pl.ANY),
        scratch_shapes=[
            pltpu.SemaphoreType.DMA((5 * nz,)),
            pltpu.SemaphoreType.DMA((5 * nz,)),
            pltpu.SemaphoreType.DMA,
        ],
        compiler_params=pltpu.CompilerParams(collective_id=collective_id, has_side_effects=True),
    )(src)


def exchange(src, axis, gather, collective_id):
    n = lax.axis_size(axis)
    block = src.shape if gather else src.shape[1:]
    return pl.pallas_call(
        functools.partial(exchange_kernel, n, axis, gather),
        out_shape=(
            jax.ShapeDtypeStruct((n,) + tuple(block), src.dtype),
            jax.ShapeDtypeStruct((block[0] // 2,) + tuple(block[1:]), src.dtype),
        ),
        in_specs=[pl.BlockSpec(memory_space=pl.ANY)],
        out_specs=(pl.BlockSpec(memory_space=pl.ANY), pl.BlockSpec(memory_space=pl.ANY)),
        scratch_shapes=[
            pltpu.SemaphoreType.DMA((n + 2,)),
            pltpu.SemaphoreType.DMA((n + 2,)),
            pltpu.SemaphoreType.DMA,
        ],
        compiler_params=pltpu.CompilerParams(collective_id=collective_id, has_side_effects=True),
    )(src)[0]


def convolve(edge_cells, fresh_cells, kernel, edge_mask):
    sequence = jnp.concatenate(
        [edge_cells * edge_mask[:, :, None].astype(edge_cells.dtype), fresh_cells], 1
    ).astype(jnp.float32)
    steps_count = fresh_cells.shape[1]
    summed = kernel[0] * sequence[:, 0:steps_count]
    for offset in range(1, kernel.shape[0]):
        summed = summed + kernel[offset] * sequence[:, offset : offset + steps_count]
    return jax.nn.silu(summed).astype(jnp.bfloat16)


def split_dot(spec, wide, narrow):
    high = wide.astype(jnp.bfloat16)
    low = (wide - high.astype(jnp.float32)).astype(jnp.bfloat16)
    return jnp.einsum(spec, high, narrow, preferred_element_type=jnp.float32) + jnp.einsum(
        spec, low, narrow, preferred_element_type=jnp.float32
    )


def shards(
    hidden_in,
    w_z,
    w_x,
    w_bc,
    w_dt,
    conv_x,
    conv_bc,
    dt_bias,
    a_log,
    d_skip,
    norm_gain,
    w_out,
    edge_x,
    edge_bc,
    pool,
    tenant_sizes,
    owner,
    accepted,
    prompt_len,
):
    highest = lax.Precision.HIGHEST
    rows_in = hidden_in[0]
    local_rows = rows_in.shape[0]
    n_req = edge_x.shape[0]
    drafts = local_rows * lax.axis_size(BLK) // n_req
    state_dim = w_bc.shape[1] // 2
    heads_here = w_dt.shape[1]
    inner_here = w_z.shape[1]
    head_dim = inner_here // heads_here
    slots_here = pool.shape[0]
    cap_group = slots_here // lax.axis_size("rep")
    weights_in = (w_z, w_x, w_dt, w_bc)
    n_blk = lax.axis_size(BLK)
    block_rows = gather2d(rows_in, 0).reshape(n_blk * local_rows, rows_in.shape[1])
    projected = jnp.concatenate(
        [
            jnp.dot(block_rows, weight_cols, preferred_element_type=jnp.float32)
            for weight_cols in weights_in
        ],
        1,
    ).astype(jnp.bfloat16)
    z_all = projected[:, :inner_here]
    u_all = projected[:, inner_here : 2 * inner_here]
    dt_raw = projected[:, 2 * inner_here : 2 * inner_here + heads_here]
    bc_all = projected[:, 2 * inner_here + heads_here :]
    edge_len = edge_x.shape[1]
    edge_mask = prompt_len[:, None] >= (edge_len - jnp.arange(edge_len, dtype=jnp.int32))[None, :]
    x_conv = convolve(edge_x, u_all.reshape(n_req, drafts, inner_here), conv_x, edge_mask)
    bc_conv = convolve(edge_bc, bc_all.reshape(n_req, drafts, 2 * state_dim), conv_bc, edge_mask)
    b_half = bc_conv[:, :, :state_dim]
    c_half = bc_conv[:, :, state_dim:]
    b_float = b_half.astype(jnp.float32)
    c_float = c_half.astype(jnp.float32)
    x_heads = x_conv.reshape(n_req, drafts, heads_here, head_dim).astype(jnp.float32)
    req_index = lax.axis_index("rep") * n_req + jnp.arange(n_req, dtype=jnp.int32)
    tenant_ends = jnp.cumsum(tenant_sizes)
    tenant_id = jnp.sum((req_index[:, None] >= tenant_ends[None, :-1]).astype(jnp.int32), axis=1)
    tenant_pick = (
        tenant_id[:, None] == jnp.arange(tenant_sizes.shape[0], dtype=jnp.int32)[None, :]
    ).astype(jnp.float32)
    bias_req = jnp.dot(tenant_pick, dt_bias, precision=highest)
    step_size = jax.nn.softplus(
        dt_raw.reshape(n_req, drafts, heads_here).astype(jnp.float32) + bias_req[:, None, :]
    )
    log_decay = jnp.cumsum(step_size * (-jnp.exp(a_log))[None, None, :], axis=1)
    draft_index = jnp.arange(drafts, dtype=jnp.int32)
    causal = draft_index[:, None] >= draft_index[None, :]
    scores = jnp.einsum("rtn,rsn->rts", c_half, b_half, preferred_element_type=jnp.float32)
    log_gap = log_decay[:, :, None, :] - log_decay[:, None, :, :]
    weight = (
        jnp.where(causal[None, :, :, None], jnp.exp(jnp.minimum(log_gap, 0.0)), 0.0)
        * step_size[:, None, :, :]
        * scores[:, :, :, None]
    )
    y_local = (
        split_dot("rtsh,rshp->rthp", weight, x_conv.reshape(n_req, drafts, heads_here, head_dim))
        + d_skip[None, None, :, None] * x_heads
    )
    pick_last = (draft_index[None, :] == accepted[:, None] - 1).astype(jnp.float32)
    log_accept = jnp.sum(pick_last[:, :, None] * log_decay, axis=1)
    keep_draft = draft_index[None, :] < accepted[:, None]
    coef = (
        jnp.where(
            keep_draft[:, :, None],
            jnp.exp(jnp.minimum(log_accept[:, None, :] - log_decay, 0.0)),
            0.0,
        )
        * step_size
    )
    carry_decay = jnp.exp(log_accept)
    decay_now = jnp.exp(log_decay)
    owner_of = owner[:, 0]
    local_index = jnp.arange(n_req, dtype=jnp.int32)
    earlier = (owner_of[None, :] == owner_of[:, None]) & (
        local_index[None, :] < local_index[:, None]
    )
    rank_within = jnp.sum(earlier.astype(jnp.int32), axis=1)
    slot_index = owner_of * cap_group + rank_within
    fetched_half = lax.all_to_all(
        pool.astype(jnp.bfloat16), "rep", split_axis=0, concat_axis=0, tiled=True
    )
    fetched = fetched_half.astype(pool.dtype)
    slots = jnp.arange(slots_here, dtype=jnp.int32)
    slot_pick = (slots[:, None] == slot_index[None, :]).astype(jnp.int32)
    slot_used = jnp.sum(slot_pick, axis=1) > 0
    slot_req = jnp.sum(slot_pick * local_index[None, :], axis=1)

    def to_slots(per_req):
        taken = jnp.take(per_req, slot_req, axis=0)
        return jnp.where(slot_used.reshape((-1,) + (1,) * (per_req.ndim - 1)), taken, 0.0)

    prior_slot = to_slots(decay_now)[:, :, :, None] * jnp.einsum(
        "jhpn,jtn->jthp", fetched_half, to_slots(c_half), preferred_element_type=jnp.float32
    )
    y_prior = jnp.take(prior_slot, slot_index, axis=0)
    buffer = to_slots(carry_decay)[:, :, None, None] * fetched + split_dot(
        "jshp,jsn->jhpn", to_slots(coef[:, :, :, None] * x_heads), to_slots(b_half)
    )
    new_pool = lax.all_to_all(
        buffer.astype(jnp.bfloat16), "rep", split_axis=0, concat_axis=0, tiled=True
    ).astype(buffer.dtype)
    y_total = (y_local + y_prior).reshape(n_req * drafts, inner_here)
    gated = y_total * jax.nn.silu(z_all.astype(jnp.float32))
    sq_part = jnp.sum(gated * gated, axis=1)
    sq_hi = sq_part.astype(jnp.bfloat16)
    sq_lo = (sq_part - sq_hi.astype(jnp.float32)).astype(jnp.bfloat16)
    scaled = (gated * norm_gain[None, :]).astype(jnp.bfloat16)
    partial = jnp.dot(scaled, w_out, preferred_element_type=jnp.float32).astype(jnp.bfloat16)
    width = partial.shape[1]
    extra = jnp.zeros((partial.shape[0], 128), jnp.bfloat16)
    extra = extra.at[:, 0].set(sq_hi).at[:, 1].set(sq_lo)
    n_y = lax.axis_size("by")
    packed = jnp.concatenate([partial, extra], 1).reshape(n_y, n_blk // n_y, local_rows, width + 128)
    half_sum = jnp.sum(exchange4(packed, "by", False, 2).astype(jnp.float32), axis=0)
    sq_mid = half_sum[:, :, width] + half_sum[:, :, width + 1]
    sq_mid_hi = sq_mid.astype(jnp.bfloat16)
    sq_mid_lo = (sq_mid - sq_mid_hi.astype(jnp.float32)).astype(jnp.bfloat16)
    half_packed = (
        half_sum.astype(jnp.bfloat16).at[:, :, width].set(sq_mid_hi).at[:, :, width + 1].set(sq_mid_lo)
    )
    summed = jnp.sum(exchange(half_packed, "bz", False, 3).astype(jnp.float32), axis=0)
    inner_all = inner_here * n_blk
    mean_sq = (summed[:, width] + summed[:, width + 1]) / inner_all
    mixed = (summed[:, :width] * lax.rsqrt(mean_sq + 1e-05)[:, None]).astype(jnp.bfloat16)
    return (mixed[None], new_pool)


def solution(mesh):
    placed = (
        P("rep", "blk", None),
        P(None, "blk"),
        P(None, "blk"),
        P(),
        P(None, "blk"),
        P(None, "blk"),
        P(),
        P(None, "blk"),
        P("blk"),
        P("blk"),
        P("blk"),
        P("blk", None),
        P("rep", None, "blk"),
        P("rep", None, None),
        P("rep", "blk", None, None),
        P(),
        P("rep", None),
        P("rep"),
        P("rep"),
    )
    n_blk, n_rep = mesh.shape["blk"], mesh.shape["rep"]
    split_mesh = jax.sharding.Mesh(
        mesh.devices.reshape(Y_CHIPS, n_blk // Y_CHIPS, n_rep), AXES
    )
    placed = tuple(P(*[BLK if part == "blk" else part for part in spec]) for spec in placed)
    return jax.shard_map(
        shards,
        mesh=split_mesh,
        in_specs=placed,
        out_specs=(P("rep", BLK, None), P("rep", BLK, None, None)),
        check_vma=False,
    )
```

```python
import functools

import jax
import jax.numpy as jnp
from jax import lax
from jax.experimental import pallas as pl
from jax.experimental.pallas import tpu as pltpu
from jax.sharding import PartitionSpec as P

MESH = pl.DeviceIdType.MESH
AXES = ("by", "bz", "rep")
BLK = ("by", "bz")
Y_CHIPS = 4


def exchange_kernel(n, axis, gather, src_ref, dst_ref, send_sem, recv_sem, local_sem):
    me = lax.axis_index(axis)
    coords = {name: lax.axis_index(name) for name in AXES}

    def device_of(peer):
        return tuple(peer if name == axis else coords[name] for name in AXES)

    barrier = pltpu.get_barrier_semaphore()
    for offset in range(1, n):
        peer = lax.rem(me + offset, n)
        pl.semaphore_signal(barrier, inc=1, device_id=device_of(peer), device_id_type=MESH)
    pl.semaphore_wait(barrier, n - 1)
    local = pltpu.make_async_copy(src_ref if gather else src_ref.at[me], dst_ref.at[me], local_sem)
    local.start()
    copies = []
    for offset in sorted(range(1, n), key=lambda offset: (min(offset, n - offset), offset)):
        peer = lax.rem(me + offset, n)
        copy = pltpu.make_async_remote_copy(
            src_ref=src_ref if gather else src_ref.at[peer],
            dst_ref=dst_ref.at[me],
            send_sem=send_sem.at[offset],
            recv_sem=recv_sem.at[offset],
            device_id=device_of(peer),
            device_id_type=MESH,
        )
        copy.start()
        copies.append(copy)
    local.wait()
    for copy in copies:
        copy.wait()


def ring4_kernel(axis, gather, src_ref, dst_ref, stage_ref, send_sem, recv_sem, local_sem):
    me = lax.axis_index(axis)
    coords = {name: lax.axis_index(name) for name in AXES}

    def device_of(peer):
        return tuple(peer if name == axis else coords[name] for name in AXES)

    right, left = lax.rem(me + 1, 4), lax.rem(me + 3, 4)
    opposite = lax.rem(me + 2, 4)
    half = dst_ref.shape[1] // 2
    first, second = pl.ds(0, half), pl.ds(half, half)

    def remote(src, dst, index, peer):
        copy = pltpu.make_async_remote_copy(
            src_ref=src,
            dst_ref=dst,
            send_sem=send_sem.at[index],
            recv_sem=recv_sem.at[index],
            device_id=device_of(peer),
            device_id_type=MESH,
        )
        copy.start()
        return copy

    barrier = pltpu.get_barrier_semaphore()
    for peer in (left, right):
        pl.semaphore_signal(barrier, inc=1, device_id=device_of(peer), device_id_type=MESH)
    pl.semaphore_wait(barrier, 2)
    if not gather:
        stage_right = remote(src_ref.at[opposite, first], stage_ref.at[0], 2, right)
        stage_left = remote(src_ref.at[opposite, second], stage_ref.at[1], 3, left)
    local = pltpu.make_async_copy(src_ref if gather else src_ref.at[me], dst_ref.at[me], local_sem)
    local.start()
    to_right = remote(src_ref if gather else src_ref.at[right], dst_ref.at[me], 0, right)
    to_left = remote(src_ref if gather else src_ref.at[left], dst_ref.at[me], 1, left)
    if gather:
        to_right.wait_recv()
        pass_right = remote(dst_ref.at[left, first], dst_ref.at[left, first], 2, right)
        to_left.wait_recv()
        pass_left = remote(dst_ref.at[right, second], dst_ref.at[right, second], 3, left)
        to_right.wait_send()
        to_left.wait_send()
    else:
        stage_right.wait_recv()
        pass_right = remote(stage_ref.at[0], dst_ref.at[left, first], 4, right)
        stage_left.wait_recv()
        pass_left = remote(stage_ref.at[1], dst_ref.at[right, second], 5, left)
        stage_right.wait_send()
        stage_left.wait_send()
        to_right.wait()
        to_left.wait()
    local.wait()
    pass_right.wait()
    pass_left.wait()


def exchange4(src, axis, gather, collective_id):
    block = src.shape if gather else src.shape[1:]
    out = jax.ShapeDtypeStruct((4,) + tuple(block), src.dtype)
    stage = jax.ShapeDtypeStruct((2, block[0] // 2) + tuple(block[1:]), src.dtype)
    return pl.pallas_call(
        functools.partial(ring4_kernel, axis, gather),
        out_shape=(out, stage),
        in_specs=[pl.BlockSpec(memory_space=pl.ANY)],
        out_specs=(pl.BlockSpec(memory_space=pl.ANY), pl.BlockSpec(memory_space=pl.ANY)),
        scratch_shapes=[
            pltpu.SemaphoreType.DMA((6,)),
            pltpu.SemaphoreType.DMA((6,)),
            pltpu.SemaphoreType.DMA,
        ],
        compiler_params=pltpu.CompilerParams(collective_id=collective_id, has_side_effects=True),
    )(src)[0]


def gather2d_kernel(nz, src_ref, dst_ref, send_sem, recv_sem, local_sem):
    y, z = lax.axis_index("by"), lax.axis_index("bz")
    rep = lax.axis_index("rep")
    right, left = lax.rem(y + 1, 4), lax.rem(y + 3, 4)
    half = src_ref.shape[0] // 2
    first, second = pl.ds(0, half), pl.ds(half, half)
    z_sem, r_sem, l_sem, ra_sem, lb_sem = 0, nz, 2 * nz, 3 * nz, 4 * nz

    def remote(src, dst, index, yy, zz):
        copy = pltpu.make_async_remote_copy(
            src_ref=src,
            dst_ref=dst,
            send_sem=send_sem.at[index],
            recv_sem=recv_sem.at[index],
            device_id=(yy, zz, rep),
            device_id_type=MESH,
        )
        copy.start()
        return copy

    barrier = pltpu.get_barrier_semaphore()
    for offset in range(1, nz):
        pl.semaphore_signal(
            barrier, inc=1, device_id=(y, lax.rem(z + offset, nz), rep), device_id_type=MESH
        )
    for yy in (left, right):
        pl.semaphore_signal(barrier, inc=1, device_id=(yy, z, rep), device_id_type=MESH)
    pl.semaphore_wait(barrier, nz + 1)
    local = pltpu.make_async_copy(src_ref, dst_ref.at[y, z], local_sem)
    local.start()
    nearest = sorted(range(1, nz), key=lambda offset: (min(offset, nz - offset), offset))
    along_z = {}
    for offset in nearest:
        along_z[offset] = remote(src_ref, dst_ref.at[y, z], z_sem + offset, y, lax.rem(z + offset, nz))
    to_right = [remote(src_ref, dst_ref.at[y, z], r_sem, right, z)]
    to_left = [remote(src_ref, dst_ref.at[y, z], l_sem, left, z)]
    relays = []

    def relay(offset):
        zs = lax.rem(z + nz - offset, nz)
        to_right[offset].wait_recv()
        relays.append(
            remote(dst_ref.at[left, zs, first], dst_ref.at[left, zs, first], ra_sem + offset, right, z)
        )
        to_left[offset].wait_recv()
        relays.append(
            remote(dst_ref.at[right, zs, second], dst_ref.at[right, zs, second], lb_sem + offset, left, z)
        )

    to_right, to_left = {0: to_right[0]}, {0: to_left[0]}
    before = 0
    for offset in nearest:
        along_z[offset].wait_recv()
        zs = lax.rem(z + nz - offset, nz)
        to_right[offset] = remote(dst_ref.at[y, zs], dst_ref.at[y, zs], r_sem + offset, right, z)
        to_left[offset] = remote(dst_ref.at[y, zs], dst_ref.at[y, zs], l_sem + offset, left, z)
        relay(before)
        before = offset
    relay(before)
    local.wait()
    for copy in list(along_z.values()) + list(to_right.values()) + list(to_left.values()):
        copy.wait_send()
    for copy in relays:
        copy.wait()


def gather2d(src, collective_id):
    nz = lax.axis_size("bz")
    return pl.pallas_call(
        functools.partial(gather2d_kernel, nz),
        out_shape=jax.ShapeDtypeStruct((4, nz) + tuple(src.shape), src.dtype),
        in_specs=[pl.BlockSpec(memory_space=pl.ANY)],
        out_specs=pl.BlockSpec(memory_space=pl.ANY),
        scratch_shapes=[
            pltpu.SemaphoreType.DMA((5 * nz,)),
            pltpu.SemaphoreType.DMA((5 * nz,)),
            pltpu.SemaphoreType.DMA,
        ],
        compiler_params=pltpu.CompilerParams(collective_id=collective_id, has_side_effects=True),
    )(src)


def exchange(src, axis, gather, collective_id):
    n = lax.axis_size(axis)
    block = src.shape if gather else src.shape[1:]
    return pl.pallas_call(
        functools.partial(exchange_kernel, n, axis, gather),
        out_shape=jax.ShapeDtypeStruct((n,) + tuple(block), src.dtype),
        in_specs=[pl.BlockSpec(memory_space=pl.ANY)],
        out_specs=pl.BlockSpec(memory_space=pl.ANY),
        scratch_shapes=[
            pltpu.SemaphoreType.DMA((n,)),
            pltpu.SemaphoreType.DMA((n,)),
            pltpu.SemaphoreType.DMA,
        ],
        compiler_params=pltpu.CompilerParams(collective_id=collective_id, has_side_effects=True),
    )(src)


def convolve(edge_cells, fresh_cells, kernel, edge_mask):
    sequence = jnp.concatenate(
        [edge_cells * edge_mask[:, :, None].astype(edge_cells.dtype), fresh_cells], 1
    ).astype(jnp.float32)
    steps_count = fresh_cells.shape[1]
    summed = kernel[0] * sequence[:, 0:steps_count]
    for offset in range(1, kernel.shape[0]):
        summed = summed + kernel[offset] * sequence[:, offset : offset + steps_count]
    return jax.nn.silu(summed).astype(jnp.bfloat16)


def split_dot(spec, wide, narrow):
    high = wide.astype(jnp.bfloat16)
    low = (wide - high.astype(jnp.float32)).astype(jnp.bfloat16)
    return jnp.einsum(spec, high, narrow, preferred_element_type=jnp.float32) + jnp.einsum(
        spec, low, narrow, preferred_element_type=jnp.float32
    )


def shards(
    hidden_in,
    w_z,
    w_x,
    w_bc,
    w_dt,
    conv_x,
    conv_bc,
    dt_bias,
    a_log,
    d_skip,
    norm_gain,
    w_out,
    edge_x,
    edge_bc,
    pool,
    tenant_sizes,
    owner,
    accepted,
    prompt_len,
):
    highest = lax.Precision.HIGHEST
    rows_in = hidden_in[0]
    local_rows = rows_in.shape[0]
    n_req = edge_x.shape[0]
    drafts = local_rows * lax.axis_size(BLK) // n_req
    state_dim = w_bc.shape[1] // 2
    heads_here = w_dt.shape[1]
    inner_here = w_z.shape[1]
    head_dim = inner_here // heads_here
    slots_here = pool.shape[0]
    cap_group = slots_here // lax.axis_size("rep")
    weights_in = (w_z, w_x, w_dt, w_bc)
    n_blk = lax.axis_size(BLK)
    block_rows = gather2d(rows_in, 0).reshape(n_blk * local_rows, rows_in.shape[1])
    projected = jnp.concatenate(
        [
            jnp.dot(block_rows, weight_cols, preferred_element_type=jnp.float32)
            for weight_cols in weights_in
        ],
        1,
    ).astype(jnp.bfloat16)
    z_all = projected[:, :inner_here]
    u_all = projected[:, inner_here : 2 * inner_here]
    dt_raw = projected[:, 2 * inner_here : 2 * inner_here + heads_here]
    bc_all = projected[:, 2 * inner_here + heads_here :]
    edge_len = edge_x.shape[1]
    edge_mask = prompt_len[:, None] >= (edge_len - jnp.arange(edge_len, dtype=jnp.int32))[None, :]
    x_conv = convolve(edge_x, u_all.reshape(n_req, drafts, inner_here), conv_x, edge_mask)
    bc_conv = convolve(edge_bc, bc_all.reshape(n_req, drafts, 2 * state_dim), conv_bc, edge_mask)
    b_half = bc_conv[:, :, :state_dim]
    c_half = bc_conv[:, :, state_dim:]
    b_float = b_half.astype(jnp.float32)
    c_float = c_half.astype(jnp.float32)
    x_heads = x_conv.reshape(n_req, drafts, heads_here, head_dim).astype(jnp.float32)
    req_index = lax.axis_index("rep") * n_req + jnp.arange(n_req, dtype=jnp.int32)
    tenant_ends = jnp.cumsum(tenant_sizes)
    tenant_id = jnp.sum((req_index[:, None] >= tenant_ends[None, :-1]).astype(jnp.int32), axis=1)
    tenant_pick = (
        tenant_id[:, None] == jnp.arange(tenant_sizes.shape[0], dtype=jnp.int32)[None, :]
    ).astype(jnp.float32)
    bias_req = jnp.dot(tenant_pick, dt_bias, precision=highest)
    step_size = jax.nn.softplus(
        dt_raw.reshape(n_req, drafts, heads_here).astype(jnp.float32) + bias_req[:, None, :]
    )
    log_decay = jnp.cumsum(step_size * (-jnp.exp(a_log))[None, None, :], axis=1)
    draft_index = jnp.arange(drafts, dtype=jnp.int32)
    causal = draft_index[:, None] >= draft_index[None, :]
    scores = jnp.einsum("rtn,rsn->rts", c_half, b_half, preferred_element_type=jnp.float32)
    log_gap = log_decay[:, :, None, :] - log_decay[:, None, :, :]
    weight = (
        jnp.where(causal[None, :, :, None], jnp.exp(jnp.minimum(log_gap, 0.0)), 0.0)
        * step_size[:, None, :, :]
        * scores[:, :, :, None]
    )
    y_local = (
        split_dot("rtsh,rshp->rthp", weight, x_conv.reshape(n_req, drafts, heads_here, head_dim))
        + d_skip[None, None, :, None] * x_heads
    )
    pick_last = (draft_index[None, :] == accepted[:, None] - 1).astype(jnp.float32)
    log_accept = jnp.sum(pick_last[:, :, None] * log_decay, axis=1)
    keep_draft = draft_index[None, :] < accepted[:, None]
    coef = (
        jnp.where(
            keep_draft[:, :, None],
            jnp.exp(jnp.minimum(log_accept[:, None, :] - log_decay, 0.0)),
            0.0,
        )
        * step_size
    )
    carry_decay = jnp.exp(log_accept)
    decay_now = jnp.exp(log_decay)
    owner_of = owner[:, 0]
    local_index = jnp.arange(n_req, dtype=jnp.int32)
    earlier = (owner_of[None, :] == owner_of[:, None]) & (
        local_index[None, :] < local_index[:, None]
    )
    rank_within = jnp.sum(earlier.astype(jnp.int32), axis=1)
    slot_index = owner_of * cap_group + rank_within
    fetched_half = lax.all_to_all(
        pool.astype(jnp.bfloat16), "rep", split_axis=0, concat_axis=0, tiled=True
    )
    fetched = fetched_half.astype(pool.dtype)
    slots = jnp.arange(slots_here, dtype=jnp.int32)
    slot_pick = (slots[:, None] == slot_index[None, :]).astype(jnp.int32)
    slot_used = jnp.sum(slot_pick, axis=1) > 0
    slot_req = jnp.sum(slot_pick * local_index[None, :], axis=1)

    def to_slots(per_req):
        taken = jnp.take(per_req, slot_req, axis=0)
        return jnp.where(slot_used.reshape((-1,) + (1,) * (per_req.ndim - 1)), taken, 0.0)

    prior_slot = to_slots(decay_now)[:, :, :, None] * jnp.einsum(
        "jhpn,jtn->jthp", fetched_half, to_slots(c_half), preferred_element_type=jnp.float32
    )
    y_prior = jnp.take(prior_slot, slot_index, axis=0)
    buffer = to_slots(carry_decay)[:, :, None, None] * fetched + split_dot(
        "jshp,jsn->jhpn", to_slots(coef[:, :, :, None] * x_heads), to_slots(b_half)
    )
    new_pool = lax.all_to_all(
        buffer.astype(jnp.bfloat16), "rep", split_axis=0, concat_axis=0, tiled=True
    ).astype(buffer.dtype)
    y_total = (y_local + y_prior).reshape(n_req * drafts, inner_here)
    gated = y_total * jax.nn.silu(z_all.astype(jnp.float32))
    sq_part = jnp.sum(gated * gated, axis=1)
    sq_hi = sq_part.astype(jnp.bfloat16)
    sq_lo = (sq_part - sq_hi.astype(jnp.float32)).astype(jnp.bfloat16)
    scaled = (gated * norm_gain[None, :]).astype(jnp.bfloat16)
    partial = jnp.dot(scaled, w_out, preferred_element_type=jnp.float32).astype(jnp.bfloat16)
    width = partial.shape[1]
    extra_column = lax.broadcasted_iota(jnp.int32, (partial.shape[0], 128), 1)
    extra = jnp.where(
        extra_column == 0, sq_hi[:, None], jnp.where(extra_column == 1, sq_lo[:, None], jnp.zeros((), jnp.bfloat16))
    )
    n_y = lax.axis_size("by")
    packed = jnp.concatenate([partial, extra], 1).reshape(n_y, n_blk // n_y, local_rows, width + 128)
    half_sum = jnp.sum(exchange4(packed, "by", False, 2).astype(jnp.float32), axis=0)
    sq_mid = half_sum[:, :, width] + half_sum[:, :, width + 1]
    sq_mid_hi = sq_mid.astype(jnp.bfloat16)
    sq_mid_lo = (sq_mid - sq_mid_hi.astype(jnp.float32)).astype(jnp.bfloat16)
    column = lax.broadcasted_iota(jnp.int32, half_sum.shape, 2)
    half_packed = jnp.where(
        column == width,
        sq_mid_hi.astype(jnp.float32)[:, :, None],
        jnp.where(column == width + 1, sq_mid_lo.astype(jnp.float32)[:, :, None], half_sum),
    ).astype(jnp.bfloat16)
    summed = jnp.sum(exchange(half_packed, "bz", False, 3).astype(jnp.float32), axis=0)
    inner_all = inner_here * n_blk
    mean_sq = (summed[:, width] + summed[:, width + 1]) / inner_all
    mixed = (summed[:, :width] * lax.rsqrt(mean_sq + 1e-05)[:, None]).astype(jnp.bfloat16)
    return (mixed[None], new_pool)


def solution(mesh):
    placed = (
        P("rep", "blk", None),
        P(None, "blk"),
        P(None, "blk"),
        P(),
        P(None, "blk"),
        P(None, "blk"),
        P(),
        P(None, "blk"),
        P("blk"),
        P("blk"),
        P("blk"),
        P("blk", None),
        P("rep", None, "blk"),
        P("rep", None, None),
        P("rep", "blk", None, None),
        P(),
        P("rep", None),
        P("rep"),
        P("rep"),
    )
    n_blk, n_rep = mesh.shape["blk"], mesh.shape["rep"]
    split_mesh = jax.sharding.Mesh(
        mesh.devices.reshape(Y_CHIPS, n_blk // Y_CHIPS, n_rep), AXES
    )
    placed = tuple(P(*[BLK if part == "blk" else part for part in spec]) for spec in placed)
    return jax.shard_map(
        shards,
        mesh=split_mesh,
        in_specs=placed,
        out_specs=(P("rep", BLK, None), P("rep", BLK, None, None)),
        check_vma=False,
    )
```

```python
import functools

import jax
import jax.numpy as jnp
from jax import lax
from jax.experimental import pallas as pl
from jax.experimental.pallas import tpu as pltpu
from jax.sharding import PartitionSpec as P

MESH = pl.DeviceIdType.MESH
AXES = ("by", "bz", "rep")
BLK = ("by", "bz")
Y_CHIPS = 4


def exchange_kernel(n, axis, gather, src_ref, dst_ref, send_sem, recv_sem, local_sem):
    me = lax.axis_index(axis)
    coords = {name: lax.axis_index(name) for name in AXES}

    def device_of(peer):
        return tuple(peer if name == axis else coords[name] for name in AXES)

    barrier = pltpu.get_barrier_semaphore()
    for offset in range(1, n):
        peer = lax.rem(me + offset, n)
        pl.semaphore_signal(barrier, inc=1, device_id=device_of(peer), device_id_type=MESH)
    pl.semaphore_wait(barrier, n - 1)
    local = pltpu.make_async_copy(src_ref if gather else src_ref.at[me], dst_ref.at[me], local_sem)
    local.start()
    copies = []
    for offset in sorted(range(1, n), key=lambda offset: (min(offset, n - offset), offset)):
        peer = lax.rem(me + offset, n)
        copy = pltpu.make_async_remote_copy(
            src_ref=src_ref if gather else src_ref.at[peer],
            dst_ref=dst_ref.at[me],
            send_sem=send_sem.at[offset],
            recv_sem=recv_sem.at[offset],
            device_id=device_of(peer),
            device_id_type=MESH,
        )
        copy.start()
        copies.append(copy)
    local.wait()
    for copy in copies:
        copy.wait()


def ring4_kernel(axis, gather, src_ref, dst_ref, stage_ref, send_sem, recv_sem, local_sem):
    me = lax.axis_index(axis)
    coords = {name: lax.axis_index(name) for name in AXES}

    def device_of(peer):
        return tuple(peer if name == axis else coords[name] for name in AXES)

    right, left = lax.rem(me + 1, 4), lax.rem(me + 3, 4)
    opposite = lax.rem(me + 2, 4)
    half = dst_ref.shape[1] // 2
    first, second = pl.ds(0, half), pl.ds(half, half)

    def remote(src, dst, index, peer):
        copy = pltpu.make_async_remote_copy(
            src_ref=src,
            dst_ref=dst,
            send_sem=send_sem.at[index],
            recv_sem=recv_sem.at[index],
            device_id=device_of(peer),
            device_id_type=MESH,
        )
        copy.start()
        return copy

    barrier = pltpu.get_barrier_semaphore()
    for peer in (left, right):
        pl.semaphore_signal(barrier, inc=1, device_id=device_of(peer), device_id_type=MESH)
    pl.semaphore_wait(barrier, 2)
    if not gather:
        stage_right = remote(src_ref.at[opposite, first], stage_ref.at[0], 2, right)
        stage_left = remote(src_ref.at[opposite, second], stage_ref.at[1], 3, left)
    local = pltpu.make_async_copy(src_ref if gather else src_ref.at[me], dst_ref.at[me], local_sem)
    local.start()
    to_right = remote(src_ref if gather else src_ref.at[right], dst_ref.at[me], 0, right)
    to_left = remote(src_ref if gather else src_ref.at[left], dst_ref.at[me], 1, left)
    if gather:
        to_right.wait_recv()
        pass_right = remote(dst_ref.at[left, first], dst_ref.at[left, first], 2, right)
        to_left.wait_recv()
        pass_left = remote(dst_ref.at[right, second], dst_ref.at[right, second], 3, left)
        to_right.wait_send()
        to_left.wait_send()
    else:
        stage_right.wait_recv()
        pass_right = remote(stage_ref.at[0], dst_ref.at[left, first], 4, right)
        stage_left.wait_recv()
        pass_left = remote(stage_ref.at[1], dst_ref.at[right, second], 5, left)
        stage_right.wait_send()
        stage_left.wait_send()
        to_right.wait()
        to_left.wait()
    local.wait()
    pass_right.wait()
    pass_left.wait()


def exchange4(src, axis, gather, collective_id):
    block = src.shape if gather else src.shape[1:]
    out = jax.ShapeDtypeStruct((4,) + tuple(block), src.dtype)
    stage = jax.ShapeDtypeStruct((2, block[0] // 2) + tuple(block[1:]), src.dtype)
    return pl.pallas_call(
        functools.partial(ring4_kernel, axis, gather),
        out_shape=(out, stage),
        in_specs=[pl.BlockSpec(memory_space=pl.ANY)],
        out_specs=(pl.BlockSpec(memory_space=pl.ANY), pl.BlockSpec(memory_space=pl.ANY)),
        scratch_shapes=[
            pltpu.SemaphoreType.DMA((6,)),
            pltpu.SemaphoreType.DMA((6,)),
            pltpu.SemaphoreType.DMA,
        ],
        compiler_params=pltpu.CompilerParams(collective_id=collective_id, has_side_effects=True),
    )(src)[0]


def gather2d_kernel(nz, src_ref, dst_ref, send_sem, recv_sem, local_sem):
    y, z = lax.axis_index("by"), lax.axis_index("bz")
    rep = lax.axis_index("rep")
    right, left = lax.rem(y + 1, 4), lax.rem(y + 3, 4)
    half = src_ref.shape[0] // 2
    first, second = pl.ds(0, half), pl.ds(half, half)
    z_sem, r_sem, l_sem, ra_sem, lb_sem = 0, nz, 2 * nz, 3 * nz, 4 * nz

    def remote(src, dst, index, yy, zz):
        copy = pltpu.make_async_remote_copy(
            src_ref=src,
            dst_ref=dst,
            send_sem=send_sem.at[index],
            recv_sem=recv_sem.at[index],
            device_id=(yy, zz, rep),
            device_id_type=MESH,
        )
        copy.start()
        return copy

    barrier = pltpu.get_barrier_semaphore()
    for offset in range(1, nz):
        pl.semaphore_signal(
            barrier, inc=1, device_id=(y, lax.rem(z + offset, nz), rep), device_id_type=MESH
        )
    for yy in (left, right):
        pl.semaphore_signal(barrier, inc=1, device_id=(yy, z, rep), device_id_type=MESH)
    pl.semaphore_wait(barrier, nz + 1)
    local = pltpu.make_async_copy(src_ref, dst_ref.at[y, z], local_sem)
    local.start()
    nearest = sorted(range(1, nz), key=lambda offset: (min(offset, nz - offset), offset))
    along_z = {}
    for offset in nearest:
        along_z[offset] = remote(src_ref, dst_ref.at[y, z], z_sem + offset, y, lax.rem(z + offset, nz))
    to_right = [remote(src_ref, dst_ref.at[y, z], r_sem, right, z)]
    to_left = [remote(src_ref, dst_ref.at[y, z], l_sem, left, z)]
    relays = []

    def relay(offset):
        zs = lax.rem(z + nz - offset, nz)
        to_right[offset].wait_recv()
        relays.append(
            remote(dst_ref.at[left, zs, first], dst_ref.at[left, zs, first], ra_sem + offset, right, z)
        )
        to_left[offset].wait_recv()
        relays.append(
            remote(dst_ref.at[right, zs, second], dst_ref.at[right, zs, second], lb_sem + offset, left, z)
        )

    to_right, to_left = {0: to_right[0]}, {0: to_left[0]}
    before = 0
    for offset in nearest:
        along_z[offset].wait_recv()
        zs = lax.rem(z + nz - offset, nz)
        to_right[offset] = remote(dst_ref.at[y, zs], dst_ref.at[y, zs], r_sem + offset, right, z)
        to_left[offset] = remote(dst_ref.at[y, zs], dst_ref.at[y, zs], l_sem + offset, left, z)
        relay(before)
        before = offset
    relay(before)
    local.wait()
    for copy in list(along_z.values()) + list(to_right.values()) + list(to_left.values()):
        copy.wait_send()
    for copy in relays:
        copy.wait()


def gather2d(src, collective_id):
    nz = lax.axis_size("bz")
    return pl.pallas_call(
        functools.partial(gather2d_kernel, nz),
        out_shape=jax.ShapeDtypeStruct((4, nz) + tuple(src.shape), src.dtype),
        in_specs=[pl.BlockSpec(memory_space=pl.ANY)],
        out_specs=pl.BlockSpec(memory_space=pl.ANY),
        scratch_shapes=[
            pltpu.SemaphoreType.DMA((5 * nz,)),
            pltpu.SemaphoreType.DMA((5 * nz,)),
            pltpu.SemaphoreType.DMA,
        ],
        compiler_params=pltpu.CompilerParams(collective_id=collective_id, has_side_effects=True),
    )(src)


def exchange(src, axis, gather, collective_id):
    n = lax.axis_size(axis)
    block = src.shape if gather else src.shape[1:]
    return pl.pallas_call(
        functools.partial(exchange_kernel, n, axis, gather),
        out_shape=jax.ShapeDtypeStruct((n,) + tuple(block), src.dtype),
        in_specs=[pl.BlockSpec(memory_space=pl.ANY)],
        out_specs=pl.BlockSpec(memory_space=pl.ANY),
        scratch_shapes=[
            pltpu.SemaphoreType.DMA((n,)),
            pltpu.SemaphoreType.DMA((n,)),
            pltpu.SemaphoreType.DMA,
        ],
        compiler_params=pltpu.CompilerParams(collective_id=collective_id, has_side_effects=True),
    )(src)


def convolve(edge_cells, fresh_cells, kernel, edge_mask):
    sequence = jnp.concatenate(
        [edge_cells * edge_mask[:, :, None].astype(edge_cells.dtype), fresh_cells], 1
    ).astype(jnp.float32)
    steps_count = fresh_cells.shape[1]
    summed = kernel[0] * sequence[:, 0:steps_count]
    for offset in range(1, kernel.shape[0]):
        summed = summed + kernel[offset] * sequence[:, offset : offset + steps_count]
    return jax.nn.silu(summed).astype(jnp.bfloat16)


def split_dot(spec, wide, narrow):
    high = wide.astype(jnp.bfloat16)
    low = (wide - high.astype(jnp.float32)).astype(jnp.bfloat16)
    return jnp.einsum(spec, high, narrow, preferred_element_type=jnp.float32) + jnp.einsum(
        spec, low, narrow, preferred_element_type=jnp.float32
    )


def shards(
    hidden_in,
    w_z,
    w_x,
    w_bc,
    w_dt,
    conv_x,
    conv_bc,
    dt_bias,
    a_log,
    d_skip,
    norm_gain,
    w_out,
    edge_x,
    edge_bc,
    pool,
    tenant_sizes,
    owner,
    accepted,
    prompt_len,
):
    highest = lax.Precision.HIGHEST
    rows_in = hidden_in[0]
    local_rows = rows_in.shape[0]
    n_req = edge_x.shape[0]
    drafts = local_rows * lax.axis_size(BLK) // n_req
    state_dim = w_bc.shape[1] // 2
    heads_here = w_dt.shape[1]
    inner_here = w_z.shape[1]
    head_dim = inner_here // heads_here
    slots_here = pool.shape[0]
    cap_group = slots_here // lax.axis_size("rep")
    weights_in = (w_z, w_x, w_dt, w_bc)
    n_blk = lax.axis_size(BLK)
    block_rows = gather2d(rows_in, 0).reshape(n_blk * local_rows, rows_in.shape[1])
    projected = jnp.concatenate(
        [
            jnp.dot(block_rows, weight_cols, preferred_element_type=jnp.float32)
            for weight_cols in weights_in
        ],
        1,
    ).astype(jnp.bfloat16)
    z_all = projected[:, :inner_here]
    u_all = projected[:, inner_here : 2 * inner_here]
    dt_raw = projected[:, 2 * inner_here : 2 * inner_here + heads_here]
    bc_all = projected[:, 2 * inner_here + heads_here :]
    edge_len = edge_x.shape[1]
    edge_mask = prompt_len[:, None] >= (edge_len - jnp.arange(edge_len, dtype=jnp.int32))[None, :]
    x_conv = convolve(edge_x, u_all.reshape(n_req, drafts, inner_here), conv_x, edge_mask)
    bc_conv = convolve(edge_bc, bc_all.reshape(n_req, drafts, 2 * state_dim), conv_bc, edge_mask)
    b_half = bc_conv[:, :, :state_dim]
    c_half = bc_conv[:, :, state_dim:]
    b_float = b_half.astype(jnp.float32)
    c_float = c_half.astype(jnp.float32)
    x_heads = x_conv.reshape(n_req, drafts, heads_here, head_dim).astype(jnp.float32)
    req_index = lax.axis_index("rep") * n_req + jnp.arange(n_req, dtype=jnp.int32)
    tenant_ends = jnp.cumsum(tenant_sizes)
    tenant_id = jnp.sum((req_index[:, None] >= tenant_ends[None, :-1]).astype(jnp.int32), axis=1)
    tenant_pick = (
        tenant_id[:, None] == jnp.arange(tenant_sizes.shape[0], dtype=jnp.int32)[None, :]
    ).astype(jnp.float32)
    bias_req = jnp.dot(tenant_pick, dt_bias, precision=highest)
    step_size = jax.nn.softplus(
        dt_raw.reshape(n_req, drafts, heads_here).astype(jnp.float32) + bias_req[:, None, :]
    )
    log_decay = jnp.cumsum(step_size * (-jnp.exp(a_log))[None, None, :], axis=1)
    draft_index = jnp.arange(drafts, dtype=jnp.int32)
    causal = draft_index[:, None] >= draft_index[None, :]
    scores = jnp.einsum("rtn,rsn->rts", c_half, b_half, preferred_element_type=jnp.float32)
    log_gap = log_decay[:, :, None, :] - log_decay[:, None, :, :]
    weight = (
        jnp.where(causal[None, :, :, None], jnp.exp(jnp.minimum(log_gap, 0.0)), 0.0)
        * step_size[:, None, :, :]
        * scores[:, :, :, None]
    )
    y_local = (
        split_dot("rtsh,rshp->rthp", weight, x_conv.reshape(n_req, drafts, heads_here, head_dim))
        + d_skip[None, None, :, None] * x_heads
    )
    pick_last = (draft_index[None, :] == accepted[:, None] - 1).astype(jnp.float32)
    log_accept = jnp.sum(pick_last[:, :, None] * log_decay, axis=1)
    keep_draft = draft_index[None, :] < accepted[:, None]
    coef = (
        jnp.where(
            keep_draft[:, :, None],
            jnp.exp(jnp.minimum(log_accept[:, None, :] - log_decay, 0.0)),
            0.0,
        )
        * step_size
    )
    carry_decay = jnp.exp(log_accept)
    decay_now = jnp.exp(log_decay)
    owner_of = owner[:, 0]
    local_index = jnp.arange(n_req, dtype=jnp.int32)
    earlier = (owner_of[None, :] == owner_of[:, None]) & (
        local_index[None, :] < local_index[:, None]
    )
    rank_within = jnp.sum(earlier.astype(jnp.int32), axis=1)
    slot_index = owner_of * cap_group + rank_within
    fetched_half = lax.all_to_all(
        pool.astype(jnp.bfloat16), "rep", split_axis=0, concat_axis=0, tiled=True
    )
    fetched = fetched_half.astype(pool.dtype)
    slots = jnp.arange(slots_here, dtype=jnp.int32)
    slot_pick = (slots[:, None] == slot_index[None, :]).astype(jnp.int32)
    slot_used = jnp.sum(slot_pick, axis=1) > 0
    slot_req = jnp.sum(slot_pick * local_index[None, :], axis=1)

    def to_slots(per_req):
        taken = jnp.take(per_req, slot_req, axis=0)
        return jnp.where(slot_used.reshape((-1,) + (1,) * (per_req.ndim - 1)), taken, 0.0)

    prior_slot = to_slots(decay_now)[:, :, :, None] * jnp.einsum(
        "jhpn,jtn->jthp", fetched_half, to_slots(c_half), preferred_element_type=jnp.float32
    )
    y_prior = jnp.take(prior_slot, slot_index, axis=0)
    buffer = to_slots(carry_decay)[:, :, None, None] * fetched + split_dot(
        "jshp,jsn->jhpn", to_slots(coef[:, :, :, None] * x_heads), to_slots(b_half)
    )
    new_pool = lax.all_to_all(
        buffer.astype(jnp.bfloat16), "rep", split_axis=0, concat_axis=0, tiled=True
    ).astype(buffer.dtype)
    y_total = (y_local + y_prior).reshape(n_req * drafts, inner_here)
    gated = y_total * jax.nn.silu(z_all.astype(jnp.float32))
    sq_part = jnp.sum(gated * gated, axis=1)
    sq_hi = sq_part.astype(jnp.bfloat16)
    sq_lo = (sq_part - sq_hi.astype(jnp.float32)).astype(jnp.bfloat16)
    scaled = (gated * norm_gain[None, :]).astype(jnp.bfloat16)
    width = w_out.shape[1]
    wide = jnp.dot(scaled, jnp.pad(w_out, ((0, 0), (0, 128))), preferred_element_type=jnp.float32)
    wide_column = lax.broadcasted_iota(jnp.int32, wide.shape, 1)
    wide = jnp.where(
        wide_column == width,
        sq_hi.astype(jnp.float32)[:, None],
        jnp.where(wide_column == width + 1, sq_lo.astype(jnp.float32)[:, None], wide),
    ).astype(jnp.bfloat16)
    n_y = lax.axis_size("by")
    packed = wide.reshape(n_y, n_blk // n_y, local_rows, width + 128)
    half_sum = jnp.sum(exchange4(packed, "by", False, 2).astype(jnp.float32), axis=0)
    sq_mid = half_sum[:, :, width] + half_sum[:, :, width + 1]
    sq_mid_hi = sq_mid.astype(jnp.bfloat16)
    sq_mid_lo = (sq_mid - sq_mid_hi.astype(jnp.float32)).astype(jnp.bfloat16)
    column = lax.broadcasted_iota(jnp.int32, half_sum.shape, 2)
    half_packed = jnp.where(
        column == width,
        sq_mid_hi.astype(jnp.float32)[:, :, None],
        jnp.where(column == width + 1, sq_mid_lo.astype(jnp.float32)[:, :, None], half_sum),
    ).astype(jnp.bfloat16)
    summed = jnp.sum(exchange(half_packed, "bz", False, 3).astype(jnp.float32), axis=0)
    inner_all = inner_here * n_blk
    mean_sq = (summed[:, width] + summed[:, width + 1]) / inner_all
    mixed = (summed[:, :width] * lax.rsqrt(mean_sq + 1e-05)[:, None]).astype(jnp.bfloat16)
    return (mixed[None], new_pool)


def solution(mesh):
    placed = (
        P("rep", "blk", None),
        P(None, "blk"),
        P(None, "blk"),
        P(),
        P(None, "blk"),
        P(None, "blk"),
        P(),
        P(None, "blk"),
        P("blk"),
        P("blk"),
        P("blk"),
        P("blk", None),
        P("rep", None, "blk"),
        P("rep", None, None),
        P("rep", "blk", None, None),
        P(),
        P("rep", None),
        P("rep"),
        P("rep"),
    )
    n_blk, n_rep = mesh.shape["blk"], mesh.shape["rep"]
    split_mesh = jax.sharding.Mesh(
        mesh.devices.reshape(Y_CHIPS, n_blk // Y_CHIPS, n_rep), AXES
    )
    placed = tuple(P(*[BLK if part == "blk" else part for part in spec]) for spec in placed)
    return jax.shard_map(
        shards,
        mesh=split_mesh,
        in_specs=placed,
        out_specs=(P("rep", BLK, None), P("rep", BLK, None, None)),
        check_vma=False,
    )
```
